128 devices in a mesh: py: 8 (over y, core), px: 16 (over z, x).
Axes of the slice: x: 4, y: 4, z: 4, core: 2. Of those that a mesh axis runs over, the one named last changes fastest.
Arguments:
- pieces: bfloat16 [8192, 128, 128], P(('py', 'px')), may hold values from -6 to 6
- owner_map: int32 [8192], P(('py', 'px')), may hold values from 0 to 127, as said below
- offsets: int32 [8192], P(('py', 'px')), may hold values from 0 to 63
- template: bfloat16 [8192, 16384], P('py', 'px'), may hold values from -32 to 32
- coefficients: float32 [3, 15], replicated, may hold values from -3 to 3
Outputs:
- difference: float32 [8192, 16384], P('py', 'px')
The draws below stay inside these ranges and needn't reach their ends.
Inputs may be any that keep to these rules, and one draw needn't show every extreme that they name: owner_map[p] is the tile of the device holding p or one of the eight tiles around it inside the grid; no device sends more than 16 pieces to one tile, and every device sends exactly 16 to one of its tiles.
All inputs are finite; a program needn't handle non-finite values.
Results may differ from the reference program's by a relative error of at most 0.0021.
Values may be sent and summed in bfloat16 or wider, within the bound.
A program may use at most 128 MiB of HBM per device.

```python
import jax
import jax.numpy as jnp
from jax import lax

BLK = 128
HALO = 16
BASES = 3
TERMS = 15
TB = 8
P_DEV = 64
CAP = 16
TILE_ROWS = 8
TILE_COLS = 16
NYP = 8192
NXP = 16384
PIECES = 8192
DEVICES = 128


def draw_owner_map(key, part):
    key_pick, key_score, key_shuffle = jax.random.split(key, 3)
    senders = jnp.arange(DEVICES, dtype=jnp.int32)
    sender_row = senders // TILE_COLS
    sender_col = senders % TILE_COLS
    buckets = jnp.arange(9, dtype=jnp.int32)
    target_row = sender_row[:, None] + (buckets // 3 - 1)[None, :]
    target_col = sender_col[:, None] + (buckets % 3 - 1)[None, :]
    usable = (target_row >= 0) & (target_row < TILE_ROWS) & (target_col >= 0) & (target_col < TILE_COLS)
    picked = jax.random.randint(key_pick, (DEVICES,), 0, 9)
    picked_ok = jnp.take_along_axis(usable, picked[:, None], axis=1)[:, 0]
    forced = jnp.where(picked_ok, picked, 4)
    slot_bucket = jnp.repeat(buckets, CAP)
    slot_ids = jnp.arange(9 * CAP, dtype=jnp.int32)
    scores = jax.random.randint(key_score, (DEVICES, 9 * CAP), 0, 1 << 20) * (9 * CAP) + slot_ids[None, :]
    scores = jnp.where(slot_bucket[None, :] == forced[:, None], slot_ids[None, :] - 9 * CAP, scores)
    scores = jnp.where(usable[:, slot_bucket], scores, (1 << 30) + slot_ids[None, :])
    ranked = jnp.argsort(scores, axis=1)[:, :P_DEV]
    chosen = jnp.take_along_axis(jnp.broadcast_to(slot_bucket[None, :], (DEVICES, 9 * CAP)), ranked, axis=1)
    shuffle_scores = jax.random.randint(key_shuffle, (DEVICES, P_DEV), 0, 1 << 20) * P_DEV + jnp.arange(P_DEV, dtype=jnp.int32)[None, :]
    chosen = jnp.take_along_axis(chosen, jnp.argsort(shuffle_scores, axis=1), axis=1)
    owner_tiles = (sender_row[:, None] + chosen // 3 - 1) * TILE_COLS + sender_col[:, None] + chosen % 3 - 1
    return owner_tiles.reshape(-1).astype(jnp.int32)


def draw_template(key, part):
    first_key, second_key = jax.random.split(key)
    spread = jax.random.truncated_normal(second_key, -4.0, 4.0, (NYP, NXP), jnp.float32)
    rough = jax.random.truncated_normal(first_key, -4.0, 4.0, (NYP, NXP), jnp.float32)
    values = 1.0 + rough * jnp.exp(0.5 * spread)
    return values.astype(jnp.bfloat16)


def place_ends(result, key, least, largest):
    dims = result.shape
    place = [jax.random.randint(jax.random.fold_in(key, axis), (), 0, dims[axis]) for axis in range(len(dims))]
    result = result.at[tuple(place)].set(least)
    longest = dims.index(max(dims))
    place[longest] = (place[longest] + 1) % dims[longest]
    return result.at[tuple(place)].set(largest)


def steps_of(stream_key, extent, cuts, smallest, top_value):
    gain = 1.0
    for axis_at, parts in cuts:
        steps = jax.random.uniform(jax.random.fold_in(jax.random.fold_in(stream_key, 6), axis_at), (parts,), jnp.float32, smallest / len(cuts), top_value / len(cuts))
        gain = gain * jnp.repeat(jnp.exp(steps), extent[axis_at] // parts).reshape((-1,) + (1,) * (len(extent) - 1 - axis_at))
    return gain


def gaussian(rng, dims, width, reach, cuts=(), held_as=jnp.bfloat16):
    values = width * jax.random.normal(rng, dims, jnp.float32)
    if cuts:
        values = values * steps_of(rng, dims, cuts, -0.22, 0.18)
    return jnp.clip(values, -reach, reach).astype(held_as)


def setup_inputs(seed: int = 0) -> dict:
    keys = jax.random.split(jax.random.key(seed), 6)
    pieces = gaussian(keys[0], (PIECES, BLK, BLK), 1.0, 6.0, ((0, 128),))
    owner_map = draw_owner_map(jax.random.fold_in(keys[5], 71), 0)
    offsets = place_ends(jax.random.randint(keys[2], (PIECES,), 0, TB * TB), jax.random.fold_in(keys[2], 1), 0, (TB * TB) - 1).astype(jnp.int32)
    template = draw_template(jax.random.fold_in(keys[5], 71), 0)
    coefficients = gaussian(keys[4], (BASES, TERMS), 0.5, 3.0, (), jnp.float32)
    return {"pieces": pieces, "owner_map": owner_map, "offsets": offsets, "template": template, "coefficients": coefficients}


sigma_fractions = (0.09375, 0.1875, 0.375)
term_powers = [(degree - power_v, power_v) for degree in range(5) for power_v in range(degree + 1)]


def gauss_taps():
    positions = jnp.arange(-HALO, HALO + 1).astype(jnp.float32)
    stacked = []
    for fraction in sigma_fractions:
        sigma = fraction * HALO
        values = jnp.exp(-positions * positions / (2.0 * sigma * sigma))
        stacked.append(values / jnp.sum(values))
    return jnp.stack(stacked).astype(jnp.bfloat16)


def spatial_weight(coef_row, rows_coord, cols_coord):
    rows_pow = [jnp.ones_like(rows_coord)]
    cols_pow = [jnp.ones_like(cols_coord)]
    for degree in range(1, 5):
        rows_pow.append(rows_pow[-1] * rows_coord)
        cols_pow.append(cols_pow[-1] * cols_coord)
    running = jnp.zeros((rows_coord.shape[0], cols_coord.shape[0]), jnp.float32)
    for power_v in range(5):
        inner_sum = jnp.zeros_like(cols_coord)
        for power_u in range(5 - power_v):
            inner_sum = inner_sum + coef_row[term_powers.index((power_u, power_v))] * cols_pow[power_u]
        running = running + rows_pow[power_v][:, None] * inner_sum[None, :]
    return running


def smooth_along(sky_image, weights, axis_pick):
    if axis_pick == 0:
        padded = jnp.pad(sky_image, ((HALO, HALO), (0, 0)))
    else:
        padded = jnp.pad(sky_image, ((0, 0), (HALO, HALO)))
    length = sky_image.shape[axis_pick]

    def add_term(tap_index, running):
        return running + weights[tap_index] * lax.dynamic_slice_in_dim(padded, tap_index, length, axis_pick)

    return lax.fori_loop(0, 2 * HALO + 1, add_term, jnp.zeros_like(sky_image))


def reference(pieces, owner_map, offsets, template, coefficients):
    blocks_across = TILE_COLS * TB
    blocks_down = TILE_ROWS * TB
    block_row = (owner_map // TILE_COLS) * TB + offsets // TB
    block_col = (owner_map % TILE_COLS) * TB + offsets % TB
    block_of = (block_row * blocks_across + block_col).astype(jnp.int32)
    block_sums = jnp.zeros((blocks_down * blocks_across, BLK, BLK), jnp.float32).at[block_of].add(pieces.astype(jnp.float32))
    coverage = jnp.zeros((blocks_down * blocks_across,), jnp.float32).at[block_of].add(1.0)
    science = block_sums / jnp.maximum(coverage, 1.0)[:, None, None]
    science = science.reshape(blocks_down, blocks_across, BLK, BLK).transpose(0, 2, 1, 3).reshape(NYP, NXP)
    taps = gauss_taps().astype(jnp.float32)
    sky_image = template.astype(jnp.float32)
    rows_coord = (jnp.arange(NYP).astype(jnp.float32) + 0.5) * (2.0 / NYP) - 1.0
    cols_coord = (jnp.arange(NXP).astype(jnp.float32) + 0.5) * (2.0 / NXP) - 1.0
    matched = jnp.zeros((NYP, NXP), jnp.float32)
    for basis_index in range(len(sigma_fractions)):
        across = smooth_along(sky_image, taps[basis_index], 1).astype(jnp.bfloat16)
        across = lax.optimization_barrier(across)
        smoothed = smooth_along(across.astype(jnp.float32), taps[basis_index], 0)
        matched = matched + spatial_weight(coefficients[basis_index], rows_coord, cols_coord) * smoothed
    return science - matched
```

```python
import functools

import jax
import jax.numpy as jnp
import numpy as np
from jax import lax
from jax.experimental import pallas as pl
from jax.experimental.pallas import tpu as pltpu
from jax.sharding import PartitionSpec as P

HALO = 16
CAP = 16
LANES = 128
BASES = 3
DEGREE = 4

sigma_fractions = (0.09375, 0.1875, 0.375)
term_powers = [(degree - power_v, power_v) for degree in range(5) for power_v in range(degree + 1)]

DIRS = ((0, 1), (0, -1), (1, 1), (1, -1), (-1, 1), (-1, -1), (1, 0), (-1, 0))
OWN = 4
MESH = pl.DeviceIdType.MESH


def bucket_of(step):
    return 3 * (step[0] + 1) + step[1] + 1


def gauss_taps():
    positions = np.arange(-HALO, HALO + 1).astype(np.float32)
    stacked = []
    for fraction in sigma_fractions:
        sigma = fraction * HALO
        values = np.exp(-positions * positions / np.float32(2.0 * sigma * sigma))
        stacked.append(values / np.sum(values))
    return np.stack(stacked).astype(jnp.bfloat16)


def band_tables():
    taps = gauss_taps()
    across = np.zeros((3 * LANES, BASES * LANES), taps.dtype)
    down = np.zeros((BASES, LANES, 2 * LANES), taps.dtype)
    for basis in range(BASES):
        for out in range(LANES):
            for tap in range(2 * HALO + 1):
                across[LANES - HALO + out + tap, basis * LANES + out] = taps[basis, tap]
                down[basis, out, out + tap] = taps[basis, tap]
    return across, down


def slots_kernel(owner, offset, index, label, count):
    row, col = lax.axis_index("py"), lax.axis_index("px")
    cols = lax.axis_size("px")
    for bucket in range(9):
        count[bucket] = 0

    def clear(slot, carry):
        for bucket in range(9):
            index[bucket, slot] = 0
            label[bucket, slot] = 0
        return carry

    lax.fori_loop(0, CAP, clear, 0)

    def place(piece, carry):
        tile = owner[piece]
        bucket = 3 * (lax.div(tile, cols) - row + 1) + lax.rem(tile, cols) - col + 1
        slot = count[bucket]
        count[bucket] = slot + 1
        index[bucket, slot] = piece
        label[bucket, slot] = offset[piece] + 1
        return carry

    lax.fori_loop(0, owner.shape[0], place, 0)


def send_kernel(
    index, coef, label, pieces, template, band_across, band_down,
    arrived, arrived_label, matched,
    held, outgoing, padded, strip_out, strip_in, across, inner, result,
    load_sem, send_sem, recv_sem, label_send, label_recv, rim_send, rim_recv, out_sem,
):
    rows, cols = lax.axis_size("py"), lax.axis_size("px")
    row, col = lax.axis_index("py"), lax.axis_index("px")
    side = template.shape[0]
    last = side - LANES

    def exists(step):
        r, c = row + step[0], col + step[1]
        return (r >= 0) & (r < rows) & (c >= 0) & (c < cols)

    def neighbour(step):
        return (row + step[0], col + step[1])

    body = padded.at[pl.ds(HALO, side)]
    loads = [
        pltpu.make_async_copy(template.at[:, pl.ds(0, LANES)], body.at[:, pl.ds(LANES, LANES)], load_sem.at[0]),
        pltpu.make_async_copy(template.at[:, pl.ds(last, LANES)], body.at[:, pl.ds(side, LANES)], load_sem.at[1]),
        pltpu.make_async_copy(pieces, held, load_sem.at[2]),
        pltpu.make_async_copy(
            template.at[:, pl.ds(LANES, side - 2 * LANES)],
            body.at[:, pl.ds(2 * LANES, side - 2 * LANES)],
            load_sem.at[3],
        ),
    ]
    for load in loads:
        load.start()

    barrier = pltpu.get_barrier_semaphore()
    for step in DIRS:
        @pl.when(exists(step))
        def _():
            pl.semaphore_signal(barrier, inc=1, device_id=neighbour(step), device_id_type=MESH)
    tall_group = 3 - jnp.where(row == 0, 1, 0) - jnp.where(row == rows - 1, 1, 0)
    wide_group = 3 - jnp.where(col == 0, 1, 0) - jnp.where(col == cols - 1, 1, 0)
    pl.semaphore_wait(barrier, tall_group * wide_group - 1)

    def opposite(step):
        return (-step[0], -step[1])

    def rim_copy(at):
        step = DIRS[at]
        if step[0] == 0:
            source = strip_out.at[0 if step[1] > 0 else 1]
            target = strip_in.at[0 if step[1] > 0 else 1]
        else:
            source_rows = pl.ds(side - HALO if step[0] > 0 else 0, HALO)
            target_rows = pl.ds(0 if step[0] > 0 else side + HALO, HALO)
            if step[1] == 0:
                source = template.at[source_rows]
                target = padded.at[target_rows, pl.ds(LANES, side)]
            else:
                source = template.at[source_rows, pl.ds(last if step[1] > 0 else 0, LANES)]
                target = padded.at[target_rows, pl.ds(0 if step[1] > 0 else side + LANES, LANES)]
        return pltpu.make_async_remote_copy(
            src_ref=source, dst_ref=target, send_sem=rim_send.at[at], recv_sem=rim_recv.at[at],
            device_id=neighbour(step), device_id_type=MESH,
        )

    def label_copy(at):
        return pltpu.make_async_remote_copy(
            src_ref=label, dst_ref=arrived_label.at[at], send_sem=label_send.at[at],
            recv_sem=label_recv.at[at], device_id=neighbour(DIRS[at]), device_id_type=MESH,
        )

    def bucket_copy(at):
        return pltpu.make_async_remote_copy(
            src_ref=outgoing.at[at], dst_ref=arrived.at[at], send_sem=send_sem.at[at],
            recv_sem=recv_sem.at[at], device_id=neighbour(DIRS[at]), device_id_type=MESH,
        )

    def pack_strip(strip, first_col, first_lane):
        lane_group = lax.broadcasted_iota(jnp.int32, (LANES, LANES), 1) // HALO
        packed = jnp.zeros((LANES, LANES), jnp.float32)
        for group in range(side // LANES):
            block = padded[pl.ds(HALO + group * LANES, LANES), pl.ds(first_col, LANES)]
            moved = pltpu.roll(
                block.astype(jnp.float32), (group * HALO - first_lane) % LANES, 1
            )
            packed = jnp.where(lane_group == group, moved, packed)
        strip_out[strip] = packed.astype(jnp.bfloat16)

    loads[0].wait()
    loads[1].wait()
    pack_strip(0, side, LANES - HALO)
    pack_strip(1, LANES, 0)
    for at, step in enumerate(DIRS):
        @pl.when(exists(step))
        def _():
            rim_copy(at).start()
            label_copy(at).start()

    loads[2].wait()
    for at, step in enumerate(DIRS):
        def pack(slot, carry):
            outgoing[at, slot] = held[index[bucket_of(step), slot]]
            return carry

        lax.fori_loop(0, CAP, pack, 0)

        @pl.when(exists(step))
        def _():
            bucket_copy(at).start()

    lane = lax.broadcasted_iota(jnp.int32, (8, side), 1)
    u = ((col * side + lane).astype(jnp.float32) + 0.5) * (2.0 / (side * cols)) - 1.0
    for basis in range(BASES):
        for power_v in range(DEGREE + 1):
            total = jnp.zeros_like(u)
            for power_u in reversed(range(DEGREE + 1 - power_v)):
                total = total * u + coef[basis, term_powers.index((power_u, power_v))]
            inner[basis, power_v] = total

    loads[3].wait()
    wide = padded.shape[1]

    @pl.when(row == 0)
    def _():
        padded[pl.ds(0, HALO)] = jnp.zeros((HALO, wide), jnp.bfloat16)

    @pl.when(row == rows - 1)
    def _():
        padded[pl.ds(side + HALO, HALO)] = jnp.zeros((HALO, wide), jnp.bfloat16)

    @pl.when(col == 0)
    def _():
        padded[:, pl.ds(0, LANES)] = jnp.zeros((padded.shape[0], LANES), jnp.bfloat16)

    @pl.when(col == cols - 1)
    def _():
        padded[:, pl.ds(side + LANES, LANES)] = jnp.zeros((padded.shape[0], LANES), jnp.bfloat16)

    for at, step in enumerate(DIRS):
        @pl.when(exists(opposite(step)))
        def _():
            rim_copy(at).wait_recv()

    def unpack_strip(strip, first_col, first_lane):
        packed = strip_in[strip].astype(jnp.float32)
        for group in range(side // LANES):
            moved = pltpu.roll(packed, (first_lane - group * HALO) % LANES, 1)
            padded[pl.ds(HALO + group * LANES, LANES), pl.ds(first_col, LANES)] = moved.astype(jnp.bfloat16)

    @pl.when(col > 0)
    def _():
        unpack_strip(0, 0, LANES - HALO)

    @pl.when(col < cols - 1)
    def _():
        unpack_strip(1, side + LANES, 0)

    tall = padded.shape[0]
    chunk = tall // 3
    blocks = side // LANES
    for basis in range(BASES):
        across[basis, pl.ds(tall, across.shape[1] - tall)] = jnp.zeros(
            (across.shape[1] - tall, side), jnp.bfloat16
        )

    def row_pass(block, carry):
        first = pl.multiple_of(block * LANES, LANES)
        for part in range(3):
            got = jnp.dot(
                padded[pl.ds(part * chunk, chunk), pl.ds(first, 3 * LANES)],
                band_across[...],
                preferred_element_type=jnp.float32,
            )
            for basis in range(BASES):
                across[basis, pl.ds(part * chunk, chunk), pl.ds(first, LANES)] = got[
                    :, basis * LANES : (basis + 1) * LANES
                ].astype(jnp.bfloat16)
        return carry

    lax.fori_loop(0, blocks, row_pass, 0)

    part_cols = 2 * LANES

    def column_pass(block, carry):
        first = pl.multiple_of(block * LANES, LANES)
        line = lax.broadcasted_iota(jnp.int32, (LANES, part_cols), 0)
        v = ((row * side + first + line).astype(jnp.float32) + 0.5) * (2.0 / (side * rows)) - 1.0
        for part in range(side // part_cols):
            columns = pl.ds(part * part_cols, part_cols)
            total = jnp.zeros((LANES, part_cols), jnp.float32)
            for basis in range(BASES):
                smoothed = jnp.dot(
                    band_down[basis],
                    across[basis, pl.ds(first, 2 * LANES), columns],
                    preferred_element_type=jnp.float32,
                )
                weight = jnp.broadcast_to(inner[basis, DEGREE, 0:1, columns], total.shape)
                for power_v in reversed(range(DEGREE)):
                    weight = weight * v + inner[basis, power_v, 0:1, columns]
                total = total + weight * smoothed
            result[pl.ds(first, LANES), columns] = total
        return carry

    lax.fori_loop(0, blocks, column_pass, 0)
    out = pltpu.make_async_copy(result, matched, out_sem)
    out.start()

    for at, step in enumerate(DIRS):
        @pl.when(exists(step))
        def _():
            rim_copy(at).wait_send()
            label_copy(at).wait_send()
            bucket_copy(at).wait_send()

        @pl.when(exists(opposite(step)))
        def _():
            label_copy(at).wait_recv()
            bucket_copy(at).wait_recv()
    out.wait()


def join_kernel(
    index, label, arrived_label, pieces, arrived, matched, out,
    held, head, following, covered, load_sem,
):
    rows, cols = lax.axis_size("py"), lax.axis_size("px")
    row, col = lax.axis_index("py"), lax.axis_index("px")
    own = pieces.shape[0]
    blocks = head.shape[0]
    per_row = out.shape[1] // LANES

    @pl.when(pl.program_id(0) == 0)
    def _():
        loads = [pltpu.make_async_copy(pieces, held.at[pl.ds(0, own)], load_sem.at[0])]
        for at in range(len(DIRS)):
            loads.append(
                pltpu.make_async_copy(
                    arrived.at[at], held.at[pl.ds(own + at * CAP, CAP)], load_sem.at[at + 1]
                )
            )
        for load in loads:
            load.start()

        def clear(block, carry):
            head[block] = 0
            covered[block] = 0
            return carry

        lax.fori_loop(0, blocks, clear, 0)

        def link(tag, piece):
            @pl.when(tag > 0)
            def _():
                following[piece] = head[tag - 1]
                head[tag - 1] = piece
                covered[tag - 1] = covered[tag - 1] + 1

        def link_own(slot, carry):
            link(label[OWN, slot], index[OWN, slot])
            return carry

        lax.fori_loop(0, CAP, link_own, 0)
        for at, step in enumerate(DIRS):
            r, c = row - step[0], col - step[1]

            @pl.when((r >= 0) & (r < rows) & (c >= 0) & (c < cols))
            def _():
                def link_arrived(slot, carry):
                    link(arrived_label[at, bucket_of(step), slot], own + at * CAP + slot)
                    return carry

                lax.fori_loop(0, CAP, link_arrived, 0)
        for load in loads:
            load.wait()

    for at in range(per_row):
        block = pl.program_id(0) * per_row + at
        count = covered[block]

        def add(_, state):
            piece, total = state
            return following[piece], total + held[piece].astype(jnp.float32)

        _, total = lax.fori_loop(
            0, count, add, (head[block], jnp.zeros((LANES, LANES), jnp.float32))
        )
        share = 1.0 / jnp.full((8, LANES), jnp.maximum(count, 1).astype(jnp.float32))
        columns = pl.ds(at * LANES, LANES)
        out[:, columns] = total * jnp.tile(share, (LANES // 8, 1)) - matched[:, columns]


def on_device(pieces, owner_map, offsets, template, coefficients):
    own, block_side = pieces.shape[0], pieces.shape[1]
    side = template.shape[0]
    blocks = (side // block_side) ** 2
    smem = pl.BlockSpec(memory_space=pltpu.SMEM)
    vmem = pl.BlockSpec(memory_space=pltpu.VMEM)
    anywhere = pl.BlockSpec(memory_space=pl.ANY)
    count = len(DIRS)

    index, label = pl.pallas_call(
        slots_kernel,
        out_shape=[jax.ShapeDtypeStruct((9, LANES), jnp.int32)] * 2,
        in_specs=[smem, smem],
        out_specs=[smem, smem],
        scratch_shapes=[pltpu.SMEM((9,), jnp.int32)],
        name="slots",
    )(owner_map, offsets)

    band_across, band_down = band_tables()
    tall = side + 2 * HALO
    dma = pltpu.SemaphoreType.DMA
    arrived, arrived_label, matched = pl.pallas_call(
        send_kernel,
        out_shape=[
            jax.ShapeDtypeStruct((count, CAP, block_side, block_side), jnp.bfloat16),
            jax.ShapeDtypeStruct((count, 9, LANES), jnp.int32),
            jax.ShapeDtypeStruct((side, side), jnp.float32),
        ],
        in_specs=[smem, smem, anywhere, anywhere, anywhere, vmem, vmem],
        out_specs=[anywhere, anywhere, anywhere],
        scratch_shapes=[
            pltpu.VMEM((own, block_side, block_side), jnp.bfloat16),
            pltpu.VMEM((count, CAP, block_side, block_side), jnp.bfloat16),
            pltpu.VMEM((tall, side + 2 * LANES), jnp.bfloat16),
            pltpu.VMEM((2, LANES, LANES), jnp.bfloat16),
            pltpu.VMEM((2, LANES, LANES), jnp.bfloat16),
            pltpu.VMEM((BASES, side + LANES, side), jnp.bfloat16),
            pltpu.VMEM((BASES, DEGREE + 1, 8, side), jnp.float32),
            pltpu.VMEM((side, side), jnp.float32),
            dma((4,)), dma((count,)), dma((count,)), dma((count,)), dma((count,)),
            dma((count,)), dma((count,)), dma,
        ],
        compiler_params=pltpu.CompilerParams(
            collective_id=0, has_side_effects=True, vmem_limit_bytes=48 << 20
        ),
        name="send",
    )(index, coefficients, label, pieces, template, jnp.asarray(band_across), jnp.asarray(band_down))

    row_block = pl.BlockSpec((block_side, side), lambda i: (i, 0))
    return pl.pallas_call(
        join_kernel,
        grid=(side // block_side,),
        out_shape=jax.ShapeDtypeStruct((side, side), jnp.float32),
        in_specs=[smem, smem, smem, anywhere, anywhere, row_block],
        out_specs=row_block,
        scratch_shapes=[
            pltpu.VMEM((own + count * CAP, block_side, block_side), jnp.bfloat16),
            pltpu.SMEM((blocks,), jnp.int32),
            pltpu.SMEM((own + count * CAP,), jnp.int32),
            pltpu.SMEM((blocks,), jnp.int32),
            dma((count + 1,)),
        ],
        compiler_params=pltpu.CompilerParams(vmem_limit_bytes=32 << 20),
        name="join",
    )(index, label, arrived_label, pieces, arrived, matched)


def solution(mesh):
    in_specs = (P(("py", "px"), None, None), P(("py", "px")), P(("py", "px")), P("py", "px"), P())
    out_specs = P("py", "px")
    return jax.shard_map(
        on_device, mesh=mesh, in_specs=in_specs, out_specs=out_specs, check_vma=False
    )
```

```python
import functools

import jax
import jax.numpy as jnp
import numpy as np
from jax import lax
from jax.experimental import pallas as pl
from jax.experimental.pallas import tpu as pltpu
from jax.sharding import PartitionSpec as P

HALO = 16
CAP = 16
LANES = 128
BASES = 3
DEGREE = 4

sigma_fractions = (0.09375, 0.1875, 0.375)
term_powers = [(degree - power_v, power_v) for degree in range(5) for power_v in range(degree + 1)]

DIRS = ((1, 1), (-1, -1), (1, -1), (-1, 1), (0, 1), (0, -1), (1, 0), (-1, 0))
OWN = 4
MESH = pl.DeviceIdType.MESH


def bucket_of(step):
    return 3 * (step[0] + 1) + step[1] + 1


def gauss_taps():
    positions = np.arange(-HALO, HALO + 1).astype(np.float32)
    stacked = []
    for fraction in sigma_fractions:
        sigma = fraction * HALO
        values = np.exp(-positions * positions / np.float32(2.0 * sigma * sigma))
        stacked.append(values / np.sum(values))
    return np.stack(stacked).astype(jnp.bfloat16)


def band_tables():
    taps = gauss_taps()
    across = np.zeros((3 * LANES, BASES * LANES), taps.dtype)
    down = np.zeros((BASES, LANES, 2 * LANES), taps.dtype)
    for basis in range(BASES):
        for out in range(LANES):
            for tap in range(2 * HALO + 1):
                across[LANES - HALO + out + tap, basis * LANES + out] = taps[basis, tap]
                down[basis, out, out + tap] = taps[basis, tap]
    return across, down


def send_kernel(
    owner, offset, coef, pieces, template, band_across, band_down,
    arrived, tags, matched,
    held, owner_row, offset_row, table, table_scalar, arrived_table,
    outgoing, padded, strip_out, strip_in, across, inner, row_band, down_band,
    load_sem, table_sem, send_sem, recv_sem, label_send, label_recv, rim_send, rim_recv,
):
    rows, cols = lax.axis_size("py"), lax.axis_size("px")
    row, col = lax.axis_index("py"), lax.axis_index("px")
    side = template.shape[0]
    last = side - LANES
    own = held.shape[0]

    def exists(step):
        r, c = row + step[0], col + step[1]
        return (r >= 0) & (r < rows) & (c >= 0) & (c < cols)

    def neighbour(step):
        return (row + step[0], col + step[1])

    body = padded.at[pl.ds(HALO, side)]
    loads = [
        pltpu.make_async_copy(owner, owner_row, load_sem.at[0]),
        pltpu.make_async_copy(offset, offset_row, load_sem.at[1]),
        pltpu.make_async_copy(pieces, held, load_sem.at[2]),
        pltpu.make_async_copy(
            template.at[:, pl.ds(0, LANES)], body.at[:, pl.ds(LANES, LANES)], load_sem.at[3]
        ),
        pltpu.make_async_copy(
            template.at[:, pl.ds(last, LANES)], body.at[:, pl.ds(side, LANES)], load_sem.at[4]
        ),
        pltpu.make_async_copy(
            template.at[:, pl.ds(LANES, side - 2 * LANES)],
            body.at[:, pl.ds(2 * LANES, side - 2 * LANES)],
            load_sem.at[5],
        ),
        pltpu.make_async_copy(band_across, row_band, load_sem.at[6]),
        pltpu.make_async_copy(band_down, down_band, load_sem.at[7]),
    ]
    for load in loads:
        load.start()

    barrier = pltpu.get_barrier_semaphore()
    for step in DIRS:
        @pl.when(exists(step))
        def _():
            pl.semaphore_signal(barrier, inc=1, device_id=neighbour(step), device_id_type=MESH)
    tall_group = 3 - jnp.where(row == 0, 1, 0) - jnp.where(row == rows - 1, 1, 0)
    wide_group = 3 - jnp.where(col == 0, 1, 0) - jnp.where(col == cols - 1, 1, 0)

    loads[0].wait()
    loads[1].wait()
    bucket_id = lax.broadcasted_iota(jnp.int32, (16, own), 0)
    target = jnp.full((16, own), -1, jnp.int32)
    for bucket in range(9):
        tile = (row + bucket // 3 - 1) * cols + col + bucket % 3 - 1
        target = jnp.where(bucket_id == bucket, tile, target)
    belongs = target == jnp.broadcast_to(owner_row[...], (16, own))
    earlier = (
        lax.broadcasted_iota(jnp.int32, (own, own), 0)
        < lax.broadcasted_iota(jnp.int32, (own, own), 1)
    )
    place = jnp.dot(
        jnp.where(belongs, 1.0, 0.0), jnp.where(earlier, 1.0, 0.0),
        preferred_element_type=jnp.float32,
    )
    code = lax.broadcasted_iota(jnp.int32, (16, own), 1) + own * (
        jnp.broadcast_to(offset_row[...], (16, own)) + 1
    )
    code = jnp.where(belongs, code.astype(jnp.float32), 0.0)
    slot_lane = lax.broadcasted_iota(jnp.int32, (16, LANES), 1)
    filled = jnp.zeros((16, LANES), jnp.float32)
    for slot in range(CAP):
        picked = jnp.sum(jnp.where(place == slot, code, 0.0), axis=1, keepdims=True)
        filled = jnp.where(slot_lane == slot, picked, filled)
    table[...] = filled.astype(jnp.int32)
    to_scalar = pltpu.make_async_copy(table, table_scalar, table_sem)
    to_scalar.start()

    loads[2].wait()
    to_scalar.wait()
    pl.semaphore_wait(barrier, tall_group * wide_group - 1)

    def opposite(step):
        return (-step[0], -step[1])

    def rim_copy(at):
        step = DIRS[at]
        if step[0] == 0:
            source = strip_out.at[0 if step[1] > 0 else 1]
            target = strip_in.at[0 if step[1] > 0 else 1]
        else:
            source_rows = pl.ds(side - HALO if step[0] > 0 else 0, HALO)
            target_rows = pl.ds(0 if step[0] > 0 else side + HALO, HALO)
            if step[1] == 0:
                source = template.at[source_rows]
                target = padded.at[target_rows, pl.ds(LANES, side)]
            else:
                source = template.at[source_rows, pl.ds(last if step[1] > 0 else 0, LANES)]
                target = padded.at[target_rows, pl.ds(0 if step[1] > 0 else side + LANES, LANES)]
        return pltpu.make_async_remote_copy(
            src_ref=source, dst_ref=target, send_sem=rim_send.at[at], recv_sem=rim_recv.at[at],
            device_id=neighbour(step), device_id_type=MESH,
        )

    def label_copy(at):
        return pltpu.make_async_remote_copy(
            src_ref=table, dst_ref=arrived_table.at[at], send_sem=label_send.at[at],
            recv_sem=label_recv.at[at], device_id=neighbour(DIRS[at]), device_id_type=MESH,
        )

    def bucket_copy(at, slots=pl.ds(0, CAP)):
        return pltpu.make_async_remote_copy(
            src_ref=outgoing.at[at, slots], dst_ref=arrived.at[at, slots], send_sem=send_sem.at[at],
            recv_sem=recv_sem.at[at], device_id=neighbour(DIRS[at]), device_id_type=MESH,
        )

    def pack_strip(strip, first_col, first_lane):
        lane_group = lax.broadcasted_iota(jnp.int32, (LANES, LANES), 1) // HALO
        packed = jnp.zeros((LANES, LANES), jnp.float32)
        for group in range(side // LANES):
            block = padded[pl.ds(HALO + group * LANES, LANES), pl.ds(first_col, LANES)]
            moved = pltpu.roll(
                block.astype(jnp.float32), (group * HALO - first_lane) % LANES, 1
            )
            packed = jnp.where(lane_group == group, moved, packed)
        strip_out[strip] = packed.astype(jnp.bfloat16)

    def send_slot(slot, carry):
        for at, step in enumerate(DIRS):
            piece = table_scalar[bucket_of(step), slot] & (own - 1)
            outgoing[at, slot] = held[piece]

            @pl.when(exists(step))
            def _():
                bucket_copy(at, pl.ds(slot, 1)).start()
        arrived[len(DIRS), slot] = held[table_scalar[OWN, slot] & (own - 1)]
        return carry

    lax.fori_loop(0, 2, send_slot, 0)
    loads[3].wait()
    loads[4].wait()
    pack_strip(0, side, LANES - HALO)
    pack_strip(1, LANES, 0)
    for at, step in enumerate(DIRS):
        @pl.when(exists(step))
        def _():
            rim_copy(at).start()
            label_copy(at).start()
    lax.fori_loop(2, CAP, send_slot, 0)

    lane = lax.broadcasted_iota(jnp.int32, (8, side), 1)
    u = ((col * side + lane).astype(jnp.float32) + 0.5) * (2.0 / (side * cols)) - 1.0
    for basis in range(BASES):
        for power_v in range(DEGREE + 1):
            total = jnp.zeros_like(u)
            for power_u in reversed(range(DEGREE + 1 - power_v)):
                total = total * u + coef[basis, term_powers.index((power_u, power_v))]
            inner[basis, power_v] = total

    for load in loads[5:]:
        load.wait()
    wide = padded.shape[1]

    @pl.when(row == 0)
    def _():
        padded[pl.ds(0, HALO)] = jnp.zeros((HALO, wide), jnp.bfloat16)

    @pl.when(row == rows - 1)
    def _():
        padded[pl.ds(side + HALO, HALO)] = jnp.zeros((HALO, wide), jnp.bfloat16)

    @pl.when(col == 0)
    def _():
        padded[:, pl.ds(0, LANES)] = jnp.zeros((padded.shape[0], LANES), jnp.bfloat16)

    @pl.when(col == cols - 1)
    def _():
        padded[:, pl.ds(side + LANES, LANES)] = jnp.zeros((padded.shape[0], LANES), jnp.bfloat16)

    for at, step in enumerate(DIRS):
        @pl.when(exists(opposite(step)))
        def _():
            rim_copy(at).wait_recv()

    def unpack_strip(strip, first_col, first_lane):
        packed = strip_in[strip].astype(jnp.float32)
        for group in range(side // LANES):
            moved = pltpu.roll(packed, (first_lane - group * HALO) % LANES, 1)
            padded[pl.ds(HALO + group * LANES, LANES), pl.ds(first_col, LANES)] = moved.astype(jnp.bfloat16)

    @pl.when(col > 0)
    def _():
        unpack_strip(0, 0, LANES - HALO)

    @pl.when(col < cols - 1)
    def _():
        unpack_strip(1, side + LANES, 0)

    tall = padded.shape[0]
    chunk = tall // 3
    blocks = side // LANES
    for basis in range(BASES):
        across[basis, pl.ds(tall, across.shape[1] - tall)] = jnp.zeros(
            (across.shape[1] - tall, side), jnp.bfloat16
        )

    def row_pass(block, carry):
        first = pl.multiple_of(block * LANES, LANES)
        for part in range(3):
            got = jnp.dot(
                padded[pl.ds(part * chunk, chunk), pl.ds(first, 3 * LANES)],
                row_band[...],
                preferred_element_type=jnp.float32,
            )
            for basis in range(BASES):
                across[basis, pl.ds(part * chunk, chunk), pl.ds(first, LANES)] = got[
                    :, basis * LANES : (basis + 1) * LANES
                ].astype(jnp.bfloat16)
        return carry

    lax.fori_loop(0, blocks, row_pass, 0)

    part_cols = 2 * LANES

    def column_pass(block, carry):
        first = pl.multiple_of(block * LANES, LANES)
        line = lax.broadcasted_iota(jnp.int32, (LANES, part_cols), 0)
        v = ((row * side + first + line).astype(jnp.float32) + 0.5) * (2.0 / (side * rows)) - 1.0
        for part in range(side // part_cols):
            columns = pl.ds(part * part_cols, part_cols)
            total = jnp.zeros((LANES, part_cols), jnp.float32)
            for basis in range(BASES):
                smoothed = jnp.dot(
                    down_band[basis],
                    across[basis, pl.ds(first, 2 * LANES), columns],
                    preferred_element_type=jnp.float32,
                )
                weight = jnp.broadcast_to(inner[basis, DEGREE, 0:1, columns], total.shape)
                for power_v in reversed(range(DEGREE)):
                    weight = weight * v + inner[basis, power_v, 0:1, columns]
                total = total + weight * smoothed
            matched[pl.ds(first, LANES), columns] = total
        return carry

    lax.fori_loop(0, blocks, column_pass, 0)

    for at, step in enumerate(DIRS):
        tags[pl.ds(at, 1)] = jnp.zeros((1, LANES), jnp.int32)

        @pl.when(exists(opposite(step)))
        def _():
            label_copy(at).wait_recv()
            tags[pl.ds(at, 1)] = arrived_table[at, pl.ds(bucket_of(step), 1)]
    tags[pl.ds(len(DIRS), 1)] = table[pl.ds(OWN, 1)]

    for at, step in enumerate(DIRS):
        @pl.when(exists(step))
        def _():
            rim_copy(at).wait_send()
            label_copy(at).wait_send()
            bucket_copy(at).wait_send()

        @pl.when(exists(opposite(step)))
        def _():
            bucket_copy(at).wait_recv()


def join_kernel(own, tags, arrived, matched, out, result, head, following, covered, out_sem):
    blocks = head.shape[0]
    side = out.shape[1]
    per_row = side // LANES

    def clear(block, carry):
        head[block] = 0
        covered[block] = 0
        return carry

    lax.fori_loop(0, blocks, clear, 0, unroll=8)

    def link(code, piece):
        tag = lax.div(code, own)

        @pl.when(tag > 0)
        def _():
            following[piece] = head[tag - 1]
            head[tag - 1] = piece
            covered[tag - 1] = covered[tag - 1] + 1

    def link_slot(slot, carry):
        for at in range(len(DIRS) + 1):
            link(tags[at, slot], at * CAP + slot)
        return carry

    lax.fori_loop(0, CAP, link_slot, 0)

    def out_copy(block_row):
        lines = pl.ds(pl.multiple_of(block_row * LANES, LANES), LANES)
        return pltpu.make_async_copy(result.at[lines], out.at[lines], out_sem.at[block_row])

    def join_row(block_row, carry):
        lines = pl.ds(pl.multiple_of(block_row * LANES, LANES), LANES)
        for at in range(per_row):
            block = block_row * per_row + at
            count = covered[block]

            def add(_, state):
                piece, total = state
                return following[piece], total + arrived[lax.div(piece, CAP), piece & (CAP - 1)].astype(jnp.float32)

            _, total = lax.fori_loop(
                0, count, add, (head[block], jnp.zeros((LANES, LANES), jnp.float32))
            )
            share = 1.0 / jnp.full((8, LANES), jnp.maximum(count, 1).astype(jnp.float32))
            columns = pl.ds(at * LANES, LANES)
            result[lines, columns] = total * jnp.tile(share, (LANES // 8, 1)) - matched[lines, columns]
        out_copy(block_row).start()
        return carry

    lax.fori_loop(0, per_row, join_row, 0)
    for block_row in range(per_row):
        out_copy(block_row).wait()


def on_device(pieces, owner_map, offsets, template, coefficients):
    own, block_side = pieces.shape[0], pieces.shape[1]
    side = template.shape[0]
    blocks = (side // block_side) ** 2
    smem = pl.BlockSpec(memory_space=pltpu.SMEM)
    vmem = pl.BlockSpec(memory_space=pltpu.VMEM)
    hbm = pl.BlockSpec(memory_space=pltpu.HBM)
    count = len(DIRS)

    band_across, band_down = band_tables()
    tall = side + 2 * HALO
    dma = pltpu.SemaphoreType.DMA
    arrived, tags, matched = pl.pallas_call(
        send_kernel,
        out_shape=[
            jax.ShapeDtypeStruct((count + 1, CAP, block_side, block_side), jnp.bfloat16),
            jax.ShapeDtypeStruct((16, LANES), jnp.int32),
            jax.ShapeDtypeStruct((side, side), jnp.float32),
        ],
        in_specs=[hbm, hbm, smem, hbm, hbm, hbm, hbm],
        out_specs=[vmem, vmem, vmem],
        scratch_shapes=[
            pltpu.VMEM((own, block_side, block_side), jnp.bfloat16),
            pltpu.VMEM((1, own), jnp.int32),
            pltpu.VMEM((1, own), jnp.int32),
            pltpu.VMEM((16, LANES), jnp.int32),
            pltpu.SMEM((16, LANES), jnp.int32),
            pltpu.VMEM((count, 16, LANES), jnp.int32),
            pltpu.VMEM((count, CAP, block_side, block_side), jnp.bfloat16),
            pltpu.VMEM((tall, side + 2 * LANES), jnp.bfloat16),
            pltpu.VMEM((2, LANES, LANES), jnp.bfloat16),
            pltpu.VMEM((2, LANES, LANES), jnp.bfloat16),
            pltpu.VMEM((BASES, side + LANES, side), jnp.bfloat16),
            pltpu.VMEM((BASES, DEGREE + 1, 8, side), jnp.float32),
            pltpu.VMEM(band_across.shape, jnp.bfloat16),
            pltpu.VMEM(band_down.shape, jnp.bfloat16),
            dma((8,)), dma, dma((count,)), dma((count,)), dma((count,)), dma((count,)),
            dma((count,)), dma((count,)),
        ],
        compiler_params=pltpu.CompilerParams(
            collective_id=0, has_side_effects=True, vmem_limit_bytes=40 << 20
        ),
        name="send",
    )(
        *(
            pltpu.with_memory_space_constraint(array, pltpu.HBM)
            for array in (
                owner_map.reshape(1, own), offsets.reshape(1, own), coefficients, pieces,
                template, jnp.asarray(band_across), jnp.asarray(band_down),
            )
        )
    )
    return pl.pallas_call(
        functools.partial(join_kernel, own),
        out_shape=jax.ShapeDtypeStruct((side, side), jnp.float32),
        in_specs=[smem, vmem, vmem],
        out_specs=hbm,
        scratch_shapes=[
            pltpu.VMEM((side, side), jnp.float32),
            pltpu.SMEM((blocks,), jnp.int32),
            pltpu.SMEM(((count + 1) * CAP,), jnp.int32),
            pltpu.SMEM((blocks,), jnp.int32),
            dma((side // block_side,)),
        ],
        compiler_params=pltpu.CompilerParams(vmem_limit_bytes=32 << 20),
        name="join",
    )(tags, arrived, matched)


def solution(mesh):
    in_specs = (P(("py", "px"), None, None), P(("py", "px")), P(("py", "px")), P("py", "px"), P())
    out_specs = P("py", "px")
    return jax.shard_map(
        on_device, mesh=mesh, in_specs=in_specs, out_specs=out_specs, check_vma=False
    )
```

```python
import functools

import jax
import jax.numpy as jnp
import numpy as np
from jax import lax
from jax.experimental import pallas as pl
from jax.experimental.pallas import tpu as pltpu
from jax.sharding import PartitionSpec as P

HALO = 16
CAP = 16
LANES = 128
BASES = 3
DEGREE = 4

sigma_fractions = (0.09375, 0.1875, 0.375)
term_powers = [(degree - power_v, power_v) for degree in range(5) for power_v in range(degree + 1)]

DIRS = ((1, 1), (-1, -1), (1, -1), (-1, 1), (0, 1), (0, -1), (1, 0), (-1, 0))
OWN = 4
MESH = pl.DeviceIdType.MESH


def bucket_of(step):
    return 3 * (step[0] + 1) + step[1] + 1


def gauss_taps():
    positions = np.arange(-HALO, HALO + 1).astype(np.float32)
    stacked = []
    for fraction in sigma_fractions:
        sigma = fraction * HALO
        values = np.exp(-positions * positions / np.float32(2.0 * sigma * sigma))
        stacked.append(values / np.sum(values))
    return np.stack(stacked).astype(jnp.bfloat16)


def band_tables():
    taps = gauss_taps()
    across = np.zeros((3 * LANES, BASES * LANES), taps.dtype)
    down = np.zeros((BASES, LANES, 2 * LANES), taps.dtype)
    for basis in range(BASES):
        for out in range(LANES):
            for tap in range(2 * HALO + 1):
                across[LANES - HALO + out + tap, basis * LANES + out] = taps[basis, tap]
                down[basis, out, out + tap] = taps[basis, tap]
    return across, down


def sort_plan(own, per_row, tags, plan, share):
    count = len(DIRS)
    blocks = per_row * per_row
    shape = (blocks, LANES)
    code = tags[...]
    block_tag = lax.shift_right_logical(code, own.bit_length() - 1).astype(jnp.float32)
    spread = jnp.zeros((8, LANES), jnp.float32)
    for at in range(count):
        one = jnp.broadcast_to(block_tag[at : at + 1], (8, LANES))
        spread = spread + pltpu.roll(one, at * CAP, 1)
    groups = (spread[0:1], block_tag[count : count + 1])

    block_id = lax.broadcasted_iota(jnp.int32, shape, 0).astype(jnp.float32)
    before = jnp.where(
        lax.broadcasted_iota(jnp.int32, (LANES, LANES), 0)
        < lax.broadcasted_iota(jnp.int32, (LANES, LANES), 1), 1.0, 0.0,
    )
    lower = jnp.where(
        lax.broadcasted_iota(jnp.int32, (blocks, blocks), 1)
        < lax.broadcasted_iota(jnp.int32, (blocks, blocks), 0), 1.0, 0.0,
    )
    hits = [jnp.where(jnp.broadcast_to(tag, shape) == block_id + 1, 1.0, 0.0) for tag in groups]
    sums = [jnp.broadcast_to(jnp.sum(hit, axis=1, keepdims=True), shape) for hit in hits]
    covered = sums[0] + sums[1]
    first = jnp.dot(lower, covered, preferred_element_type=jnp.float32)
    ahead = (first, first + sums[0])

    line = lax.broadcasted_iota(jnp.int32, (8, LANES), 0)
    lane = lax.broadcasted_iota(jnp.int32, (8, LANES), 1).astype(jnp.float32)
    target = lax.broadcasted_iota(jnp.int32, (2 * LANES, LANES), 0).astype(jnp.float32)
    over_lanes = (((1,), (1,)), ((), ()))
    listed = jnp.zeros((8, 2 * LANES), jnp.float32)
    ends = jnp.zeros((8, 2 * LANES), jnp.float32)
    for group in range(2):
        hit, tag = hits[group], groups[group]
        rank = ahead[group] + jnp.dot(hit, before, preferred_element_type=jnp.float32)
        place = jnp.sum(hit * rank, axis=0, keepdims=True)
        shares = jnp.sum(hit * covered, axis=0, keepdims=True)
        place = jnp.where(tag > 0, place, -1.0)
        chosen = jnp.where(jnp.broadcast_to(place, target.shape) == target, 1.0, 0.0)
        values = jnp.where(line == 0, lane + group * LANES, 0.0)
        values = jnp.where(line == 1, jnp.broadcast_to(tag - 1, values.shape), values)
        values = jnp.where(line == 2, jnp.broadcast_to(shares, values.shape), values)
        listed = listed + lax.dot_general(
            values, chosen, over_lanes, preferred_element_type=jnp.float32
        )
        wide_tag = jnp.broadcast_to(tag, target.shape)
        inside = jnp.where((wide_tag > 0) & (wide_tag <= (target + 1) * per_row), 1.0, 0.0)
        ends = ends + lax.dot_general(
            jnp.ones((8, LANES), jnp.float32), inside, over_lanes,
            preferred_element_type=jnp.float32,
        )
    wide_line = lax.broadcasted_iota(jnp.int32, listed.shape, 0)
    plan[...] = jnp.where(wide_line == 2, ends, listed).astype(jnp.int32)
    share[...] = 1.0 / jnp.maximum(listed, 1.0)


def send_kernel(
    owner, offset, coef, pieces, template, band_across, band_down,
    arrived, plan, share, matched,
    held, owner_row, offset_row, table, table_scalar, arrived_table,
    tags, outgoing, padded, strip_out, strip_in, across, inner, row_band, down_band,
    load_sem, table_sem, send_sem, recv_sem, label_send, label_recv, rim_send, rim_recv,
):
    rows, cols = lax.axis_size("py"), lax.axis_size("px")
    row, col = lax.axis_index("py"), lax.axis_index("px")
    side = template.shape[0]
    last = side - LANES
    own = held.shape[0]

    def exists(step):
        r, c = row + step[0], col + step[1]
        return (r >= 0) & (r < rows) & (c >= 0) & (c < cols)

    def neighbour(step):
        return (row + step[0], col + step[1])

    barrier = pltpu.get_barrier_semaphore()
    for step in DIRS:
        @pl.when(exists(step))
        def _():
            pl.semaphore_signal(barrier, inc=1, device_id=neighbour(step), device_id_type=MESH)

    body = padded.at[pl.ds(HALO, side)]
    loads = [
        pltpu.make_async_copy(owner, owner_row, load_sem.at[0]),
        pltpu.make_async_copy(offset, offset_row, load_sem.at[1]),
        pltpu.make_async_copy(
            template.at[:, pl.ds(0, LANES)], body.at[:, pl.ds(LANES, LANES)], load_sem.at[2]
        ),
        pltpu.make_async_copy(
            template.at[:, pl.ds(last, LANES)], body.at[:, pl.ds(side, LANES)], load_sem.at[3]
        ),
        pltpu.make_async_copy(pieces, held, load_sem.at[4]),
        pltpu.make_async_copy(
            template.at[:, pl.ds(LANES, side - 2 * LANES)],
            body.at[:, pl.ds(2 * LANES, side - 2 * LANES)],
            load_sem.at[5],
        ),
        pltpu.make_async_copy(band_across, row_band, load_sem.at[6]),
        pltpu.make_async_copy(band_down, down_band, load_sem.at[7]),
    ]
    for load in loads:
        load.start()

    loads[0].wait()
    loads[1].wait()
    bucket_id = lax.broadcasted_iota(jnp.int32, (16, own), 0)
    target = jnp.full((16, own), -1, jnp.int32)
    for bucket in range(9):
        tile = (row + bucket // 3 - 1) * cols + col + bucket % 3 - 1
        target = jnp.where(bucket_id == bucket, tile, target)
    belongs = target == jnp.broadcast_to(owner_row[...], (16, own))
    earlier = (
        lax.broadcasted_iota(jnp.int32, (own, own), 0)
        < lax.broadcasted_iota(jnp.int32, (own, own), 1)
    )
    place = jnp.dot(
        jnp.where(belongs, 1.0, 0.0), jnp.where(earlier, 1.0, 0.0),
        preferred_element_type=jnp.float32,
    )
    code = lax.broadcasted_iota(jnp.int32, (16, own), 1) + own * (
        jnp.broadcast_to(offset_row[...], (16, own)) + 1
    )
    code = jnp.where(belongs, code.astype(jnp.float32), 0.0)
    slot_lane = lax.broadcasted_iota(jnp.int32, (16, LANES), 1)
    filled = jnp.zeros((16, LANES), jnp.float32)
    for slot in range(CAP):
        picked = jnp.sum(jnp.where(place == slot, code, 0.0), axis=1, keepdims=True)
        filled = jnp.where(slot_lane == slot, picked, filled)
    table[...] = filled.astype(jnp.int32)
    to_scalar = pltpu.make_async_copy(table, table_scalar, table_sem)
    to_scalar.start()

    def opposite(step):
        return (-step[0], -step[1])

    def rim_copy(at):
        step = DIRS[at]
        if step[0] == 0:
            source = strip_out.at[0 if step[1] > 0 else 1]
            target = strip_in.at[0 if step[1] > 0 else 1]
        else:
            source_rows = pl.ds(side - HALO if step[0] > 0 else 0, HALO)
            target_rows = pl.ds(0 if step[0] > 0 else side + HALO, HALO)
            if step[1] == 0:
                source = template.at[source_rows]
                target = padded.at[target_rows, pl.ds(LANES, side)]
            else:
                source = template.at[source_rows, pl.ds(last if step[1] > 0 else 0, LANES)]
                target = padded.at[target_rows, pl.ds(0 if step[1] > 0 else side + LANES, LANES)]
        return pltpu.make_async_remote_copy(
            src_ref=source, dst_ref=target, send_sem=rim_send.at[at], recv_sem=rim_recv.at[at],
            device_id=neighbour(step), device_id_type=MESH,
        )

    def label_copy(at):
        return pltpu.make_async_remote_copy(
            src_ref=table, dst_ref=arrived_table.at[at], send_sem=label_send.at[at],
            recv_sem=label_recv.at[at], device_id=neighbour(DIRS[at]), device_id_type=MESH,
        )

    def bucket_copy(at, slots=pl.ds(0, CAP)):
        return pltpu.make_async_remote_copy(
            src_ref=outgoing.at[at, slots], dst_ref=arrived.at[at, slots], send_sem=send_sem.at[at],
            recv_sem=recv_sem.at[at], device_id=neighbour(DIRS[at]), device_id_type=MESH,
        )

    def pack_strip(strip, first_col, first_lane):
        lane_group = lax.broadcasted_iota(jnp.int32, (LANES, LANES), 1) // HALO
        packed = jnp.zeros((LANES, LANES), jnp.float32)
        for group in range(side // LANES):
            block = padded[pl.ds(HALO + group * LANES, LANES), pl.ds(first_col, LANES)]
            moved = pltpu.roll(
                block.astype(jnp.float32), (group * HALO - first_lane) % LANES, 1
            )
            packed = jnp.where(lane_group == group, moved, packed)
        strip_out[strip] = packed.astype(jnp.bfloat16)

    def send_slot(slot, carry):
        for at, step in enumerate(DIRS):
            piece = table_scalar[bucket_of(step), slot] & (own - 1)
            outgoing[at, slot] = held[piece]

            @pl.when(exists(step))
            def _():
                bucket_copy(at, pl.ds(slot, 1)).start()
        arrived[len(DIRS), slot] = held[table_scalar[OWN, slot] & (own - 1)]
        return carry

    loads[2].wait()
    loads[3].wait()
    pack_strip(0, side, LANES - HALO)
    pack_strip(1, LANES, 0)
    tall_group = 3 - jnp.where(row == 0, 1, 0) - jnp.where(row == rows - 1, 1, 0)
    wide_group = 3 - jnp.where(col == 0, 1, 0) - jnp.where(col == cols - 1, 1, 0)
    pl.semaphore_wait(barrier, tall_group * wide_group - 1)
    for at, step in enumerate(DIRS):
        @pl.when(exists(step))
        def _():
            rim_copy(at).start()
            label_copy(at).start()
    loads[4].wait()
    to_scalar.wait()
    lax.fori_loop(0, CAP, send_slot, 0)

    lane = lax.broadcasted_iota(jnp.int32, (8, side), 1)
    u = ((col * side + lane).astype(jnp.float32) + 0.5) * (2.0 / (side * cols)) - 1.0
    for basis in range(BASES):
        for power_v in range(DEGREE + 1):
            total = jnp.zeros_like(u)
            for power_u in reversed(range(DEGREE + 1 - power_v)):
                total = total * u + coef[basis, term_powers.index((power_u, power_v))]
            inner[basis, power_v] = total

    for load in loads[5:]:
        load.wait()
    wide = padded.shape[1]

    @pl.when(row == 0)
    def _():
        padded[pl.ds(0, HALO)] = jnp.zeros((HALO, wide), jnp.bfloat16)

    @pl.when(row == rows - 1)
    def _():
        padded[pl.ds(side + HALO, HALO)] = jnp.zeros((HALO, wide), jnp.bfloat16)

    @pl.when(col == 0)
    def _():
        padded[:, pl.ds(0, LANES)] = jnp.zeros((padded.shape[0], LANES), jnp.bfloat16)

    @pl.when(col == cols - 1)
    def _():
        padded[:, pl.ds(side + LANES, LANES)] = jnp.zeros((padded.shape[0], LANES), jnp.bfloat16)

    for at, step in enumerate(DIRS):
        @pl.when(exists(opposite(step)))
        def _():
            rim_copy(at).wait_recv()

    def unpack_strip(strip, first_col, first_lane):
        packed = strip_in[strip].astype(jnp.float32)
        for group in range(side // LANES):
            moved = pltpu.roll(packed, (first_lane - group * HALO) % LANES, 1)
            padded[pl.ds(HALO + group * LANES, LANES), pl.ds(first_col, LANES)] = moved.astype(jnp.bfloat16)

    @pl.when(col > 0)
    def _():
        unpack_strip(0, 0, LANES - HALO)

    @pl.when(col < cols - 1)
    def _():
        unpack_strip(1, side + LANES, 0)

    tall = padded.shape[0]
    chunk = tall // 3
    blocks = side // LANES
    for basis in range(BASES):
        across[basis, pl.ds(tall, across.shape[1] - tall)] = jnp.zeros(
            (across.shape[1] - tall, side), jnp.bfloat16
        )

    def row_pass(block, carry):
        first = pl.multiple_of(block * LANES, LANES)
        for part in range(3):
            got = jnp.dot(
                padded[pl.ds(part * chunk, chunk), pl.ds(first, 3 * LANES)],
                row_band[...],
                preferred_element_type=jnp.float32,
            )
            for basis in range(BASES):
                across[basis, pl.ds(part * chunk, chunk), pl.ds(first, LANES)] = got[
                    :, basis * LANES : (basis + 1) * LANES
                ].astype(jnp.bfloat16)
        return carry

    lax.fori_loop(0, blocks, row_pass, 0)

    part_cols = 2 * LANES

    def column_pass(block, carry):
        first = pl.multiple_of(block * LANES, LANES)
        line = lax.broadcasted_iota(jnp.int32, (LANES, part_cols), 0)
        v = ((row * side + first + line).astype(jnp.float32) + 0.5) * (2.0 / (side * rows)) - 1.0
        for part in range(side // part_cols):
            columns = pl.ds(part * part_cols, part_cols)
            total = jnp.zeros((LANES, part_cols), jnp.float32)
            for basis in range(BASES):
                smoothed = jnp.dot(
                    down_band[basis],
                    across[basis, pl.ds(first, 2 * LANES), columns],
                    preferred_element_type=jnp.float32,
                )
                weight = jnp.broadcast_to(inner[basis, DEGREE, 0:1, columns], total.shape)
                for power_v in reversed(range(DEGREE)):
                    weight = weight * v + inner[basis, power_v, 0:1, columns]
                total = total - weight * smoothed
            matched[pl.ds(first, LANES), columns] = total
        return carry

    lax.fori_loop(0, blocks, column_pass, 0)

    for at, step in enumerate(DIRS):
        tags[pl.ds(at, 1)] = jnp.zeros((1, LANES), jnp.int32)

        @pl.when(exists(opposite(step)))
        def _():
            label_copy(at).wait_recv()
            tags[pl.ds(at, 1)] = arrived_table[at, pl.ds(bucket_of(step), 1)]
    tags[pl.ds(len(DIRS), 1)] = table[pl.ds(OWN, 1)]
    sort_plan(own, side // LANES, tags, plan, share)

    for at, step in enumerate(DIRS):
        @pl.when(exists(step))
        def _():
            rim_copy(at).wait_send()
            label_copy(at).wait_send()
            bucket_copy(at).wait_send()

        @pl.when(exists(opposite(step)))
        def _():
            bucket_copy(at).wait_recv()


def join_kernel(plan, share, arrived, matched, out, total, out_sem):
    side = out.shape[1]
    per_row = side // LANES

    def row_lines(block_row):
        return pl.ds(pl.multiple_of(block_row * LANES, LANES), LANES)

    def out_copy(block_row):
        lines = row_lines(block_row)
        return pltpu.make_async_copy(total.at[lines], out.at[lines], out_sem.at[block_row])

    def join_row(block_row, start):
        end = plan[2, block_row]
        lines = row_lines(block_row)

        def add(at, carry):
            slot = plan[0, at]
            column = pl.multiple_of((plan[1, at] - block_row * per_row) * LANES, LANES)
            columns = pl.ds(column, LANES)
            piece = arrived[lax.div(slot, CAP), slot & (CAP - 1)].astype(jnp.float32)
            total[lines, columns] = total[lines, columns] + share[2, at] * piece
            return carry

        lax.fori_loop(start, end, add, 0)
        out_copy(block_row).start()
        return end

    lax.fori_loop(0, per_row, join_row, 0)
    for block_row in range(per_row):
        out_copy(block_row).wait()


def on_device(pieces, owner_map, offsets, template, coefficients):
    own, block_side = pieces.shape[0], pieces.shape[1]
    side = template.shape[0]
    smem = pl.BlockSpec(memory_space=pltpu.SMEM)
    vmem = pl.BlockSpec(memory_space=pltpu.VMEM)
    hbm = pl.BlockSpec(memory_space=pltpu.HBM)
    count = len(DIRS)

    band_across, band_down = band_tables()
    tall = side + 2 * HALO
    dma = pltpu.SemaphoreType.DMA
    arrived, plan, share, matched = pl.pallas_call(
        send_kernel,
        out_shape=[
            jax.ShapeDtypeStruct((count + 1, CAP, block_side, block_side), jnp.bfloat16),
            jax.ShapeDtypeStruct((8, 2 * LANES), jnp.int32),
            jax.ShapeDtypeStruct((8, 2 * LANES), jnp.float32),
            jax.ShapeDtypeStruct((side, side), jnp.float32),
        ],
        in_specs=[hbm, hbm, smem, hbm, hbm, hbm, hbm],
        out_specs=[vmem, vmem, vmem, vmem],
        scratch_shapes=[
            pltpu.VMEM((own, block_side, block_side), jnp.bfloat16),
            pltpu.VMEM((1, own), jnp.int32),
            pltpu.VMEM((1, own), jnp.int32),
            pltpu.VMEM((16, LANES), jnp.int32),
            pltpu.SMEM((16, LANES), jnp.int32),
            pltpu.VMEM((count, 16, LANES), jnp.int32),
            pltpu.VMEM((16, LANES), jnp.int32),
            pltpu.VMEM((count, CAP, block_side, block_side), jnp.bfloat16),
            pltpu.VMEM((tall, side + 2 * LANES), jnp.bfloat16),
            pltpu.VMEM((2, LANES, LANES), jnp.bfloat16),
            pltpu.VMEM((2, LANES, LANES), jnp.bfloat16),
            pltpu.VMEM((BASES, side + LANES, side), jnp.bfloat16),
            pltpu.VMEM((BASES, DEGREE + 1, 8, side), jnp.float32),
            pltpu.VMEM(band_across.shape, jnp.bfloat16),
            pltpu.VMEM(band_down.shape, jnp.bfloat16),
            dma((8,)), dma, dma((count,)), dma((count,)), dma((count,)), dma((count,)),
            dma((count,)), dma((count,)),
        ],
        compiler_params=pltpu.CompilerParams(
            collective_id=0, has_side_effects=True, vmem_limit_bytes=40 << 20
        ),
        name="send",
    )(
        *(
            pltpu.with_memory_space_constraint(array, pltpu.HBM)
            for array in (
                owner_map.reshape(1, own), offsets.reshape(1, own), coefficients, pieces,
                template, jnp.asarray(band_across), jnp.asarray(band_down),
            )
        )
    )
    joined, _ = pl.pallas_call(
        join_kernel,
        out_shape=[jax.ShapeDtypeStruct((side, side), jnp.float32)] * 2,
        in_specs=[smem, smem, vmem, vmem],
        out_specs=[hbm, vmem],
        input_output_aliases={3: 1},
        scratch_shapes=[dma((side // block_side,))],
        compiler_params=pltpu.CompilerParams(vmem_limit_bytes=32 << 20),
        name="join",
    )(plan, share, arrived, matched)
    return joined


def solution(mesh):
    in_specs = (P(("py", "px"), None, None), P(("py", "px")), P(("py", "px")), P("py", "px"), P())
    out_specs = P("py", "px")
    return jax.shard_map(
        on_device, mesh=mesh, in_specs=in_specs, out_specs=out_specs, check_vma=False
    )
```

```python
import functools

import jax
import jax.numpy as jnp
import numpy as np
from jax import lax
from jax.experimental import pallas as pl
from jax.experimental.pallas import tpu as pltpu
from jax.sharding import PartitionSpec as P

HALO = 16
CAP = 16
LANES = 128
BASES = 3
DEGREE = 4

sigma_fractions = (0.09375, 0.1875, 0.375)
term_powers = [(degree - power_v, power_v) for degree in range(5) for power_v in range(degree + 1)]

DIRS = ((1, 1), (-1, -1), (1, -1), (-1, 1), (0, 1), (0, -1), (1, 0), (-1, 0))
OWN = 4
MESH = pl.DeviceIdType.MESH


def bucket_of(step):
    return 3 * (step[0] + 1) + step[1] + 1


def gauss_taps():
    positions = np.arange(-HALO, HALO + 1).astype(np.float32)
    stacked = []
    for fraction in sigma_fractions:
        sigma = fraction * HALO
        values = np.exp(-positions * positions / np.float32(2.0 * sigma * sigma))
        stacked.append(values / np.sum(values))
    return np.stack(stacked).astype(jnp.bfloat16)


def band_tables():
    taps = gauss_taps()
    across = np.zeros((3 * LANES, BASES * LANES), taps.dtype)
    down = np.zeros((BASES, LANES, 2 * LANES), taps.dtype)
    for basis in range(BASES):
        for out in range(LANES):
            for tap in range(2 * HALO + 1):
                across[LANES - HALO + out + tap, basis * LANES + out] = taps[basis, tap]
                down[basis, out, out + tap] = taps[basis, tap]
    return across, down


def sort_plan(own, per_row, tags, plan):
    count = len(DIRS)
    blocks = per_row * per_row
    shape = (blocks, LANES)
    code = tags[...]
    block_tag = lax.shift_right_logical(code, own.bit_length() - 1).astype(jnp.float32)
    spread = jnp.zeros((8, LANES), jnp.float32)
    for at in range(count):
        one = jnp.broadcast_to(block_tag[at : at + 1], (8, LANES))
        spread = spread + pltpu.roll(one, at * CAP, 1)
    groups = (spread[0:1], block_tag[count : count + 1])

    block_id = lax.broadcasted_iota(jnp.int32, shape, 0).astype(jnp.float32)
    before = jnp.where(
        lax.broadcasted_iota(jnp.int32, (LANES, LANES), 0)
        < lax.broadcasted_iota(jnp.int32, (LANES, LANES), 1), 1.0, 0.0,
    )
    lower = jnp.where(
        lax.broadcasted_iota(jnp.int32, (blocks, blocks), 1)
        < lax.broadcasted_iota(jnp.int32, (blocks, blocks), 0), 1.0, 0.0,
    )
    hits = [jnp.where(jnp.broadcast_to(tag, shape) == block_id + 1, 1.0, 0.0) for tag in groups]
    sums = [jnp.broadcast_to(jnp.sum(hit, axis=1, keepdims=True), shape) for hit in hits]
    covered = sums[0] + sums[1]
    first = jnp.dot(lower, covered, preferred_element_type=jnp.float32)
    ahead = (first, first + sums[0])

    line = lax.broadcasted_iota(jnp.int32, (8, LANES), 0)
    lane = lax.broadcasted_iota(jnp.int32, (8, LANES), 1).astype(jnp.float32)
    target = lax.broadcasted_iota(jnp.int32, (2 * LANES, LANES), 0).astype(jnp.float32)
    over_lanes = (((1,), (1,)), ((), ()))
    listed = jnp.zeros((8, 2 * LANES), jnp.float32)
    ends = jnp.zeros((8, 2 * LANES), jnp.float32)
    for group in range(2):
        hit, tag = hits[group], groups[group]
        rank = ahead[group] + jnp.dot(hit, before, preferred_element_type=jnp.float32)
        place = jnp.sum(hit * rank, axis=0, keepdims=True)
        shares = jnp.sum(hit * covered, axis=0, keepdims=True)
        place = jnp.where(tag > 0, place, -1.0)
        chosen = jnp.where(jnp.broadcast_to(place, target.shape) == target, 1.0, 0.0)
        values = jnp.where(line == 0, lane + group * LANES, 0.0)
        values = jnp.where(line == 1, jnp.broadcast_to(tag - 1, values.shape), values)
        values = jnp.where(line == 2, jnp.broadcast_to(shares, values.shape), values)
        listed = listed + lax.dot_general(
            values, chosen, over_lanes, preferred_element_type=jnp.float32
        )
        wide_tag = jnp.broadcast_to(tag, target.shape)
        inside = jnp.where((wide_tag > 0) & (wide_tag <= (target + 1) * per_row), 1.0, 0.0)
        ends = ends + lax.dot_general(
            jnp.ones((8, LANES), jnp.float32), inside, over_lanes,
            preferred_element_type=jnp.float32,
        )
    wide_line = lax.broadcasted_iota(jnp.int32, listed.shape, 0)
    plan[...] = jnp.where(wide_line == 3, ends, listed).astype(jnp.int32)


def send_kernel(
    owner, offset, coef_hbm, pieces, template, band_across, band_down,
    arrived, plan, matched,
    held, coef, owner_row, offset_row, table, rows_out, table_scalar, arrived_table,
    tags, outgoing, padded, strip_out, strip_in, across, inner, row_band, down_band,
    load_sem, table_sem, send_sem, recv_sem, label_send, label_recv, rim_send, rim_recv,
):
    rows, cols = lax.axis_size("py"), lax.axis_size("px")
    row, col = lax.axis_index("py"), lax.axis_index("px")
    side = template.shape[0]
    last = side - LANES
    own = held.shape[0]

    def exists(step):
        r, c = row + step[0], col + step[1]
        return (r >= 0) & (r < rows) & (c >= 0) & (c < cols)

    def neighbour(step):
        return (row + step[0], col + step[1])

    barrier = pltpu.get_barrier_semaphore()
    for step in DIRS:
        @pl.when(exists(step))
        def _():
            pl.semaphore_signal(barrier, inc=1, device_id=neighbour(step), device_id_type=MESH)

    body = padded.at[pl.ds(HALO, side)]
    loads = [
        pltpu.make_async_copy(
            template.at[:, pl.ds(0, LANES)], body.at[:, pl.ds(LANES, LANES)], load_sem.at[0]
        ),
        pltpu.make_async_copy(
            template.at[:, pl.ds(last, LANES)], body.at[:, pl.ds(side, LANES)], load_sem.at[1]
        ),
        pltpu.make_async_copy(owner, owner_row, load_sem.at[2]),
        pltpu.make_async_copy(offset, offset_row, load_sem.at[3]),
        pltpu.make_async_copy(pieces, held, load_sem.at[4]),
        pltpu.make_async_copy(
            template.at[:, pl.ds(LANES, side - 2 * LANES)],
            body.at[:, pl.ds(2 * LANES, side - 2 * LANES)],
            load_sem.at[5],
        ),
        pltpu.make_async_copy(band_across, row_band, load_sem.at[6]),
        pltpu.make_async_copy(band_down, down_band, load_sem.at[7]),
        pltpu.make_async_copy(coef_hbm, coef, load_sem.at[8]),
    ]
    for load in (loads[2], loads[4], loads[3], loads[0], loads[1]):
        load.start()

    def opposite(step):
        return (-step[0], -step[1])

    def rim_copy(at):
        step = DIRS[at]
        if step[0] == 0:
            source = strip_out.at[0 if step[1] > 0 else 1]
            target = strip_in.at[0 if step[1] > 0 else 1]
        else:
            source_rows = pl.ds(side - HALO if step[0] > 0 else 0, HALO)
            target_rows = pl.ds(0 if step[0] > 0 else side + HALO, HALO)
            if step[1] == 0:
                source = template.at[source_rows]
                target = padded.at[target_rows, pl.ds(LANES, side)]
            else:
                source = template.at[source_rows, pl.ds(last if step[1] > 0 else 0, LANES)]
                target = padded.at[target_rows, pl.ds(0 if step[1] > 0 else side + LANES, LANES)]
        return pltpu.make_async_remote_copy(
            src_ref=source, dst_ref=target, send_sem=rim_send.at[at], recv_sem=rim_recv.at[at],
            device_id=neighbour(step), device_id_type=MESH,
        )

    def label_copy(at):
        return pltpu.make_async_remote_copy(
            src_ref=rows_out.at[bucket_of(DIRS[at])], dst_ref=arrived_table.at[at], send_sem=label_send.at[at],
            recv_sem=label_recv.at[at], device_id=neighbour(DIRS[at]), device_id_type=MESH,
        )

    def bucket_copy(at, slots=pl.ds(0, CAP)):
        return pltpu.make_async_remote_copy(
            src_ref=outgoing.at[at, slots], dst_ref=arrived.at[at, slots], send_sem=send_sem.at[at],
            recv_sem=recv_sem.at[at], device_id=neighbour(DIRS[at]), device_id_type=MESH,
        )

    def pack_strip(strip, first_col, first_lane):
        lane_group = lax.broadcasted_iota(jnp.int32, (LANES, LANES), 1) // HALO
        packed = jnp.zeros((LANES, LANES), jnp.float32)
        for group in range(side // LANES):
            block = padded[pl.ds(HALO + group * LANES, LANES), pl.ds(first_col, LANES)]
            moved = pltpu.roll(
                block.astype(jnp.float32), (group * HALO - first_lane) % LANES, 1
            )
            packed = jnp.where(lane_group == group, moved, packed)
        strip_out[strip] = packed.astype(jnp.bfloat16)

    def send_pieces(slot, piece_of):
        for at, step in enumerate(DIRS):
            outgoing[at, slot] = held[piece_of(bucket_of(step))]

            @pl.when(exists(step))
            def _():
                bucket_copy(at, pl.ds(slot, 1)).start()
        arrived[len(DIRS), slot] = held[piece_of(OWN)]

    def send_slot(slot, carry):
        send_pieces(slot, lambda bucket: table_scalar[bucket, slot] & (own - 1))
        return carry

    loads[2].wait()
    bucket_id = lax.broadcasted_iota(jnp.int32, (16, own), 0)
    target = jnp.full((16, own), -1, jnp.int32)
    for bucket in range(9):
        tile = (row + bucket // 3 - 1) * cols + col + bucket % 3 - 1
        target = jnp.where(bucket_id == bucket, tile, target)
    belongs = target == jnp.broadcast_to(owner_row[...], (16, own))
    number = lax.broadcasted_iota(jnp.int32, (16, own), 1).astype(jnp.float32)
    leader = [
        jnp.min(jnp.where(belongs & (bucket_id == bucket), number, own - 1.0)).astype(jnp.int32)
        & (own - 1)
        for bucket in range(9)
    ]
    tall_group = 3 - jnp.where(row == 0, 1, 0) - jnp.where(row == rows - 1, 1, 0)
    wide_group = 3 - jnp.where(col == 0, 1, 0) - jnp.where(col == cols - 1, 1, 0)
    pl.semaphore_wait(barrier, tall_group * wide_group - 1)
    loads[4].wait()
    send_pieces(0, lambda bucket: leader[bucket])

    loads[3].wait()
    earlier = (
        lax.broadcasted_iota(jnp.int32, (own, own), 0)
        < lax.broadcasted_iota(jnp.int32, (own, own), 1)
    )
    place = jnp.dot(
        jnp.where(belongs, 1.0, 0.0), jnp.where(earlier, 1.0, 0.0),
        preferred_element_type=jnp.float32,
    )
    code = lax.broadcasted_iota(jnp.int32, (16, own), 1) + own * (
        jnp.broadcast_to(offset_row[...], (16, own)) + 1
    )
    code = jnp.where(belongs, code.astype(jnp.float32), 0.0)
    slot_lane = lax.broadcasted_iota(jnp.int32, (16, LANES), 1)
    filled = jnp.zeros((16, LANES), jnp.float32)
    for slot in range(CAP):
        picked = jnp.sum(jnp.where(place == slot, code, 0.0), axis=1, keepdims=True)
        filled = jnp.where(slot_lane == slot, picked, filled)
    filled = filled.astype(jnp.int32)
    table[...] = filled
    for bucket in range(9):
        rows_out[bucket] = filled[bucket : bucket + 1]
    to_scalar = pltpu.make_async_copy(table, table_scalar, table_sem)
    to_scalar.start()

    loads[0].wait()
    loads[1].wait()
    pack_strip(0, side, LANES - HALO)
    pack_strip(1, LANES, 0)
    for at, step in enumerate(DIRS):
        @pl.when(exists(step))
        def _():
            rim_copy(at).start()
            label_copy(at).start()
    to_scalar.wait()
    lax.fori_loop(1, 4, send_slot, 0)
    for load in loads[5:]:
        load.start()
    lax.fori_loop(4, CAP, send_slot, 0)

    loads[8].wait()
    lane = lax.broadcasted_iota(jnp.int32, (8, side), 1)
    u = ((col * side + lane).astype(jnp.float32) + 0.5) * (2.0 / (side * cols)) - 1.0
    for basis in range(BASES):
        for power_v in range(DEGREE + 1):
            total = jnp.zeros_like(u)
            for power_u in reversed(range(DEGREE + 1 - power_v)):
                total = total * u + coef[basis, term_powers.index((power_u, power_v))]
            inner[basis, power_v] = total

    for load in loads[5:8]:
        load.wait()
    wide = padded.shape[1]

    @pl.when(row == 0)
    def _():
        padded[pl.ds(0, HALO)] = jnp.zeros((HALO, wide), jnp.bfloat16)

    @pl.when(row == rows - 1)
    def _():
        padded[pl.ds(side + HALO, HALO)] = jnp.zeros((HALO, wide), jnp.bfloat16)

    @pl.when(col == 0)
    def _():
        padded[:, pl.ds(0, LANES)] = jnp.zeros((padded.shape[0], LANES), jnp.bfloat16)

    @pl.when(col == cols - 1)
    def _():
        padded[:, pl.ds(side + LANES, LANES)] = jnp.zeros((padded.shape[0], LANES), jnp.bfloat16)

    for at, step in enumerate(DIRS):
        @pl.when(exists(opposite(step)))
        def _():
            rim_copy(at).wait_recv()

    def unpack_strip(strip, first_col, first_lane):
        packed = strip_in[strip].astype(jnp.float32)
        for group in range(side // LANES):
            moved = pltpu.roll(packed, (first_lane - group * HALO) % LANES, 1)
            padded[pl.ds(HALO + group * LANES, LANES), pl.ds(first_col, LANES)] = moved.astype(jnp.bfloat16)

    @pl.when(col > 0)
    def _():
        unpack_strip(0, 0, LANES - HALO)

    @pl.when(col < cols - 1)
    def _():
        unpack_strip(1, side + LANES, 0)

    tall = padded.shape[0]
    chunk = tall // 3
    blocks = side // LANES
    for basis in range(BASES):
        across[basis, pl.ds(tall, across.shape[1] - tall)] = jnp.zeros(
            (across.shape[1] - tall, side), jnp.bfloat16
        )

    def row_pass(block, carry):
        first = pl.multiple_of(block * LANES, LANES)
        for part in range(3):
            got = jnp.dot(
                padded[pl.ds(part * chunk, chunk), pl.ds(first, 3 * LANES)],
                row_band[...],
                preferred_element_type=jnp.float32,
            )
            for basis in range(BASES):
                across[basis, pl.ds(part * chunk, chunk), pl.ds(first, LANES)] = got[
                    :, basis * LANES : (basis + 1) * LANES
                ].astype(jnp.bfloat16)
        return carry

    lax.fori_loop(0, blocks, row_pass, 0)

    part_cols = 2 * LANES

    def column_pass(block, carry):
        first = pl.multiple_of(block * LANES, LANES)
        line = lax.broadcasted_iota(jnp.int32, (LANES, part_cols), 0)
        v = ((row * side + first + line).astype(jnp.float32) + 0.5) * (2.0 / (side * rows)) - 1.0
        for part in range(side // part_cols):
            columns = pl.ds(part * part_cols, part_cols)
            total = jnp.zeros((LANES, part_cols), jnp.float32)
            for basis in range(BASES):
                smoothed = jnp.dot(
                    down_band[basis],
                    across[basis, pl.ds(first, 2 * LANES), columns],
                    preferred_element_type=jnp.float32,
                )
                weight = jnp.broadcast_to(inner[basis, DEGREE, 0:1, columns], total.shape)
                for power_v in reversed(range(DEGREE)):
                    weight = weight * v + inner[basis, power_v, 0:1, columns]
                total = total - weight * smoothed
            matched[pl.ds(first, LANES), columns] = total
        return carry

    lax.fori_loop(0, blocks, column_pass, 0)

    for at, step in enumerate(DIRS):
        tags[pl.ds(at, 1)] = jnp.zeros((1, LANES), jnp.int32)

        @pl.when(exists(opposite(step)))
        def _():
            label_copy(at).wait_recv()
            tags[pl.ds(at, 1)] = arrived_table[at]
    tags[pl.ds(len(DIRS), 1)] = table[pl.ds(OWN, 1)]
    sort_plan(own, side // LANES, tags, plan)

    for at, step in enumerate(DIRS):
        @pl.when(exists(step))
        def _():
            rim_copy(at).wait_send()
            label_copy(at).wait_send()
            bucket_copy(at).wait_send()

        @pl.when(exists(opposite(step)))
        def _():
            bucket_copy(at).wait_recv()


def join_kernel(plan, arrived, matched, out, total, out_sem):
    side = out.shape[1]
    per_row = side // LANES

    def row_lines(block_row):
        return pl.ds(pl.multiple_of(block_row * LANES, LANES), LANES)

    def out_copy(block_row):
        lines = row_lines(block_row)
        return pltpu.make_async_copy(total.at[lines], out.at[lines], out_sem.at[block_row])

    def join_row(block_row, start):
        end = plan[3, block_row]
        lines = row_lines(block_row)

        def add(at, carry):
            slot = plan[0, at]
            column = pl.multiple_of((plan[1, at] - block_row * per_row) * LANES, LANES)
            columns = pl.ds(column, LANES)
            piece = arrived[lax.div(slot, CAP), slot & (CAP - 1)].astype(jnp.float32)
            share = 1.0 / jnp.full((8, LANES), jnp.maximum(plan[2, at], 1).astype(jnp.float32))
            share = jnp.tile(share, (LANES // 8, 1))
            total[lines, columns] = total[lines, columns] + share * piece
            return carry

        lax.fori_loop(start, end, add, 0)
        out_copy(block_row).start()
        return end

    lax.fori_loop(0, per_row, join_row, 0)
    for block_row in range(per_row):
        out_copy(block_row).wait()


def on_device(pieces, owner_map, offsets, template, coefficients):
    own, block_side = pieces.shape[0], pieces.shape[1]
    side = template.shape[0]
    smem = pl.BlockSpec(memory_space=pltpu.SMEM)
    vmem = pl.BlockSpec(memory_space=pltpu.VMEM)
    hbm = pl.BlockSpec(memory_space=pltpu.HBM)
    count = len(DIRS)

    band_across, band_down = band_tables()
    tall = side + 2 * HALO
    dma = pltpu.SemaphoreType.DMA
    arrived, plan, matched = pl.pallas_call(
        send_kernel,
        out_shape=[
            jax.ShapeDtypeStruct((count + 1, CAP, block_side, block_side), jnp.bfloat16),
            jax.ShapeDtypeStruct((8, 2 * LANES), jnp.int32),
            jax.ShapeDtypeStruct((side, side), jnp.float32),
        ],
        in_specs=[hbm] * 7,
        out_specs=[vmem, vmem, vmem],
        scratch_shapes=[
            pltpu.VMEM((own, block_side, block_side), jnp.bfloat16),
            pltpu.SMEM(coefficients.shape, jnp.float32),
            pltpu.VMEM((1, own), jnp.int32),
            pltpu.VMEM((1, own), jnp.int32),
            pltpu.VMEM((16, LANES), jnp.int32),
            pltpu.VMEM((9, 1, LANES), jnp.int32),
            pltpu.SMEM((16, LANES), jnp.int32),
            pltpu.VMEM((count, 1, LANES), jnp.int32),
            pltpu.VMEM((16, LANES), jnp.int32),
            pltpu.VMEM((count, CAP, block_side, block_side), jnp.bfloat16),
            pltpu.VMEM((tall, side + 2 * LANES), jnp.bfloat16),
            pltpu.VMEM((2, LANES, LANES), jnp.bfloat16),
            pltpu.VMEM((2, LANES, LANES), jnp.bfloat16),
            pltpu.VMEM((BASES, side + LANES, side), jnp.bfloat16),
            pltpu.VMEM((BASES, DEGREE + 1, 8, side), jnp.float32),
            pltpu.VMEM(band_across.shape, jnp.bfloat16),
            pltpu.VMEM(band_down.shape, jnp.bfloat16),
            dma((9,)), dma, dma((count,)), dma((count,)), dma((count,)), dma((count,)),
            dma((count,)), dma((count,)),
        ],
        compiler_params=pltpu.CompilerParams(
            collective_id=0, has_side_effects=True, vmem_limit_bytes=40 << 20
        ),
        name="send",
    )(
        *(
            pltpu.with_memory_space_constraint(array, pltpu.HBM)
            for array in (
                owner_map.reshape(1, own), offsets.reshape(1, own), coefficients, pieces,
                template, jnp.asarray(band_across), jnp.asarray(band_down),
            )
        )
    )
    joined, _ = pl.pallas_call(
        join_kernel,
        out_shape=[jax.ShapeDtypeStruct((side, side), jnp.float32)] * 2,
        in_specs=[smem, vmem, vmem],
        out_specs=[hbm, vmem],
        input_output_aliases={2: 1},
        scratch_shapes=[dma((side // block_side,))],
        compiler_params=pltpu.CompilerParams(vmem_limit_bytes=32 << 20),
        name="join",
    )(plan, arrived, matched)
    return joined


def solution(mesh):
    in_specs = (P(("py", "px"), None, None), P(("py", "px")), P(("py", "px")), P("py", "px"), P())
    out_specs = P("py", "px")
    return jax.shard_map(
        on_device, mesh=mesh, in_specs=in_specs, out_specs=out_specs, check_vma=False
    )
```

```python
import functools

import jax
import jax.numpy as jnp
import numpy as np
from jax import lax
from jax.experimental import pallas as pl
from jax.experimental.pallas import tpu as pltpu
from jax.sharding import PartitionSpec as P

HALO = 16
CAP = 16
LANES = 128
BASES = 3
DEGREE = 4

sigma_fractions = (0.09375, 0.1875, 0.375)
term_powers = [(degree - power_v, power_v) for degree in range(5) for power_v in range(degree + 1)]

DIRS = ((1, 1), (-1, -1), (1, -1), (-1, 1), (0, 1), (0, -1), (1, 0), (-1, 0))
DIAGONALS = 4
RELAYED = 8
EARLY = 12
OWN = 4
MESH = pl.DeviceIdType.MESH


def bucket_of(step):
    return 3 * (step[0] + 1) + step[1] + 1


def gauss_taps():
    positions = np.arange(-HALO, HALO + 1).astype(np.float32)
    stacked = []
    for fraction in sigma_fractions:
        sigma = fraction * HALO
        values = np.exp(-positions * positions / np.float32(2.0 * sigma * sigma))
        stacked.append(values / np.sum(values))
    return np.stack(stacked).astype(jnp.bfloat16)


def band_tables():
    taps = gauss_taps()
    across = np.zeros((3 * LANES, BASES * LANES), taps.dtype)
    down = np.zeros((BASES, LANES, 2 * LANES), taps.dtype)
    for basis in range(BASES):
        for out in range(LANES):
            for tap in range(2 * HALO + 1):
                across[LANES - HALO + out + tap, basis * LANES + out] = taps[basis, tap]
                down[basis, out, out + tap] = taps[basis, tap]
    return across, down


def sort_plan(own, per_row, tags, plan):
    count = len(DIRS)
    blocks = per_row * per_row
    shape = (blocks, LANES)
    code = tags[...]
    block_tag = lax.shift_right_logical(code, own.bit_length() - 1).astype(jnp.float32)
    spread = jnp.zeros((8, LANES), jnp.float32)
    for at in range(count):
        one = jnp.broadcast_to(block_tag[at : at + 1], (8, LANES))
        spread = spread + pltpu.roll(one, at * CAP, 1)
    groups = (spread[0:1], block_tag[count : count + 1])

    block_id = lax.broadcasted_iota(jnp.int32, shape, 0).astype(jnp.float32)
    before = jnp.where(
        lax.broadcasted_iota(jnp.int32, (LANES, LANES), 0)
        < lax.broadcasted_iota(jnp.int32, (LANES, LANES), 1), 1.0, 0.0,
    )
    lower = jnp.where(
        lax.broadcasted_iota(jnp.int32, (blocks, blocks), 1)
        < lax.broadcasted_iota(jnp.int32, (blocks, blocks), 0), 1.0, 0.0,
    )
    hits = [jnp.where(jnp.broadcast_to(tag, shape) == block_id + 1, 1.0, 0.0) for tag in groups]
    sums = [jnp.broadcast_to(jnp.sum(hit, axis=1, keepdims=True), shape) for hit in hits]
    covered = sums[0] + sums[1]
    first = jnp.dot(lower, covered, preferred_element_type=jnp.float32)
    ahead = (first, first + sums[0])

    line = lax.broadcasted_iota(jnp.int32, (8, LANES), 0)
    lane = lax.broadcasted_iota(jnp.int32, (8, LANES), 1).astype(jnp.float32)
    target = lax.broadcasted_iota(jnp.int32, (2 * LANES, LANES), 0).astype(jnp.float32)
    over_lanes = (((1,), (1,)), ((), ()))
    listed = jnp.zeros((8, 2 * LANES), jnp.float32)
    ends = jnp.zeros((8, 2 * LANES), jnp.float32)
    for group in range(2):
        hit, tag = hits[group], groups[group]
        rank = ahead[group] + jnp.dot(hit, before, preferred_element_type=jnp.float32)
        place = jnp.sum(hit * rank, axis=0, keepdims=True)
        shares = jnp.sum(hit * covered, axis=0, keepdims=True)
        place = jnp.where(tag > 0, place, -1.0)
        chosen = jnp.where(jnp.broadcast_to(place, target.shape) == target, 1.0, 0.0)
        values = jnp.where(line == 0, lane + group * LANES, 0.0)
        values = jnp.where(line == 1, jnp.broadcast_to(tag - 1, values.shape), values)
        values = jnp.where(line == 2, jnp.broadcast_to(shares, values.shape), values)
        listed = listed + lax.dot_general(
            values, chosen, over_lanes, preferred_element_type=jnp.float32
        )
        wide_tag = jnp.broadcast_to(tag, target.shape)
        inside = jnp.where((wide_tag > 0) & (wide_tag <= (target + 1) * per_row), 1.0, 0.0)
        ends = ends + lax.dot_general(
            jnp.ones((8, LANES), jnp.float32), inside, over_lanes,
            preferred_element_type=jnp.float32,
        )
    wide_line = lax.broadcasted_iota(jnp.int32, listed.shape, 0)
    plan[...] = jnp.where(wide_line == 3, ends, listed).astype(jnp.int32)


def send_kernel(
    owner, offset, coef_hbm, pieces, template, band_across, band_down,
    arrived, plan, matched,
    held, coef, owner_row, offset_row, table, rows_out, table_scalar, arrived_table,
    tags, outgoing, padded, strip_out, strip_in, across, inner, row_band, down_band,
    relay, load_sem, table_sem, send_sem, recv_sem, label_send, label_recv, rim_send, rim_recv,
    relay_recv, onward_send,
):
    rows, cols = lax.axis_size("py"), lax.axis_size("px")
    row, col = lax.axis_index("py"), lax.axis_index("px")
    side = template.shape[0]
    last = side - LANES
    own = held.shape[0]

    def exists(step):
        r, c = row + step[0], col + step[1]
        return (r >= 0) & (r < rows) & (c >= 0) & (c < cols)

    def neighbour(step):
        return (row + step[0], col + step[1])

    barrier = pltpu.get_barrier_semaphore()
    for step in DIRS:
        @pl.when(exists(step))
        def _():
            pl.semaphore_signal(barrier, inc=1, device_id=neighbour(step), device_id_type=MESH)

    body = padded.at[pl.ds(HALO, side)]
    loads = [
        pltpu.make_async_copy(
            template.at[:, pl.ds(0, LANES)], body.at[:, pl.ds(LANES, LANES)], load_sem.at[0]
        ),
        pltpu.make_async_copy(
            template.at[:, pl.ds(last, LANES)], body.at[:, pl.ds(side, LANES)], load_sem.at[1]
        ),
        pltpu.make_async_copy(owner, owner_row, load_sem.at[2]),
        pltpu.make_async_copy(offset, offset_row, load_sem.at[3]),
        pltpu.make_async_copy(pieces, held, load_sem.at[4]),
        pltpu.make_async_copy(
            template.at[:, pl.ds(LANES, side - 2 * LANES)],
            body.at[:, pl.ds(2 * LANES, side - 2 * LANES)],
            load_sem.at[5],
        ),
        pltpu.make_async_copy(band_across, row_band, load_sem.at[6]),
        pltpu.make_async_copy(band_down, down_band, load_sem.at[7]),
        pltpu.make_async_copy(coef_hbm, coef, load_sem.at[8]),
    ]
    for load in (loads[2], loads[4], loads[3], loads[0], loads[1]):
        load.start()

    def opposite(step):
        return (-step[0], -step[1])

    def rim_copy(at):
        step = DIRS[at]
        if step[0] == 0:
            source = strip_out.at[0 if step[1] > 0 else 1]
            target = strip_in.at[0 if step[1] > 0 else 1]
        else:
            source_rows = pl.ds(side - HALO if step[0] > 0 else 0, HALO)
            target_rows = pl.ds(0 if step[0] > 0 else side + HALO, HALO)
            if step[1] == 0:
                source = template.at[source_rows]
                target = padded.at[target_rows, pl.ds(LANES, side)]
            else:
                source = template.at[source_rows, pl.ds(last if step[1] > 0 else 0, LANES)]
                target = padded.at[target_rows, pl.ds(0 if step[1] > 0 else side + LANES, LANES)]
        return pltpu.make_async_remote_copy(
            src_ref=source, dst_ref=target, send_sem=rim_send.at[at], recv_sem=rim_recv.at[at],
            device_id=neighbour(step), device_id_type=MESH,
        )

    def label_copy(at):
        return pltpu.make_async_remote_copy(
            src_ref=rows_out.at[bucket_of(DIRS[at])], dst_ref=arrived_table.at[at], send_sem=label_send.at[at],
            recv_sem=label_recv.at[at], device_id=neighbour(DIRS[at]), device_id_type=MESH,
        )

    def bucket_copy(at, slots=pl.ds(0, CAP)):
        return pltpu.make_async_remote_copy(
            src_ref=outgoing.at[at, slots], dst_ref=arrived.at[at, slots], send_sem=send_sem.at[at],
            recv_sem=recv_sem.at[at], device_id=neighbour(DIRS[at]), device_id_type=MESH,
        )

    def pack_strip(strip, first_col, first_lane):
        lane_group = lax.broadcasted_iota(jnp.int32, (LANES, LANES), 1) // HALO
        packed = jnp.zeros((LANES, LANES), jnp.float32)
        for group in range(side // LANES):
            block = padded[pl.ds(HALO + group * LANES, LANES), pl.ds(first_col, LANES)]
            moved = pltpu.roll(
                block.astype(jnp.float32), (group * HALO - first_lane) % LANES, 1
            )
            packed = jnp.where(lane_group == group, moved, packed)
        strip_out[strip] = packed.astype(jnp.bfloat16)

    def column_first(step):
        return row == (2 if step[0] < 0 else rows - 3)

    def row_first(step):
        return row == (1 if step[0] > 0 else rows - 2)

    def relay_copy(at, slots):
        step = DIRS[at]
        return pltpu.make_async_remote_copy(
            src_ref=outgoing.at[at, slots], dst_ref=relay.at[at, slots],
            send_sem=send_sem.at[at], recv_sem=relay_recv.at[at],
            device_id=(
                row + jnp.where(row_first(step), 0, step[0]),
                col + jnp.where(column_first(step), 0, step[1]),
            ),
            device_id_type=MESH,
        )

    def turns_column(step):
        return row == (1 if step[0] < 0 else rows - 2)

    def turns_row(step):
        return row == (1 if step[0] > 0 else rows - 2)

    def turns(step):
        ahead, behind = col + step[1], col - step[1]
        return (turns_column(step) & (ahead >= 0) & (ahead < cols)) | (
            turns_row(step) & (behind >= 0) & (behind < cols)
        )

    def onward_copy(at, slots):
        step = DIRS[at]
        return pltpu.make_async_remote_copy(
            src_ref=relay.at[at, slots], dst_ref=arrived.at[at, slots],
            send_sem=onward_send.at[at], recv_sem=recv_sem.at[at],
            device_id=(
                row + jnp.where(turns_row(step), step[0], 0),
                col + jnp.where(turns_column(step), step[1], 0),
            ),
            device_id_type=MESH,
        )

    def send_pieces(slot, piece_of, relayed):
        for at, step in enumerate(DIRS):
            outgoing[at, slot] = held[piece_of(bucket_of(step))]
            direct = exists(step)
            if relayed and at < DIAGONALS:
                turned = column_first(step) | row_first(step)

                @pl.when(direct & turned)
                def _():
                    relay_copy(at, pl.ds(slot, 1)).start()
                direct = direct & jnp.logical_not(turned)

            @pl.when(direct)
            def _():
                bucket_copy(at, pl.ds(slot, 1)).start()
        arrived[len(DIRS), slot] = held[piece_of(OWN)]

    def send_slot(relayed, slot, carry):
        send_pieces(slot, lambda bucket: table_scalar[bucket, slot] & (own - 1), relayed)
        return carry

    loads[2].wait()
    bucket_id = lax.broadcasted_iota(jnp.int32, (16, own), 0)
    target = jnp.full((16, own), -1, jnp.int32)
    for bucket in range(9):
        tile = (row + bucket // 3 - 1) * cols + col + bucket % 3 - 1
        target = jnp.where(bucket_id == bucket, tile, target)
    belongs = target == jnp.broadcast_to(owner_row[...], (16, own))
    number = lax.broadcasted_iota(jnp.int32, (16, own), 1).astype(jnp.float32)
    leader = [
        jnp.min(jnp.where(belongs & (bucket_id == bucket), number, own - 1.0)).astype(jnp.int32)
        & (own - 1)
        for bucket in range(9)
    ]
    tall_group = 3 - jnp.where(row == 0, 1, 0) - jnp.where(row == rows - 1, 1, 0)
    wide_group = 3 - jnp.where(col == 0, 1, 0) - jnp.where(col == cols - 1, 1, 0)
    pl.semaphore_wait(barrier, tall_group * wide_group - 1)
    loads[4].wait()
    send_pieces(0, lambda bucket: leader[bucket], True)

    loads[3].wait()
    earlier = (
        lax.broadcasted_iota(jnp.int32, (own, own), 0)
        < lax.broadcasted_iota(jnp.int32, (own, own), 1)
    )
    place = jnp.dot(
        jnp.where(belongs, 1.0, 0.0), jnp.where(earlier, 1.0, 0.0),
        preferred_element_type=jnp.float32,
    )
    code = lax.broadcasted_iota(jnp.int32, (16, own), 1) + own * (
        jnp.broadcast_to(offset_row[...], (16, own)) + 1
    )
    code = jnp.where(belongs, code.astype(jnp.float32), 0.0)
    slot_lane = lax.broadcasted_iota(jnp.int32, (16, LANES), 1)
    filled = jnp.zeros((16, LANES), jnp.float32)
    for slot in range(CAP):
        picked = jnp.sum(jnp.where(place == slot, code, 0.0), axis=1, keepdims=True)
        filled = jnp.where(slot_lane == slot, picked, filled)
    filled = filled.astype(jnp.int32)
    table[...] = filled
    for bucket in range(9):
        rows_out[bucket] = filled[bucket : bucket + 1]
    to_scalar = pltpu.make_async_copy(table, table_scalar, table_sem)
    to_scalar.start()

    loads[0].wait()
    loads[1].wait()
    pack_strip(0, side, LANES - HALO)
    pack_strip(1, LANES, 0)
    for at, step in enumerate(DIRS):
        @pl.when(exists(step))
        def _():
            rim_copy(at).start()
            label_copy(at).start()
    to_scalar.wait()
    lax.fori_loop(1, 4, functools.partial(send_slot, True), 0)
    for load in loads[5:]:
        load.start()
    lax.fori_loop(4, RELAYED, functools.partial(send_slot, True), 0)
    lax.fori_loop(RELAYED, EARLY, functools.partial(send_slot, False), 0)

    loads[8].wait()
    lane = lax.broadcasted_iota(jnp.int32, (8, side), 1)
    u = ((col * side + lane).astype(jnp.float32) + 0.5) * (2.0 / (side * cols)) - 1.0
    for basis in range(BASES):
        for power_v in range(DEGREE + 1):
            total = jnp.zeros_like(u)
            for power_u in reversed(range(DEGREE + 1 - power_v)):
                total = total * u + coef[basis, term_powers.index((power_u, power_v))]
            inner[basis, power_v] = total

    for load in loads[5:8]:
        load.wait()
    wide = padded.shape[1]

    @pl.when(row == 0)
    def _():
        padded[pl.ds(0, HALO)] = jnp.zeros((HALO, wide), jnp.bfloat16)

    @pl.when(row == rows - 1)
    def _():
        padded[pl.ds(side + HALO, HALO)] = jnp.zeros((HALO, wide), jnp.bfloat16)

    @pl.when(col == 0)
    def _():
        padded[:, pl.ds(0, LANES)] = jnp.zeros((padded.shape[0], LANES), jnp.bfloat16)

    @pl.when(col == cols - 1)
    def _():
        padded[:, pl.ds(side + LANES, LANES)] = jnp.zeros((padded.shape[0], LANES), jnp.bfloat16)

    for at, step in enumerate(DIRS):
        @pl.when(exists(opposite(step)))
        def _():
            rim_copy(at).wait_recv()

    def unpack_strip(strip, first_col, first_lane):
        packed = strip_in[strip].astype(jnp.float32)
        for group in range(side // LANES):
            moved = pltpu.roll(packed, (first_lane - group * HALO) % LANES, 1)
            padded[pl.ds(HALO + group * LANES, LANES), pl.ds(first_col, LANES)] = moved.astype(jnp.bfloat16)

    @pl.when(col > 0)
    def _():
        unpack_strip(0, 0, LANES - HALO)

    @pl.when(col < cols - 1)
    def _():
        unpack_strip(1, side + LANES, 0)

    tall = padded.shape[0]
    chunk = tall // 3
    blocks = side // LANES
    for basis in range(BASES):
        across[basis, pl.ds(tall, across.shape[1] - tall)] = jnp.zeros(
            (across.shape[1] - tall, side), jnp.bfloat16
        )

    def row_pass(block, carry):
        first = pl.multiple_of(block * LANES, LANES)
        for part in range(3):
            got = jnp.dot(
                padded[pl.ds(part * chunk, chunk), pl.ds(first, 3 * LANES)],
                row_band[...],
                preferred_element_type=jnp.float32,
            )
            for basis in range(BASES):
                across[basis, pl.ds(part * chunk, chunk), pl.ds(first, LANES)] = got[
                    :, basis * LANES : (basis + 1) * LANES
                ].astype(jnp.bfloat16)
        return carry

    lax.fori_loop(0, blocks, row_pass, 0)

    part_cols = 2 * LANES

    def column_pass(block, carry):
        first = pl.multiple_of(block * LANES, LANES)
        line = lax.broadcasted_iota(jnp.int32, (LANES, part_cols), 0)
        v = ((row * side + first + line).astype(jnp.float32) + 0.5) * (2.0 / (side * rows)) - 1.0
        for part in range(side // part_cols):
            columns = pl.ds(part * part_cols, part_cols)
            total = jnp.zeros((LANES, part_cols), jnp.float32)
            for basis in range(BASES):
                smoothed = jnp.dot(
                    down_band[basis],
                    across[basis, pl.ds(first, 2 * LANES), columns],
                    preferred_element_type=jnp.float32,
                )
                weight = jnp.broadcast_to(inner[basis, DEGREE, 0:1, columns], total.shape)
                for power_v in reversed(range(DEGREE)):
                    weight = weight * v + inner[basis, power_v, 0:1, columns]
                total = total - weight * smoothed
            matched[pl.ds(first, LANES), columns] = total
        return carry

    lax.fori_loop(0, blocks, column_pass, 0)

    for at in range(DIAGONALS):
        @pl.when(turns(DIRS[at]))
        def _():
            relay_copy(at, pl.ds(0, RELAYED)).wait_recv()

            def pass_on(slot, carry):
                onward_copy(at, pl.ds(slot, 1)).start()
                return carry

            lax.fori_loop(0, RELAYED, pass_on, 0)
    lax.fori_loop(EARLY, CAP, functools.partial(send_slot, False), 0)

    for at, step in enumerate(DIRS):
        tags[pl.ds(at, 1)] = jnp.zeros((1, LANES), jnp.int32)

        @pl.when(exists(opposite(step)))
        def _():
            label_copy(at).wait_recv()
            tags[pl.ds(at, 1)] = arrived_table[at]
    tags[pl.ds(len(DIRS), 1)] = table[pl.ds(OWN, 1)]
    sort_plan(own, side // LANES, tags, plan)

    for at in range(DIAGONALS):
        @pl.when(turns(DIRS[at]))
        def _():
            onward_copy(at, pl.ds(0, RELAYED)).wait_send()
    for at, step in enumerate(DIRS):
        @pl.when(exists(step))
        def _():
            rim_copy(at).wait_send()
            label_copy(at).wait_send()
            bucket_copy(at).wait_send()

        @pl.when(exists(opposite(step)))
        def _():
            bucket_copy(at).wait_recv()


def join_kernel(plan, arrived, matched, out, total, out_sem):
    side = out.shape[1]
    per_row = side // LANES

    def row_lines(block_row):
        return pl.ds(pl.multiple_of(block_row * LANES, LANES), LANES)

    def out_copy(block_row):
        lines = row_lines(block_row)
        return pltpu.make_async_copy(total.at[lines], out.at[lines], out_sem.at[block_row])

    def join_row(block_row, start):
        end = plan[3, block_row]
        lines = row_lines(block_row)

        def add(at, carry):
            slot = plan[0, at]
            column = pl.multiple_of((plan[1, at] - block_row * per_row) * LANES, LANES)
            columns = pl.ds(column, LANES)
            piece = arrived[lax.div(slot, CAP), slot & (CAP - 1)].astype(jnp.float32)
            share = 1.0 / jnp.full((8, LANES), jnp.maximum(plan[2, at], 1).astype(jnp.float32))
            share = jnp.tile(share, (LANES // 8, 1))
            total[lines, columns] = total[lines, columns] + share * piece
            return carry

        lax.fori_loop(start, end, add, 0)
        out_copy(block_row).start()
        return end

    lax.fori_loop(0, per_row, join_row, 0)
    for block_row in range(per_row):
        out_copy(block_row).wait()


def on_device(pieces, owner_map, offsets, template, coefficients):
    own, block_side = pieces.shape[0], pieces.shape[1]
    side = template.shape[0]
    smem = pl.BlockSpec(memory_space=pltpu.SMEM)
    vmem = pl.BlockSpec(memory_space=pltpu.VMEM)
    hbm = pl.BlockSpec(memory_space=pltpu.HBM)
    count = len(DIRS)

    band_across, band_down = band_tables()
    tall = side + 2 * HALO
    dma = pltpu.SemaphoreType.DMA
    arrived, plan, matched = pl.pallas_call(
        send_kernel,
        out_shape=[
            jax.ShapeDtypeStruct((count + 1, CAP, block_side, block_side), jnp.bfloat16),
            jax.ShapeDtypeStruct((8, 2 * LANES), jnp.int32),
            jax.ShapeDtypeStruct((side, side), jnp.float32),
        ],
        in_specs=[hbm] * 7,
        out_specs=[vmem, vmem, vmem],
        scratch_shapes=[
            pltpu.VMEM((own, block_side, block_side), jnp.bfloat16),
            pltpu.SMEM(coefficients.shape, jnp.float32),
            pltpu.VMEM((1, own), jnp.int32),
            pltpu.VMEM((1, own), jnp.int32),
            pltpu.VMEM((16, LANES), jnp.int32),
            pltpu.VMEM((9, 1, LANES), jnp.int32),
            pltpu.SMEM((16, LANES), jnp.int32),
            pltpu.VMEM((count, 1, LANES), jnp.int32),
            pltpu.VMEM((16, LANES), jnp.int32),
            pltpu.VMEM((count, CAP, block_side, block_side), jnp.bfloat16),
            pltpu.VMEM((tall, side + 2 * LANES), jnp.bfloat16),
            pltpu.VMEM((2, LANES, LANES), jnp.bfloat16),
            pltpu.VMEM((2, LANES, LANES), jnp.bfloat16),
            pltpu.VMEM((BASES, side + LANES, side), jnp.bfloat16),
            pltpu.VMEM((BASES, DEGREE + 1, 8, side), jnp.float32),
            pltpu.VMEM(band_across.shape, jnp.bfloat16),
            pltpu.VMEM(band_down.shape, jnp.bfloat16),
            pltpu.VMEM((DIAGONALS, RELAYED, block_side, block_side), jnp.bfloat16),
            dma((9,)), dma, dma((count,)), dma((count,)), dma((count,)), dma((count,)),
            dma((count,)), dma((count,)), dma((DIAGONALS,)), dma((DIAGONALS,)),
        ],
        compiler_params=pltpu.CompilerParams(
            collective_id=0, has_side_effects=True, vmem_limit_bytes=40 << 20
        ),
        name="send",
    )(
        *(
            pltpu.with_memory_space_constraint(array, pltpu.HBM)
            for array in (
                owner_map.reshape(1, own), offsets.reshape(1, own), coefficients, pieces,
                template, jnp.asarray(band_across), jnp.asarray(band_down),
            )
        )
    )
    joined, _ = pl.pallas_call(
        join_kernel,
        out_shape=[jax.ShapeDtypeStruct((side, side), jnp.float32)] * 2,
        in_specs=[smem, vmem, vmem],
        out_specs=[hbm, vmem],
        input_output_aliases={2: 1},
        scratch_shapes=[dma((side // block_side,))],
        compiler_params=pltpu.CompilerParams(vmem_limit_bytes=32 << 20),
        name="join",
    )(plan, arrived, matched)
    return joined


def solution(mesh):
    in_specs = (P(("py", "px"), None, None), P(("py", "px")), P(("py", "px")), P("py", "px"), P())
    out_specs = P("py", "px")
    return jax.shard_map(
        on_device, mesh=mesh, in_specs=in_specs, out_specs=out_specs, check_vma=False
    )
```

```python
import functools

import jax
import jax.numpy as jnp
import numpy as np
from jax import lax
from jax.experimental import pallas as pl
from jax.experimental.pallas import tpu as pltpu
from jax.sharding import PartitionSpec as P

HALO = 16
CAP = 16
LANES = 128
BASES = 3
DEGREE = 4

sigma_fractions = (0.09375, 0.1875, 0.375)
term_powers = [(degree - power_v, power_v) for degree in range(5) for power_v in range(degree + 1)]

DIRS = ((1, 1), (-1, -1), (1, -1), (-1, 1), (0, 1), (0, -1), (1, 0), (-1, 0))
DIAGONALS = 4
RELAYED = 8
OWN = 4
MESH = pl.DeviceIdType.MESH


def bucket_of(step):
    return 3 * (step[0] + 1) + step[1] + 1


def gauss_taps():
    positions = np.arange(-HALO, HALO + 1).astype(np.float32)
    stacked = []
    for fraction in sigma_fractions:
        sigma = fraction * HALO
        values = np.exp(-positions * positions / np.float32(2.0 * sigma * sigma))
        stacked.append(values / np.sum(values))
    return np.stack(stacked).astype(jnp.bfloat16)


def band_tables():
    taps = gauss_taps()
    across = np.zeros((3 * LANES, BASES * LANES), taps.dtype)
    down = np.zeros((BASES, LANES, 2 * LANES), taps.dtype)
    for basis in range(BASES):
        for out in range(LANES):
            for tap in range(2 * HALO + 1):
                across[LANES - HALO + out + tap, basis * LANES + out] = taps[basis, tap]
                down[basis, out, out + tap] = taps[basis, tap]
    return across, down


def sort_plan(own, per_row, tags, plan, share):
    count = len(DIRS)
    blocks = per_row * per_row
    shape = (blocks, LANES)
    code = tags[...]
    block_tag = lax.shift_right_logical(code, own.bit_length() - 1).astype(jnp.float32)
    spread = jnp.zeros((8, LANES), jnp.float32)
    for at in range(count):
        one = jnp.broadcast_to(block_tag[at : at + 1], (8, LANES))
        spread = spread + pltpu.roll(one, at * CAP, 1)
    groups = (spread[0:1], block_tag[count : count + 1])

    block_id = lax.broadcasted_iota(jnp.int32, shape, 0).astype(jnp.float32)
    before = jnp.where(
        lax.broadcasted_iota(jnp.int32, (LANES, LANES), 0)
        < lax.broadcasted_iota(jnp.int32, (LANES, LANES), 1), 1.0, 0.0,
    )
    lower = jnp.where(
        lax.broadcasted_iota(jnp.int32, (blocks, blocks), 1)
        < lax.broadcasted_iota(jnp.int32, (blocks, blocks), 0), 1.0, 0.0,
    )
    hits = [jnp.where(jnp.broadcast_to(tag, shape) == block_id + 1, 1.0, 0.0) for tag in groups]
    sums = [jnp.broadcast_to(jnp.sum(hit, axis=1, keepdims=True), shape) for hit in hits]
    covered = sums[0] + sums[1]
    first = jnp.dot(lower, covered, preferred_element_type=jnp.float32)
    ahead = (first, first + sums[0])

    line = lax.broadcasted_iota(jnp.int32, (8, LANES), 0)
    lane = lax.broadcasted_iota(jnp.int32, (8, LANES), 1).astype(jnp.float32)
    target = lax.broadcasted_iota(jnp.int32, (2 * LANES, LANES), 0).astype(jnp.float32)
    over_lanes = (((1,), (1,)), ((), ()))
    listed = jnp.zeros((8, 2 * LANES), jnp.float32)
    ends = jnp.zeros((8, 2 * LANES), jnp.float32)
    for group in range(2):
        hit, tag = hits[group], groups[group]
        rank = ahead[group] + jnp.dot(hit, before, preferred_element_type=jnp.float32)
        place = jnp.sum(hit * rank, axis=0, keepdims=True)
        shares = jnp.sum(hit * covered, axis=0, keepdims=True)
        place = jnp.where(tag > 0, place, -1.0)
        chosen = jnp.where(jnp.broadcast_to(place, target.shape) == target, 1.0, 0.0)
        values = jnp.where(line == 0, lane + group * LANES, 0.0)
        values = jnp.where(line == 1, jnp.broadcast_to(tag - 1, values.shape), values)
        values = jnp.where(line == 2, jnp.broadcast_to(shares, values.shape), values)
        listed = listed + lax.dot_general(
            values, chosen, over_lanes, preferred_element_type=jnp.float32
        )
        wide_tag = jnp.broadcast_to(tag, target.shape)
        inside = jnp.where((wide_tag > 0) & (wide_tag <= (target + 1) * per_row), 1.0, 0.0)
        ends = ends + lax.dot_general(
            jnp.ones((8, LANES), jnp.float32), inside, over_lanes,
            preferred_element_type=jnp.float32,
        )
    wide_line = lax.broadcasted_iota(jnp.int32, listed.shape, 0)
    plan[...] = jnp.where(wide_line == 3, ends, listed).astype(jnp.int32)
    share[...] = 1.0 / jnp.maximum(listed, 1.0)


def send_kernel(
    owner, offset, coef_hbm, pieces, template, band_across, band_down,
    arrived, plan_scalar, share_scalar, matched,
    plan, share,
    held, coef, owner_row, offset_row, table, rows_out, table_scalar, arrived_table,
    tags, outgoing, padded, strip_out, strip_in, across, inner, row_band, down_band,
    relay, load_sem, table_sem, send_sem, recv_sem, label_send, label_recv, rim_send, rim_recv,
    relay_recv, onward_send,
):
    rows, cols = lax.axis_size("py"), lax.axis_size("px")
    row, col = lax.axis_index("py"), lax.axis_index("px")
    side = template.shape[0]
    last = side - LANES
    own = held.shape[0]

    def exists(step):
        r, c = row + step[0], col + step[1]
        return (r >= 0) & (r < rows) & (c >= 0) & (c < cols)

    def neighbour(step):
        return (row + step[0], col + step[1])

    barrier = pltpu.get_barrier_semaphore()
    for step in DIRS:
        @pl.when(exists(step))
        def _():
            pl.semaphore_signal(barrier, inc=1, device_id=neighbour(step), device_id_type=MESH)

    body = padded.at[pl.ds(HALO, side)]
    loads = [
        pltpu.make_async_copy(
            template.at[:, pl.ds(0, LANES)], body.at[:, pl.ds(LANES, LANES)], load_sem.at[0]
        ),
        pltpu.make_async_copy(
            template.at[:, pl.ds(last, LANES)], body.at[:, pl.ds(side, LANES)], load_sem.at[1]
        ),
        pltpu.make_async_copy(owner, owner_row, load_sem.at[2]),
        pltpu.make_async_copy(offset, offset_row, load_sem.at[3]),
        pltpu.make_async_copy(pieces, held, load_sem.at[4]),
        pltpu.make_async_copy(
            template.at[:, pl.ds(LANES, side - 2 * LANES)],
            body.at[:, pl.ds(2 * LANES, side - 2 * LANES)],
            load_sem.at[5],
        ),
        pltpu.make_async_copy(band_across, row_band, load_sem.at[6]),
        pltpu.make_async_copy(band_down, down_band, load_sem.at[7]),
        pltpu.make_async_copy(coef_hbm, coef, load_sem.at[8]),
    ]
    for load in (loads[2], loads[4], loads[3], loads[0], loads[1]):
        load.start()

    def opposite(step):
        return (-step[0], -step[1])

    def rim_copy(at):
        step = DIRS[at]
        if step[0] == 0:
            source = strip_out.at[0 if step[1] > 0 else 1]
            target = strip_in.at[0 if step[1] > 0 else 1]
        else:
            source_rows = pl.ds(side - HALO if step[0] > 0 else 0, HALO)
            target_rows = pl.ds(0 if step[0] > 0 else side + HALO, HALO)
            if step[1] == 0:
                source = template.at[source_rows]
                target = padded.at[target_rows, pl.ds(LANES, side)]
            else:
                source = template.at[source_rows, pl.ds(last if step[1] > 0 else 0, LANES)]
                target = padded.at[target_rows, pl.ds(0 if step[1] > 0 else side + LANES, LANES)]
        return pltpu.make_async_remote_copy(
            src_ref=source, dst_ref=target, send_sem=rim_send.at[at], recv_sem=rim_recv.at[at],
            device_id=neighbour(step), device_id_type=MESH,
        )

    def label_copy(at):
        return pltpu.make_async_remote_copy(
            src_ref=rows_out.at[bucket_of(DIRS[at])], dst_ref=arrived_table.at[at], send_sem=label_send.at[at],
            recv_sem=label_recv.at[at], device_id=neighbour(DIRS[at]), device_id_type=MESH,
        )

    def bucket_copy(at, slots=pl.ds(0, CAP)):
        return pltpu.make_async_remote_copy(
            src_ref=outgoing.at[at, slots], dst_ref=arrived.at[at, slots], send_sem=send_sem.at[at],
            recv_sem=recv_sem.at[at], device_id=neighbour(DIRS[at]), device_id_type=MESH,
        )

    def pack_strip(strip, first_col, first_lane):
        lane_group = lax.broadcasted_iota(jnp.int32, (LANES, LANES), 1) // HALO
        packed = jnp.zeros((LANES, LANES), jnp.float32)
        for group in range(side // LANES):
            block = padded[pl.ds(HALO + group * LANES, LANES), pl.ds(first_col, LANES)]
            moved = pltpu.roll(
                block.astype(jnp.float32), (group * HALO - first_lane) % LANES, 1
            )
            packed = jnp.where(lane_group == group, moved, packed)
        strip_out[strip] = packed.astype(jnp.bfloat16)

    def column_first(step):
        return row == (2 if step[0] < 0 else rows - 3)

    def row_first(step):
        return row == (1 if step[0] > 0 else rows - 2)

    def relay_copy(at, slots):
        step = DIRS[at]
        return pltpu.make_async_remote_copy(
            src_ref=outgoing.at[at, slots], dst_ref=relay.at[at, slots],
            send_sem=send_sem.at[at], recv_sem=relay_recv.at[at],
            device_id=(
                row + jnp.where(row_first(step), 0, step[0]),
                col + jnp.where(column_first(step), 0, step[1]),
            ),
            device_id_type=MESH,
        )

    def turns_column(step):
        return row == (1 if step[0] < 0 else rows - 2)

    def turns_row(step):
        return row == (1 if step[0] > 0 else rows - 2)

    def turns(step):
        ahead, behind = col + step[1], col - step[1]
        return (turns_column(step) & (ahead >= 0) & (ahead < cols)) | (
            turns_row(step) & (behind >= 0) & (behind < cols)
        )

    def onward_copy(at, slots):
        step = DIRS[at]
        return pltpu.make_async_remote_copy(
            src_ref=relay.at[at, slots], dst_ref=arrived.at[at, slots],
            send_sem=onward_send.at[at], recv_sem=recv_sem.at[at],
            device_id=(
                row + jnp.where(turns_row(step), step[0], 0),
                col + jnp.where(turns_column(step), step[1], 0),
            ),
            device_id_type=MESH,
        )

    def send_pieces(slot, piece_of, relayed):
        for at, step in enumerate(DIRS):
            outgoing[at, slot] = held[piece_of(bucket_of(step))]
            direct = exists(step)
            if relayed and at < DIAGONALS:
                turned = column_first(step) | row_first(step)

                @pl.when(direct & turned)
                def _():
                    relay_copy(at, pl.ds(slot, 1)).start()
                direct = direct & jnp.logical_not(turned)

            @pl.when(direct)
            def _():
                bucket_copy(at, pl.ds(slot, 1)).start()
        arrived[len(DIRS), slot] = held[piece_of(OWN)]

    def send_slot(relayed, slot, carry):
        send_pieces(slot, lambda bucket: table_scalar[bucket, slot] & (own - 1), relayed)
        return carry

    loads[2].wait()
    bucket_id = lax.broadcasted_iota(jnp.int32, (16, own), 0)
    target = jnp.full((16, own), -1, jnp.int32)
    for bucket in range(9):
        tile = (row + bucket // 3 - 1) * cols + col + bucket % 3 - 1
        target = jnp.where(bucket_id == bucket, tile, target)
    belongs = target == jnp.broadcast_to(owner_row[...], (16, own))
    number = lax.broadcasted_iota(jnp.int32, (16, own), 1).astype(jnp.float32)
    leader = [
        jnp.min(jnp.where(belongs & (bucket_id == bucket), number, own - 1.0)).astype(jnp.int32)
        & (own - 1)
        for bucket in range(9)
    ]
    tall_group = 3 - jnp.where(row == 0, 1, 0) - jnp.where(row == rows - 1, 1, 0)
    wide_group = 3 - jnp.where(col == 0, 1, 0) - jnp.where(col == cols - 1, 1, 0)
    pl.semaphore_wait(barrier, tall_group * wide_group - 1)
    loads[4].wait()
    send_pieces(0, lambda bucket: leader[bucket], True)

    loads[3].wait()
    earlier = (
        lax.broadcasted_iota(jnp.int32, (own, own), 0)
        < lax.broadcasted_iota(jnp.int32, (own, own), 1)
    )
    place = jnp.dot(
        jnp.where(belongs, 1.0, 0.0), jnp.where(earlier, 1.0, 0.0),
        preferred_element_type=jnp.float32,
    )
    code = lax.broadcasted_iota(jnp.int32, (16, own), 1) + own * (
        jnp.broadcast_to(offset_row[...], (16, own)) + 1
    )
    code = jnp.where(belongs, code.astype(jnp.float32), 0.0)
    slot_lane = lax.broadcasted_iota(jnp.int32, (16, LANES), 1)
    filled = jnp.zeros((16, LANES), jnp.float32)
    for slot in range(CAP):
        picked = jnp.sum(jnp.where(place == slot, code, 0.0), axis=1, keepdims=True)
        filled = jnp.where(slot_lane == slot, picked, filled)
    filled = filled.astype(jnp.int32)
    table[...] = filled
    for bucket in range(9):
        rows_out[bucket] = filled[bucket : bucket + 1]
    to_scalar = pltpu.make_async_copy(table, table_scalar, table_sem)
    to_scalar.start()

    loads[0].wait()
    loads[1].wait()
    pack_strip(0, side, LANES - HALO)
    pack_strip(1, LANES, 0)
    for at, step in enumerate(DIRS):
        @pl.when(exists(step))
        def _():
            rim_copy(at).start()
            label_copy(at).start()
    to_scalar.wait()
    lax.fori_loop(1, 4, functools.partial(send_slot, True), 0)
    for load in loads[5:]:
        load.start()
    lax.fori_loop(4, RELAYED, functools.partial(send_slot, True), 0)
    lax.fori_loop(RELAYED, CAP, functools.partial(send_slot, False), 0)

    loads[8].wait()
    lane = lax.broadcasted_iota(jnp.int32, (8, side), 1)
    u = ((col * side + lane).astype(jnp.float32) + 0.5) * (2.0 / (side * cols)) - 1.0
    for basis in range(BASES):
        for power_v in range(DEGREE + 1):
            total = jnp.zeros_like(u)
            for power_u in reversed(range(DEGREE + 1 - power_v)):
                total = total * u + coef[basis, term_powers.index((power_u, power_v))]
            inner[basis, power_v] = total

    for load in loads[5:8]:
        load.wait()
    wide = padded.shape[1]

    @pl.when(row == 0)
    def _():
        padded[pl.ds(0, HALO)] = jnp.zeros((HALO, wide), jnp.bfloat16)

    @pl.when(row == rows - 1)
    def _():
        padded[pl.ds(side + HALO, HALO)] = jnp.zeros((HALO, wide), jnp.bfloat16)

    @pl.when(col == 0)
    def _():
        padded[:, pl.ds(0, LANES)] = jnp.zeros((padded.shape[0], LANES), jnp.bfloat16)

    @pl.when(col == cols - 1)
    def _():
        padded[:, pl.ds(side + LANES, LANES)] = jnp.zeros((padded.shape[0], LANES), jnp.bfloat16)

    for at, step in enumerate(DIRS):
        @pl.when(exists(opposite(step)))
        def _():
            rim_copy(at).wait_recv()

    def unpack_strip(strip, first_col, first_lane):
        packed = strip_in[strip].astype(jnp.float32)
        for group in range(side // LANES):
            moved = pltpu.roll(packed, (first_lane - group * HALO) % LANES, 1)
            padded[pl.ds(HALO + group * LANES, LANES), pl.ds(first_col, LANES)] = moved.astype(jnp.bfloat16)

    @pl.when(col > 0)
    def _():
        unpack_strip(0, 0, LANES - HALO)

    @pl.when(col < cols - 1)
    def _():
        unpack_strip(1, side + LANES, 0)

    tall = padded.shape[0]
    chunk = tall // 3
    blocks = side // LANES
    for basis in range(BASES):
        across[basis, pl.ds(tall, across.shape[1] - tall)] = jnp.zeros(
            (across.shape[1] - tall, side), jnp.bfloat16
        )

    def row_pass(block, carry):
        first = pl.multiple_of(block * LANES, LANES)
        for part in range(3):
            got = jnp.dot(
                padded[pl.ds(part * chunk, chunk), pl.ds(first, 3 * LANES)],
                row_band[...],
                preferred_element_type=jnp.float32,
            )
            for basis in range(BASES):
                across[basis, pl.ds(part * chunk, chunk), pl.ds(first, LANES)] = got[
                    :, basis * LANES : (basis + 1) * LANES
                ].astype(jnp.bfloat16)
        return carry

    lax.fori_loop(0, blocks, row_pass, 0)

    part_cols = 2 * LANES

    def column_pass(block, carry):
        first = pl.multiple_of(block * LANES, LANES)
        line = lax.broadcasted_iota(jnp.int32, (LANES, part_cols), 0)
        v = ((row * side + first + line).astype(jnp.float32) + 0.5) * (2.0 / (side * rows)) - 1.0
        for part in range(side // part_cols):
            columns = pl.ds(part * part_cols, part_cols)
            total = jnp.zeros((LANES, part_cols), jnp.float32)
            for basis in range(BASES):
                smoothed = jnp.dot(
                    down_band[basis],
                    across[basis, pl.ds(first, 2 * LANES), columns],
                    preferred_element_type=jnp.float32,
                )
                weight = jnp.broadcast_to(inner[basis, DEGREE, 0:1, columns], total.shape)
                for power_v in reversed(range(DEGREE)):
                    weight = weight * v + inner[basis, power_v, 0:1, columns]
                total = total - weight * smoothed
            matched[pl.ds(first, LANES), columns] = total
        return carry

    lax.fori_loop(0, blocks, column_pass, 0)

    for at in range(DIAGONALS):
        @pl.when(turns(DIRS[at]))
        def _():
            relay_copy(at, pl.ds(0, RELAYED)).wait_recv()

            def pass_on(slot, carry):
                onward_copy(at, pl.ds(slot, 1)).start()
                return carry

            lax.fori_loop(0, RELAYED, pass_on, 0)

    for at, step in enumerate(DIRS):
        tags[pl.ds(at, 1)] = jnp.zeros((1, LANES), jnp.int32)

        @pl.when(exists(opposite(step)))
        def _():
            label_copy(at).wait_recv()
            tags[pl.ds(at, 1)] = arrived_table[at]
    tags[pl.ds(len(DIRS), 1)] = table[pl.ds(OWN, 1)]
    sort_plan(own, side // LANES, tags, plan, share)
    plan_copies = [
        pltpu.make_async_copy(plan, plan_scalar, load_sem.at[0]),
        pltpu.make_async_copy(share, share_scalar, load_sem.at[1]),
    ]
    for plan_copy in plan_copies:
        plan_copy.start()

    for at in range(DIAGONALS):
        @pl.when(turns(DIRS[at]))
        def _():
            onward_copy(at, pl.ds(0, RELAYED)).wait_send()
    for at, step in enumerate(DIRS):
        @pl.when(exists(step))
        def _():
            rim_copy(at).wait_send()
            label_copy(at).wait_send()
            bucket_copy(at).wait_send()

        @pl.when(exists(opposite(step)))
        def _():
            bucket_copy(at).wait_recv()
    for plan_copy in plan_copies:
        plan_copy.wait()


def join_kernel(plan, share, arrived, matched, out, total, out_sem):
    side = out.shape[1]
    per_row = side // LANES

    def row_lines(block_row):
        return pl.ds(pl.multiple_of(block_row * LANES, LANES), LANES)

    def out_copy(block_row):
        lines = row_lines(block_row)
        return pltpu.make_async_copy(total.at[lines], out.at[lines], out_sem.at[block_row])

    def join_row(block_row, start):
        end = plan[3, block_row]
        lines = row_lines(block_row)

        def add(at, carry):
            slot = plan[0, at]
            column = pl.multiple_of((plan[1, at] - block_row * per_row) * LANES, LANES)
            columns = pl.ds(column, LANES)
            piece = arrived[lax.div(slot, CAP), slot & (CAP - 1)].astype(jnp.float32)
            total[lines, columns] = total[lines, columns] + share[2, at] * piece
            return carry

        lax.fori_loop(start, end, add, 0)
        out_copy(block_row).start()
        return end

    lax.fori_loop(0, per_row, join_row, 0)
    for block_row in range(per_row):
        out_copy(block_row).wait()


def on_device(pieces, owner_map, offsets, template, coefficients):
    own, block_side = pieces.shape[0], pieces.shape[1]
    side = template.shape[0]
    smem = pl.BlockSpec(memory_space=pltpu.SMEM)
    vmem = pl.BlockSpec(memory_space=pltpu.VMEM)
    hbm = pl.BlockSpec(memory_space=pltpu.HBM)
    count = len(DIRS)

    band_across, band_down = band_tables()
    tall = side + 2 * HALO
    dma = pltpu.SemaphoreType.DMA
    arrived, plan, share, matched = pl.pallas_call(
        send_kernel,
        out_shape=[
            jax.ShapeDtypeStruct((count + 1, CAP, block_side, block_side), jnp.bfloat16),
            pltpu.SMEM((8, 2 * LANES), jnp.int32),
            pltpu.SMEM((8, 2 * LANES), jnp.float32),
            jax.ShapeDtypeStruct((side, side), jnp.float32),
        ],
        in_specs=[hbm] * 7,
        out_specs=[vmem, smem, smem, vmem],
        scratch_shapes=[
            pltpu.VMEM((8, 2 * LANES), jnp.int32),
            pltpu.VMEM((8, 2 * LANES), jnp.float32),
            pltpu.VMEM((own, block_side, block_side), jnp.bfloat16),
            pltpu.SMEM(coefficients.shape, jnp.float32),
            pltpu.VMEM((1, own), jnp.int32),
            pltpu.VMEM((1, own), jnp.int32),
            pltpu.VMEM((16, LANES), jnp.int32),
            pltpu.VMEM((9, 1, LANES), jnp.int32),
            pltpu.SMEM((16, LANES), jnp.int32),
            pltpu.VMEM((count, 1, LANES), jnp.int32),
            pltpu.VMEM((16, LANES), jnp.int32),
            pltpu.VMEM((count, CAP, block_side, block_side), jnp.bfloat16),
            pltpu.VMEM((tall, side + 2 * LANES), jnp.bfloat16),
            pltpu.VMEM((2, LANES, LANES), jnp.bfloat16),
            pltpu.VMEM((2, LANES, LANES), jnp.bfloat16),
            pltpu.VMEM((BASES, side + LANES, side), jnp.bfloat16),
            pltpu.VMEM((BASES, DEGREE + 1, 8, side), jnp.float32),
            pltpu.VMEM(band_across.shape, jnp.bfloat16),
            pltpu.VMEM(band_down.shape, jnp.bfloat16),
            pltpu.VMEM((DIAGONALS, RELAYED, block_side, block_side), jnp.bfloat16),
            dma((9,)), dma, dma((count,)), dma((count,)), dma((count,)), dma((count,)),
            dma((count,)), dma((count,)), dma((DIAGONALS,)), dma((DIAGONALS,)),
        ],
        compiler_params=pltpu.CompilerParams(
            collective_id=0, has_side_effects=True, vmem_limit_bytes=40 << 20
        ),
        name="send",
    )(
        *(
            pltpu.with_memory_space_constraint(array, pltpu.HBM)
            for array in (
                owner_map.reshape(1, own), offsets.reshape(1, own), coefficients, pieces,
                template, jnp.asarray(band_across), jnp.asarray(band_down),
            )
        )
    )
    joined, _ = pl.pallas_call(
        join_kernel,
        out_shape=[jax.ShapeDtypeStruct((side, side), jnp.float32)] * 2,
        in_specs=[smem, smem, vmem, vmem],
        out_specs=[hbm, vmem],
        input_output_aliases={3: 1},
        scratch_shapes=[dma((side // block_side,))],
        compiler_params=pltpu.CompilerParams(vmem_limit_bytes=32 << 20),
        name="join",
    )(plan, share, arrived, matched)
    return joined


def solution(mesh):
    in_specs = (P(("py", "px"), None, None), P(("py", "px")), P(("py", "px")), P("py", "px"), P())
    out_specs = P("py", "px")
    return jax.shard_map(
        on_device, mesh=mesh, in_specs=in_specs, out_specs=out_specs, check_vma=False
    )
```

```python
import functools

import jax
import jax.numpy as jnp
import numpy as np
from jax import lax
from jax.experimental import pallas as pl
from jax.experimental.pallas import tpu as pltpu
from jax.sharding import PartitionSpec as P

HALO = 16
CAP = 16
LANES = 128
BASES = 3
DEGREE = 4

sigma_fractions = (0.09375, 0.1875, 0.375)
term_powers = [(degree - power_v, power_v) for degree in range(5) for power_v in range(degree + 1)]

DIRS = ((1, 1), (-1, -1), (1, -1), (-1, 1), (0, 1), (0, -1), (1, 0), (-1, 0))
DIAGONALS = 4
RELAYED = 8
PLANE = 4
DETOUR = 3
EARLY = 12
OWN = 4
MESH = pl.DeviceIdType.MESH


def bucket_of(step):
    return 3 * (step[0] + 1) + step[1] + 1


def gauss_taps():
    positions = np.arange(-HALO, HALO + 1).astype(np.float32)
    stacked = []
    for fraction in sigma_fractions:
        sigma = fraction * HALO
        values = np.exp(-positions * positions / np.float32(2.0 * sigma * sigma))
        stacked.append(values / np.sum(values))
    return np.stack(stacked).astype(jnp.bfloat16)


def band_tables():
    taps = gauss_taps()
    across = np.zeros((3 * LANES, BASES * LANES), taps.dtype)
    down = np.zeros((BASES, LANES, 2 * LANES), taps.dtype)
    for basis in range(BASES):
        for out in range(LANES):
            for tap in range(2 * HALO + 1):
                across[LANES - HALO + out + tap, basis * LANES + out] = taps[basis, tap]
                down[basis, out, out + tap] = taps[basis, tap]
    return across, down


def sort_plan(own, per_row, tags, plan, share):
    count = len(DIRS)
    blocks = per_row * per_row
    shape = (blocks, LANES)
    code = tags[...]
    block_tag = lax.shift_right_logical(code, own.bit_length() - 1).astype(jnp.float32)
    spread = jnp.zeros((8, LANES), jnp.float32)
    for at in range(count):
        one = jnp.broadcast_to(block_tag[at : at + 1], (8, LANES))
        spread = spread + pltpu.roll(one, at * CAP, 1)
    groups = (spread[0:1], block_tag[count : count + 1])

    block_id = lax.broadcasted_iota(jnp.int32, shape, 0).astype(jnp.float32)
    before = jnp.where(
        lax.broadcasted_iota(jnp.int32, (LANES, LANES), 0)
        < lax.broadcasted_iota(jnp.int32, (LANES, LANES), 1), 1.0, 0.0,
    )
    lower = jnp.where(
        lax.broadcasted_iota(jnp.int32, (blocks, blocks), 1)
        < lax.broadcasted_iota(jnp.int32, (blocks, blocks), 0), 1.0, 0.0,
    )
    hits = [jnp.where(jnp.broadcast_to(tag, shape) == block_id + 1, 1.0, 0.0) for tag in groups]
    sums = [jnp.broadcast_to(jnp.sum(hit, axis=1, keepdims=True), shape) for hit in hits]
    covered = sums[0] + sums[1]
    first = jnp.dot(lower, covered, preferred_element_type=jnp.float32)
    ahead = (first, first + sums[0])

    line = lax.broadcasted_iota(jnp.int32, (8, LANES), 0)
    lane = lax.broadcasted_iota(jnp.int32, (8, LANES), 1).astype(jnp.float32)
    target = lax.broadcasted_iota(jnp.int32, (2 * LANES, LANES), 0).astype(jnp.float32)
    over_lanes = (((1,), (1,)), ((), ()))
    listed = jnp.zeros((8, 2 * LANES), jnp.float32)
    ends = jnp.zeros((8, 2 * LANES), jnp.float32)
    for group in range(2):
        hit, tag = hits[group], groups[group]
        rank = ahead[group] + jnp.dot(hit, before, preferred_element_type=jnp.float32)
        place = jnp.sum(hit * rank, axis=0, keepdims=True)
        shares = jnp.sum(hit * covered, axis=0, keepdims=True)
        place = jnp.where(tag > 0, place, -1.0)
        chosen = jnp.where(jnp.broadcast_to(place, target.shape) == target, 1.0, 0.0)
        values = jnp.where(line == 0, lane + group * LANES, 0.0)
        values = jnp.where(line == 1, jnp.broadcast_to(tag - 1, values.shape), values)
        values = jnp.where(line == 2, jnp.broadcast_to(shares, values.shape), values)
        listed = listed + lax.dot_general(
            values, chosen, over_lanes, preferred_element_type=jnp.float32
        )
        wide_tag = jnp.broadcast_to(tag, target.shape)
        inside = jnp.where((wide_tag > 0) & (wide_tag <= (target + 1) * per_row), 1.0, 0.0)
        ends = ends + lax.dot_general(
            jnp.ones((8, LANES), jnp.float32), inside, over_lanes,
            preferred_element_type=jnp.float32,
        )
    wide_line = lax.broadcasted_iota(jnp.int32, listed.shape, 0)
    plan[...] = jnp.where(wide_line == 3, ends, listed).astype(jnp.int32)
    share[...] = 1.0 / jnp.maximum(listed, 1.0)


def send_kernel(
    owner, offset, coef_hbm, pieces, template, band_across, band_down,
    arrived, plan_scalar, share_scalar, matched,
    plan, share,
    held, coef, owner_row, offset_row, table, rows_out, table_scalar, arrived_table,
    tags, outgoing, padded, strip_out, strip_in, across, inner, row_band, down_band,
    relay, load_sem, table_sem, send_sem, recv_sem, label_send, label_recv, rim_send, rim_recv,
    relay_recv, onward_send, detour, detour_recv, detour_send,
):
    rows, cols = lax.axis_size("py"), lax.axis_size("px")
    row, col = lax.axis_index("py"), lax.axis_index("px")
    side = template.shape[0]
    last = side - LANES
    own = held.shape[0]

    def exists(step):
        r, c = row + step[0], col + step[1]
        return (r >= 0) & (r < rows) & (c >= 0) & (c < cols)

    def neighbour(step):
        return (row + step[0], col + step[1])

    plane = lax.div(col, PLANE)
    planes = cols // PLANE
    leads = col - plane * PLANE == 0
    trails = col - plane * PLANE == PLANE - 1

    barrier = pltpu.get_barrier_semaphore()
    for step in DIRS:
        @pl.when(exists(step))
        def _():
            pl.semaphore_signal(barrier, inc=1, device_id=neighbour(step), device_id_type=MESH)

    for far, there in (
        (PLANE - 1, leads),
        (1 - PLANE, trails),
        (PLANE, (leads | trails) & (plane < planes - 1)),
        (-PLANE, (leads | trails) & (plane > 0)),
    ):
        @pl.when(there)
        def _():
            pl.semaphore_signal(
                barrier, inc=1, device_id=(row, col + far), device_id_type=MESH
            )

    body = padded.at[pl.ds(HALO, side)]
    loads = [
        pltpu.make_async_copy(
            template.at[:, pl.ds(0, LANES)], body.at[:, pl.ds(LANES, LANES)], load_sem.at[0]
        ),
        pltpu.make_async_copy(
            template.at[:, pl.ds(last, LANES)], body.at[:, pl.ds(side, LANES)], load_sem.at[1]
        ),
        pltpu.make_async_copy(owner, owner_row, load_sem.at[2]),
        pltpu.make_async_copy(offset, offset_row, load_sem.at[3]),
        pltpu.make_async_copy(pieces, held, load_sem.at[4]),
        pltpu.make_async_copy(
            template.at[:, pl.ds(LANES, side - 2 * LANES)],
            body.at[:, pl.ds(2 * LANES, side - 2 * LANES)],
            load_sem.at[5],
        ),
        pltpu.make_async_copy(band_across, row_band, load_sem.at[6]),
        pltpu.make_async_copy(band_down, down_band, load_sem.at[7]),
        pltpu.make_async_copy(coef_hbm, coef, load_sem.at[8]),
    ]
    for load in (loads[2], loads[4], loads[3], loads[0], loads[1]):
        load.start()

    def opposite(step):
        return (-step[0], -step[1])

    def rim_copy(at):
        step = DIRS[at]
        if step[0] == 0:
            source = strip_out.at[0 if step[1] > 0 else 1]
            target = strip_in.at[0 if step[1] > 0 else 1]
        else:
            source_rows = pl.ds(side - HALO if step[0] > 0 else 0, HALO)
            target_rows = pl.ds(0 if step[0] > 0 else side + HALO, HALO)
            if step[1] == 0:
                source = template.at[source_rows]
                target = padded.at[target_rows, pl.ds(LANES, side)]
            else:
                source = template.at[source_rows, pl.ds(last if step[1] > 0 else 0, LANES)]
                target = padded.at[target_rows, pl.ds(0 if step[1] > 0 else side + LANES, LANES)]
        return pltpu.make_async_remote_copy(
            src_ref=source, dst_ref=target, send_sem=rim_send.at[at], recv_sem=rim_recv.at[at],
            device_id=neighbour(step), device_id_type=MESH,
        )

    def label_copy(at):
        return pltpu.make_async_remote_copy(
            src_ref=rows_out.at[bucket_of(DIRS[at])], dst_ref=arrived_table.at[at], send_sem=label_send.at[at],
            recv_sem=label_recv.at[at], device_id=neighbour(DIRS[at]), device_id_type=MESH,
        )

    def bucket_copy(at, slots=pl.ds(0, CAP)):
        return pltpu.make_async_remote_copy(
            src_ref=outgoing.at[at, slots], dst_ref=arrived.at[at, slots], send_sem=send_sem.at[at],
            recv_sem=recv_sem.at[at], device_id=neighbour(DIRS[at]), device_id_type=MESH,
        )

    def pack_strip(strip, first_col, first_lane):
        lane_group = lax.broadcasted_iota(jnp.int32, (LANES, LANES), 1) // HALO
        packed = jnp.zeros((LANES, LANES), jnp.float32)
        for group in range(side // LANES):
            block = padded[pl.ds(HALO + group * LANES, LANES), pl.ds(first_col, LANES)]
            moved = pltpu.roll(
                block.astype(jnp.float32), (group * HALO - first_lane) % LANES, 1
            )
            packed = jnp.where(lane_group == group, moved, packed)
        strip_out[strip] = packed.astype(jnp.bfloat16)

    def column_first(step):
        return row == (2 if step[0] < 0 else rows - 3)

    def row_first(step):
        return row == (1 if step[0] > 0 else rows - 2)

    def relay_copy(at, slots):
        step = DIRS[at]
        return pltpu.make_async_remote_copy(
            src_ref=outgoing.at[at, slots], dst_ref=relay.at[at, slots],
            send_sem=send_sem.at[at], recv_sem=relay_recv.at[at],
            device_id=(
                row + jnp.where(row_first(step), 0, step[0]),
                col + jnp.where(column_first(step), 0, step[1]),
            ),
            device_id_type=MESH,
        )

    def turns_column(step):
        return row == (1 if step[0] < 0 else rows - 2)

    def turns_row(step):
        return row == (1 if step[0] > 0 else rows - 2)

    def turns(step):
        ahead, behind = col + step[1], col - step[1]
        return (turns_column(step) & (ahead >= 0) & (ahead < cols)) | (
            turns_row(step) & (behind >= 0) & (behind < cols)
        )

    def onward_copy(at, slots):
        step = DIRS[at]
        return pltpu.make_async_remote_copy(
            src_ref=relay.at[at, slots], dst_ref=arrived.at[at, slots],
            send_sem=onward_send.at[at], recv_sem=recv_sem.at[at],
            device_id=(
                row + jnp.where(turns_row(step), step[0], 0),
                col + jnp.where(turns_column(step), step[1], 0),
            ),
            device_id_type=MESH,
        )

    detours = (
        (DIRS.index((0, 1)), 1, trails & (plane < planes - 1), DETOUR * (plane + 1)),
        (DIRS.index((0, -1)), -1, leads & (plane > 0), DETOUR * (planes - plane)),
    )
    passes = (
        (DIRS.index((0, 1)), 1, trails, plane),
        (DIRS.index((0, -1)), -1, leads, planes - 1 - plane),
    )

    def detour_copy(at, way, slots):
        return pltpu.make_async_remote_copy(
            src_ref=outgoing.at[at, slots], dst_ref=detour.at[slots],
            send_sem=send_sem.at[at], recv_sem=detour_recv,
            device_id=(row, col + way * PLANE), device_id_type=MESH,
        )

    def rejoin_copy(at, way, slots):
        return pltpu.make_async_remote_copy(
            src_ref=detour.at[slots], dst_ref=arrived.at[at, slots],
            send_sem=detour_send, recv_sem=recv_sem.at[at],
            device_id=(row, col - way * (PLANE - 1)), device_id_type=MESH,
        )

    def send_pieces(slot, piece_of, relayed):
        for at, step in enumerate(DIRS):
            outgoing[at, slot] = held[piece_of(bucket_of(step))]
            direct = exists(step)
            if relayed and at < DIAGONALS:
                turned = column_first(step) | row_first(step)

                @pl.when(direct & turned)
                def _():
                    relay_copy(at, pl.ds(slot, 1)).start()
                direct = direct & jnp.logical_not(turned)
            for detour_at, way, here, slots in detours:
                if at == detour_at:
                    around = here & (slot < slots)

                    @pl.when(around)
                    def _():
                        detour_copy(at, way, pl.ds(slot, 1)).start()
                    direct = direct & jnp.logical_not(around)

            @pl.when(direct)
            def _():
                bucket_copy(at, pl.ds(slot, 1)).start()
        arrived[len(DIRS), slot] = held[piece_of(OWN)]

    def send_slot(relayed, slot, carry):
        send_pieces(slot, lambda bucket: table_scalar[bucket, slot] & (own - 1), relayed)
        return carry

    loads[2].wait()
    bucket_id = lax.broadcasted_iota(jnp.int32, (16, own), 0)
    target = jnp.full((16, own), -1, jnp.int32)
    for bucket in range(9):
        tile = (row + bucket // 3 - 1) * cols + col + bucket % 3 - 1
        target = jnp.where(bucket_id == bucket, tile, target)
    belongs = target == jnp.broadcast_to(owner_row[...], (16, own))
    number = lax.broadcasted_iota(jnp.int32, (16, own), 1).astype(jnp.float32)
    leader = [
        jnp.min(jnp.where(belongs & (bucket_id == bucket), number, own - 1.0)).astype(jnp.int32)
        & (own - 1)
        for bucket in range(9)
    ]
    tall_group = 3 - jnp.where(row == 0, 1, 0) - jnp.where(row == rows - 1, 1, 0)
    wide_group = 3 - jnp.where(col == 0, 1, 0) - jnp.where(col == cols - 1, 1, 0)
    mates = 3 - jnp.where(plane == 0, 1, 0) - jnp.where(plane == planes - 1, 1, 0)
    mates = jnp.where(leads | trails, mates, 0)
    pl.semaphore_wait(barrier, tall_group * wide_group - 1 + mates)
    loads[4].wait()
    send_pieces(0, lambda bucket: leader[bucket], True)

    loads[3].wait()
    earlier = (
        lax.broadcasted_iota(jnp.int32, (own, own), 0)
        < lax.broadcasted_iota(jnp.int32, (own, own), 1)
    )
    place = jnp.dot(
        jnp.where(belongs, 1.0, 0.0), jnp.where(earlier, 1.0, 0.0),
        preferred_element_type=jnp.float32,
    )
    code = lax.broadcasted_iota(jnp.int32, (16, own), 1) + own * (
        jnp.broadcast_to(offset_row[...], (16, own)) + 1
    )
    code = jnp.where(belongs, code.astype(jnp.float32), 0.0)
    slot_lane = lax.broadcasted_iota(jnp.int32, (16, LANES), 1)
    filled = jnp.zeros((16, LANES), jnp.float32)
    for slot in range(CAP):
        picked = jnp.sum(jnp.where(place == slot, code, 0.0), axis=1, keepdims=True)
        filled = jnp.where(slot_lane == slot, picked, filled)
    filled = filled.astype(jnp.int32)
    table[...] = filled
    for bucket in range(9):
        rows_out[bucket] = filled[bucket : bucket + 1]
    to_scalar = pltpu.make_async_copy(table, table_scalar, table_sem)
    to_scalar.start()

    loads[0].wait()
    loads[1].wait()
    pack_strip(0, side, LANES - HALO)
    pack_strip(1, LANES, 0)
    for at, step in enumerate(DIRS):
        @pl.when(exists(step))
        def _():
            rim_copy(at).start()
            label_copy(at).start()
    to_scalar.wait()
    lax.fori_loop(1, 4, functools.partial(send_slot, True), 0)
    for load in loads[5:]:
        load.start()
    lax.fori_loop(4, RELAYED, functools.partial(send_slot, True), 0)
    lax.fori_loop(RELAYED, EARLY, functools.partial(send_slot, False), 0)

    loads[8].wait()
    lane = lax.broadcasted_iota(jnp.int32, (8, side), 1)
    u = ((col * side + lane).astype(jnp.float32) + 0.5) * (2.0 / (side * cols)) - 1.0
    for basis in range(BASES):
        for power_v in range(DEGREE + 1):
            total = jnp.zeros_like(u)
            for power_u in reversed(range(DEGREE + 1 - power_v)):
                total = total * u + coef[basis, term_powers.index((power_u, power_v))]
            inner[basis, power_v] = total

    for load in loads[5:8]:
        load.wait()
    wide = padded.shape[1]

    @pl.when(row == 0)
    def _():
        padded[pl.ds(0, HALO)] = jnp.zeros((HALO, wide), jnp.bfloat16)

    @pl.when(row == rows - 1)
    def _():
        padded[pl.ds(side + HALO, HALO)] = jnp.zeros((HALO, wide), jnp.bfloat16)

    @pl.when(col == 0)
    def _():
        padded[:, pl.ds(0, LANES)] = jnp.zeros((padded.shape[0], LANES), jnp.bfloat16)

    @pl.when(col == cols - 1)
    def _():
        padded[:, pl.ds(side + LANES, LANES)] = jnp.zeros((padded.shape[0], LANES), jnp.bfloat16)

    for at, step in enumerate(DIRS):
        @pl.when(exists(opposite(step)))
        def _():
            rim_copy(at).wait_recv()

    def unpack_strip(strip, first_col, first_lane):
        packed = strip_in[strip].astype(jnp.float32)
        for group in range(side // LANES):
            moved = pltpu.roll(packed, (first_lane - group * HALO) % LANES, 1)
            padded[pl.ds(HALO + group * LANES, LANES), pl.ds(first_col, LANES)] = moved.astype(jnp.bfloat16)

    @pl.when(col > 0)
    def _():
        unpack_strip(0, 0, LANES - HALO)

    @pl.when(col < cols - 1)
    def _():
        unpack_strip(1, side + LANES, 0)

    tall = padded.shape[0]
    chunk = tall // 3
    blocks = side // LANES
    for basis in range(BASES):
        across[basis, pl.ds(tall, across.shape[1] - tall)] = jnp.zeros(
            (across.shape[1] - tall, side), jnp.bfloat16
        )

    def row_pass(block, carry):
        first = pl.multiple_of(block * LANES, LANES)
        for part in range(3):
            got = jnp.dot(
                padded[pl.ds(part * chunk, chunk), pl.ds(first, 3 * LANES)],
                row_band[...],
                preferred_element_type=jnp.float32,
            )
            for basis in range(BASES):
                across[basis, pl.ds(part * chunk, chunk), pl.ds(first, LANES)] = got[
                    :, basis * LANES : (basis + 1) * LANES
                ].astype(jnp.bfloat16)
        return carry

    lax.fori_loop(0, blocks, row_pass, 0)

    part_cols = 2 * LANES

    def column_pass(block, carry):
        first = pl.multiple_of(block * LANES, LANES)
        line = lax.broadcasted_iota(jnp.int32, (LANES, part_cols), 0)
        v = ((row * side + first + line).astype(jnp.float32) + 0.5) * (2.0 / (side * rows)) - 1.0
        for part in range(side // part_cols):
            columns = pl.ds(part * part_cols, part_cols)
            total = jnp.zeros((LANES, part_cols), jnp.float32)
            for basis in range(BASES):
                smoothed = jnp.dot(
                    down_band[basis],
                    across[basis, pl.ds(first, 2 * LANES), columns],
                    preferred_element_type=jnp.float32,
                )
                weight = jnp.broadcast_to(inner[basis, DEGREE, 0:1, columns], total.shape)
                for power_v in reversed(range(DEGREE)):
                    weight = weight * v + inner[basis, power_v, 0:1, columns]
                total = total - weight * smoothed
            matched[pl.ds(first, LANES), columns] = total
        return carry

    lax.fori_loop(0, blocks, column_pass, 0)

    for at in range(DIAGONALS):
        @pl.when(turns(DIRS[at]))
        def _():
            relay_copy(at, pl.ds(0, RELAYED)).wait_recv()

            def pass_on(slot, carry):
                onward_copy(at, pl.ds(slot, 1)).start()
                return carry

            lax.fori_loop(0, RELAYED, pass_on, 0)
    for at, way, here, share_of in passes:
        for thirds in range(1, planes):
            @pl.when(here & (share_of == thirds))
            def _():
                detour_copy(at, way, pl.ds(0, DETOUR * thirds)).wait_recv()

                def rejoin(slot, carry):
                    rejoin_copy(at, way, pl.ds(slot, 1)).start()
                    return carry

                lax.fori_loop(0, DETOUR * thirds, rejoin, 0)
    lax.fori_loop(EARLY, CAP, functools.partial(send_slot, False), 0)

    for at, step in enumerate(DIRS):
        tags[pl.ds(at, 1)] = jnp.zeros((1, LANES), jnp.int32)

        @pl.when(exists(opposite(step)))
        def _():
            label_copy(at).wait_recv()
            tags[pl.ds(at, 1)] = arrived_table[at]
    tags[pl.ds(len(DIRS), 1)] = table[pl.ds(OWN, 1)]
    sort_plan(own, side // LANES, tags, plan, share)
    plan_copies = [
        pltpu.make_async_copy(plan, plan_scalar, load_sem.at[0]),
        pltpu.make_async_copy(share, share_scalar, load_sem.at[1]),
    ]
    for plan_copy in plan_copies:
        plan_copy.start()

    for at in range(DIAGONALS):
        @pl.when(turns(DIRS[at]))
        def _():
            onward_copy(at, pl.ds(0, RELAYED)).wait_send()
    for at, way, here, share_of in passes:
        for thirds in range(1, planes):
            @pl.when(here & (share_of == thirds))
            def _():
                rejoin_copy(at, way, pl.ds(0, DETOUR * thirds)).wait_send()
    for at, step in enumerate(DIRS):
        @pl.when(exists(step))
        def _():
            rim_copy(at).wait_send()
            label_copy(at).wait_send()
            bucket_copy(at).wait_send()

        @pl.when(exists(opposite(step)))
        def _():
            bucket_copy(at).wait_recv()
    for plan_copy in plan_copies:
        plan_copy.wait()


def join_kernel(plan, share, arrived, matched, out, total, out_sem):
    side = out.shape[1]
    per_row = side // LANES

    def row_lines(block_row):
        return pl.ds(pl.multiple_of(block_row * LANES, LANES), LANES)

    def out_copy(block_row):
        lines = row_lines(block_row)
        return pltpu.make_async_copy(total.at[lines], out.at[lines], out_sem.at[block_row])

    def join_row(block_row, start):
        end = plan[3, block_row]
        lines = row_lines(block_row)

        def add(at, carry):
            slot = plan[0, at]
            column = pl.multiple_of((plan[1, at] - block_row * per_row) * LANES, LANES)
            columns = pl.ds(column, LANES)
            piece = arrived[lax.div(slot, CAP), slot & (CAP - 1)].astype(jnp.float32)
            total[lines, columns] = total[lines, columns] + share[2, at] * piece
            return carry

        lax.fori_loop(start, end, add, 0)
        out_copy(block_row).start()
        return end

    lax.fori_loop(0, per_row, join_row, 0)
    for block_row in range(per_row):
        out_copy(block_row).wait()


def on_device(pieces, owner_map, offsets, template, coefficients):
    own, block_side = pieces.shape[0], pieces.shape[1]
    side = template.shape[0]
    smem = pl.BlockSpec(memory_space=pltpu.SMEM)
    vmem = pl.BlockSpec(memory_space=pltpu.VMEM)
    hbm = pl.BlockSpec(memory_space=pltpu.HBM)
    count = len(DIRS)

    band_across, band_down = band_tables()
    tall = side + 2 * HALO
    dma = pltpu.SemaphoreType.DMA
    arrived, plan, share, matched = pl.pallas_call(
        send_kernel,
        out_shape=[
            jax.ShapeDtypeStruct((count + 1, CAP, block_side, block_side), jnp.bfloat16),
            pltpu.SMEM((8, 2 * LANES), jnp.int32),
            pltpu.SMEM((8, 2 * LANES), jnp.float32),
            jax.ShapeDtypeStruct((side, side), jnp.float32),
        ],
        in_specs=[hbm] * 7,
        out_specs=[vmem, smem, smem, vmem],
        scratch_shapes=[
            pltpu.VMEM((8, 2 * LANES), jnp.int32),
            pltpu.VMEM((8, 2 * LANES), jnp.float32),
            pltpu.VMEM((own, block_side, block_side), jnp.bfloat16),
            pltpu.SMEM(coefficients.shape, jnp.float32),
            pltpu.VMEM((1, own), jnp.int32),
            pltpu.VMEM((1, own), jnp.int32),
            pltpu.VMEM((16, LANES), jnp.int32),
            pltpu.VMEM((9, 1, LANES), jnp.int32),
            pltpu.SMEM((16, LANES), jnp.int32),
            pltpu.VMEM((count, 1, LANES), jnp.int32),
            pltpu.VMEM((16, LANES), jnp.int32),
            pltpu.VMEM((count, CAP, block_side, block_side), jnp.bfloat16),
            pltpu.VMEM((tall, side + 2 * LANES), jnp.bfloat16),
            pltpu.VMEM((2, LANES, LANES), jnp.bfloat16),
            pltpu.VMEM((2, LANES, LANES), jnp.bfloat16),
            pltpu.VMEM((BASES, side + LANES, side), jnp.bfloat16),
            pltpu.VMEM((BASES, DEGREE + 1, 8, side), jnp.float32),
            pltpu.VMEM(band_across.shape, jnp.bfloat16),
            pltpu.VMEM(band_down.shape, jnp.bfloat16),
            pltpu.VMEM((DIAGONALS, RELAYED, block_side, block_side), jnp.bfloat16),
            dma((9,)), dma, dma((count,)), dma((count,)), dma((count,)), dma((count,)),
            dma((count,)), dma((count,)), dma((DIAGONALS,)), dma((DIAGONALS,)),
            pltpu.VMEM((3 * DETOUR, block_side, block_side), jnp.bfloat16), dma, dma,
        ],
        compiler_params=pltpu.CompilerParams(
            collective_id=0, has_side_effects=True, vmem_limit_bytes=40 << 20
        ),
        name="send",
    )(
        *(
            pltpu.with_memory_space_constraint(array, pltpu.HBM)
            for array in (
                owner_map.reshape(1, own), offsets.reshape(1, own), coefficients, pieces,
                template, jnp.asarray(band_across), jnp.asarray(band_down),
            )
        )
    )
    joined, _ = pl.pallas_call(
        join_kernel,
        out_shape=[jax.ShapeDtypeStruct((side, side), jnp.float32)] * 2,
        in_specs=[smem, smem, vmem, vmem],
        out_specs=[hbm, vmem],
        input_output_aliases={3: 1},
        scratch_shapes=[dma((side // block_side,))],
        compiler_params=pltpu.CompilerParams(vmem_limit_bytes=32 << 20),
        name="join",
    )(plan, share, arrived, matched)
    return joined


def solution(mesh):
    in_specs = (P(("py", "px"), None, None), P(("py", "px")), P(("py", "px")), P("py", "px"), P())
    out_specs = P("py", "px")
    return jax.shard_map(
        on_device, mesh=mesh, in_specs=in_specs, out_specs=out_specs, check_vma=False
    )
```

```python
import functools

import jax
import jax.numpy as jnp
import numpy as np
from jax import lax
from jax.experimental import pallas as pl
from jax.experimental.pallas import tpu as pltpu
from jax.sharding import PartitionSpec as P

HALO = 16
CAP = 16
LANES = 128
BASES = 3
DEGREE = 4

sigma_fractions = (0.09375, 0.1875, 0.375)
term_powers = [(degree - power_v, power_v) for degree in range(5) for power_v in range(degree + 1)]

DIRS = ((1, 1), (-1, -1), (1, -1), (-1, 1), (0, 1), (0, -1), (1, 0), (-1, 0))
DIAGONALS = 4
RELAYED = 8
PLANE = 4
DETOUR = 3
EARLY = 14
OWN = 4
MESH = pl.DeviceIdType.MESH


def bucket_of(step):
    return 3 * (step[0] + 1) + step[1] + 1


def gauss_taps():
    positions = np.arange(-HALO, HALO + 1).astype(np.float32)
    stacked = []
    for fraction in sigma_fractions:
        sigma = fraction * HALO
        values = np.exp(-positions * positions / np.float32(2.0 * sigma * sigma))
        stacked.append(values / np.sum(values))
    return np.stack(stacked).astype(jnp.bfloat16)


def band_tables():
    taps = gauss_taps()
    across = np.zeros((3 * LANES, BASES * LANES), taps.dtype)
    down = np.zeros((BASES, LANES, 2 * LANES), taps.dtype)
    for basis in range(BASES):
        for out in range(LANES):
            for tap in range(2 * HALO + 1):
                across[LANES - HALO + out + tap, basis * LANES + out] = taps[basis, tap]
                down[basis, out, out + tap] = taps[basis, tap]
    return across, down


def sort_plan(own, per_row, tags, plan, share):
    count = len(DIRS)
    blocks = per_row * per_row
    shape = (blocks, LANES)
    code = tags[...]
    block_tag = lax.shift_right_logical(code, own.bit_length() - 1).astype(jnp.float32)
    spread = jnp.zeros((8, LANES), jnp.float32)
    for at in range(count):
        one = jnp.broadcast_to(block_tag[at : at + 1], (8, LANES))
        spread = spread + pltpu.roll(one, at * CAP, 1)
    groups = (spread[0:1], block_tag[count : count + 1])

    block_id = lax.broadcasted_iota(jnp.int32, shape, 0).astype(jnp.float32)
    before = jnp.where(
        lax.broadcasted_iota(jnp.int32, (LANES, LANES), 0)
        < lax.broadcasted_iota(jnp.int32, (LANES, LANES), 1), 1.0, 0.0,
    )
    lower = jnp.where(
        lax.broadcasted_iota(jnp.int32, (blocks, blocks), 1)
        < lax.broadcasted_iota(jnp.int32, (blocks, blocks), 0), 1.0, 0.0,
    )
    hits = [jnp.where(jnp.broadcast_to(tag, shape) == block_id + 1, 1.0, 0.0) for tag in groups]
    sums = [jnp.broadcast_to(jnp.sum(hit, axis=1, keepdims=True), shape) for hit in hits]
    covered = sums[0] + sums[1]
    first = jnp.dot(lower, covered, preferred_element_type=jnp.float32)
    ahead = (first, first + sums[0])

    line = lax.broadcasted_iota(jnp.int32, (8, LANES), 0)
    lane = lax.broadcasted_iota(jnp.int32, (8, LANES), 1).astype(jnp.float32)
    target = lax.broadcasted_iota(jnp.int32, (2 * LANES, LANES), 0).astype(jnp.float32)
    over_lanes = (((1,), (1,)), ((), ()))
    listed = jnp.zeros((8, 2 * LANES), jnp.float32)
    ends = jnp.zeros((8, 2 * LANES), jnp.float32)
    for group in range(2):
        hit, tag = hits[group], groups[group]
        rank = ahead[group] + jnp.dot(hit, before, preferred_element_type=jnp.float32)
        place = jnp.sum(hit * rank, axis=0, keepdims=True)
        shares = jnp.sum(hit * covered, axis=0, keepdims=True)
        place = jnp.where(tag > 0, place, -1.0)
        chosen = jnp.where(jnp.broadcast_to(place, target.shape) == target, 1.0, 0.0)
        values = jnp.where(line == 0, lane + group * LANES, 0.0)
        values = jnp.where(line == 1, jnp.broadcast_to(tag - 1, values.shape), values)
        values = jnp.where(line == 2, jnp.broadcast_to(shares, values.shape), values)
        listed = listed + lax.dot_general(
            values, chosen, over_lanes, preferred_element_type=jnp.float32
        )
        wide_tag = jnp.broadcast_to(tag, target.shape)
        inside = jnp.where((wide_tag > 0) & (wide_tag <= (target + 1) * per_row), 1.0, 0.0)
        ends = ends + lax.dot_general(
            jnp.ones((8, LANES), jnp.float32), inside, over_lanes,
            preferred_element_type=jnp.float32,
        )
    wide_line = lax.broadcasted_iota(jnp.int32, listed.shape, 0)
    plan[...] = jnp.where(wide_line == 3, ends, listed).astype(jnp.int32)
    share[...] = 1.0 / jnp.maximum(listed, 1.0)


def send_kernel(
    owner, offset, coef_hbm, pieces, template, band_across, band_down,
    arrived, plan_scalar, share_scalar, matched,
    plan, share,
    held, coef, owner_row, offset_row, table, rows_out, table_scalar, arrived_table,
    tags, outgoing, padded, strip_out, strip_in, across, inner, row_band, down_band,
    relay, load_sem, table_sem, send_sem, recv_sem, label_send, label_recv, rim_send, rim_recv,
    relay_recv, onward_send, detour, detour_recv, detour_send,
):
    rows, cols = lax.axis_size("py"), lax.axis_size("px")
    row, col = lax.axis_index("py"), lax.axis_index("px")
    side = template.shape[0]
    last = side - LANES
    own = held.shape[0]

    def exists(step):
        r, c = row + step[0], col + step[1]
        return (r >= 0) & (r < rows) & (c >= 0) & (c < cols)

    def neighbour(step):
        return (row + step[0], col + step[1])

    plane = lax.div(col, PLANE)
    planes = cols // PLANE
    leads = col - plane * PLANE == 0
    trails = col - plane * PLANE == PLANE - 1

    barrier = pltpu.get_barrier_semaphore()
    for step in DIRS:
        @pl.when(exists(step))
        def _():
            pl.semaphore_signal(barrier, inc=1, device_id=neighbour(step), device_id_type=MESH)

    for far, there in (
        (PLANE - 1, leads),
        (1 - PLANE, trails),
        (PLANE, (leads | trails) & (plane < planes - 1)),
        (-PLANE, (leads | trails) & (plane > 0)),
    ):
        @pl.when(there)
        def _():
            pl.semaphore_signal(
                barrier, inc=1, device_id=(row, col + far), device_id_type=MESH
            )

    body = padded.at[pl.ds(HALO, side)]
    loads = [
        pltpu.make_async_copy(
            template.at[:, pl.ds(0, LANES)], body.at[:, pl.ds(LANES, LANES)], load_sem.at[0]
        ),
        pltpu.make_async_copy(
            template.at[:, pl.ds(last, LANES)], body.at[:, pl.ds(side, LANES)], load_sem.at[1]
        ),
        pltpu.make_async_copy(owner, owner_row, load_sem.at[2]),
        pltpu.make_async_copy(offset, offset_row, load_sem.at[3]),
        pltpu.make_async_copy(pieces, held, load_sem.at[4]),
        pltpu.make_async_copy(
            template.at[:, pl.ds(LANES, side - 2 * LANES)],
            body.at[:, pl.ds(2 * LANES, side - 2 * LANES)],
            load_sem.at[5],
        ),
        pltpu.make_async_copy(band_across, row_band, load_sem.at[6]),
        pltpu.make_async_copy(band_down, down_band, load_sem.at[7]),
        pltpu.make_async_copy(coef_hbm, coef, load_sem.at[8]),
    ]
    for load in (loads[2], loads[4], loads[3], loads[0], loads[1]):
        load.start()

    def opposite(step):
        return (-step[0], -step[1])

    def rim_copy(at):
        step = DIRS[at]
        if step[0] == 0:
            source = strip_out.at[0 if step[1] > 0 else 1]
            target = strip_in.at[0 if step[1] > 0 else 1]
        else:
            source_rows = pl.ds(side - HALO if step[0] > 0 else 0, HALO)
            target_rows = pl.ds(0 if step[0] > 0 else side + HALO, HALO)
            if step[1] == 0:
                source = template.at[source_rows]
                target = padded.at[target_rows, pl.ds(LANES, side)]
            else:
                source = template.at[source_rows, pl.ds(last if step[1] > 0 else 0, LANES)]
                target = padded.at[target_rows, pl.ds(0 if step[1] > 0 else side + LANES, LANES)]
        return pltpu.make_async_remote_copy(
            src_ref=source, dst_ref=target, send_sem=rim_send.at[at], recv_sem=rim_recv.at[at],
            device_id=neighbour(step), device_id_type=MESH,
        )

    def label_copy(at):
        return pltpu.make_async_remote_copy(
            src_ref=rows_out.at[bucket_of(DIRS[at])], dst_ref=arrived_table.at[at], send_sem=label_send.at[at],
            recv_sem=label_recv.at[at], device_id=neighbour(DIRS[at]), device_id_type=MESH,
        )

    def bucket_copy(at, slots=pl.ds(0, CAP)):
        return pltpu.make_async_remote_copy(
            src_ref=outgoing.at[at, slots], dst_ref=arrived.at[at, slots], send_sem=send_sem.at[at],
            recv_sem=recv_sem.at[at], device_id=neighbour(DIRS[at]), device_id_type=MESH,
        )

    def pack_strip(strip, first_col, first_lane):
        lane_group = lax.broadcasted_iota(jnp.int32, (LANES, LANES), 1) // HALO
        packed = jnp.zeros((LANES, LANES), jnp.float32)
        for group in range(side // LANES):
            block = padded[pl.ds(HALO + group * LANES, LANES), pl.ds(first_col, LANES)]
            moved = pltpu.roll(
                block.astype(jnp.float32), (group * HALO - first_lane) % LANES, 1
            )
            packed = jnp.where(lane_group == group, moved, packed)
        strip_out[strip] = packed.astype(jnp.bfloat16)

    def column_first(step):
        return row == (2 if step[0] < 0 else rows - 3)

    def row_first(step):
        return row == (1 if step[0] > 0 else rows - 2)

    def relay_copy(at, slots):
        step = DIRS[at]
        return pltpu.make_async_remote_copy(
            src_ref=outgoing.at[at, slots], dst_ref=relay.at[at, slots],
            send_sem=send_sem.at[at], recv_sem=relay_recv.at[at],
            device_id=(
                row + jnp.where(row_first(step), 0, step[0]),
                col + jnp.where(column_first(step), 0, step[1]),
            ),
            device_id_type=MESH,
        )

    def turns_column(step):
        return row == (1 if step[0] < 0 else rows - 2)

    def turns_row(step):
        return row == (1 if step[0] > 0 else rows - 2)

    def turns(step):
        ahead, behind = col + step[1], col - step[1]
        return (turns_column(step) & (ahead >= 0) & (ahead < cols)) | (
            turns_row(step) & (behind >= 0) & (behind < cols)
        )

    def onward_copy(at, slots):
        step = DIRS[at]
        return pltpu.make_async_remote_copy(
            src_ref=relay.at[at, slots], dst_ref=arrived.at[at, slots],
            send_sem=onward_send.at[at], recv_sem=recv_sem.at[at],
            device_id=(
                row + jnp.where(turns_row(step), step[0], 0),
                col + jnp.where(turns_column(step), step[1], 0),
            ),
            device_id_type=MESH,
        )

    detours = (
        (DIRS.index((0, 1)), 1, trails & (plane < planes - 1), DETOUR * (plane + 1)),
        (DIRS.index((0, -1)), -1, leads & (plane > 0), DETOUR * (planes - plane)),
    )
    passes = (
        (DIRS.index((0, 1)), 1, trails, plane),
        (DIRS.index((0, -1)), -1, leads, planes - 1 - plane),
    )

    def detour_copy(at, way, slots):
        return pltpu.make_async_remote_copy(
            src_ref=outgoing.at[at, slots], dst_ref=detour.at[slots],
            send_sem=send_sem.at[at], recv_sem=detour_recv,
            device_id=(row, col + way * PLANE), device_id_type=MESH,
        )

    def rejoin_copy(at, way, slots):
        return pltpu.make_async_remote_copy(
            src_ref=detour.at[slots], dst_ref=arrived.at[at, slots],
            send_sem=detour_send, recv_sem=recv_sem.at[at],
            device_id=(row, col - way * (PLANE - 1)), device_id_type=MESH,
        )

    def send_pieces(slot, piece_of, relayed):
        for at, step in enumerate(DIRS):
            outgoing[at, slot] = held[piece_of(bucket_of(step))]
            direct = exists(step)
            if relayed and at < DIAGONALS:
                turned = column_first(step) | row_first(step)

                @pl.when(direct & turned)
                def _():
                    relay_copy(at, pl.ds(slot, 1)).start()
                direct = direct & jnp.logical_not(turned)
            for detour_at, way, here, slots in detours:
                if at == detour_at:
                    around = here & (slot < slots)

                    @pl.when(around)
                    def _():
                        detour_copy(at, way, pl.ds(slot, 1)).start()
                    direct = direct & jnp.logical_not(around)

            @pl.when(direct)
            def _():
                bucket_copy(at, pl.ds(slot, 1)).start()
        arrived[len(DIRS), slot] = held[piece_of(OWN)]

    def send_slot(relayed, slot, carry):
        send_pieces(slot, lambda bucket: table_scalar[bucket, slot] & (own - 1), relayed)
        return carry

    loads[2].wait()
    bucket_id = lax.broadcasted_iota(jnp.int32, (16, own), 0)
    target = jnp.full((16, own), -1, jnp.int32)
    for bucket in range(9):
        tile = (row + bucket // 3 - 1) * cols + col + bucket % 3 - 1
        target = jnp.where(bucket_id == bucket, tile, target)
    belongs = target == jnp.broadcast_to(owner_row[...], (16, own))
    number = lax.broadcasted_iota(jnp.int32, (16, own), 1).astype(jnp.float32)
    leader = [
        jnp.min(jnp.where(belongs & (bucket_id == bucket), number, own - 1.0)).astype(jnp.int32)
        & (own - 1)
        for bucket in range(9)
    ]
    tall_group = 3 - jnp.where(row == 0, 1, 0) - jnp.where(row == rows - 1, 1, 0)
    wide_group = 3 - jnp.where(col == 0, 1, 0) - jnp.where(col == cols - 1, 1, 0)
    mates = 3 - jnp.where(plane == 0, 1, 0) - jnp.where(plane == planes - 1, 1, 0)
    mates = jnp.where(leads | trails, mates, 0)
    pl.semaphore_wait(barrier, tall_group * wide_group - 1 + mates)
    loads[4].wait()
    send_pieces(0, lambda bucket: leader[bucket], True)

    loads[3].wait()
    earlier = (
        lax.broadcasted_iota(jnp.int32, (own, own), 0)
        < lax.broadcasted_iota(jnp.int32, (own, own), 1)
    )
    place = jnp.dot(
        jnp.where(belongs, 1.0, 0.0), jnp.where(earlier, 1.0, 0.0),
        preferred_element_type=jnp.float32,
    )
    code = lax.broadcasted_iota(jnp.int32, (16, own), 1) + own * (
        jnp.broadcast_to(offset_row[...], (16, own)) + 1
    )
    code = jnp.where(belongs, code.astype(jnp.float32), 0.0)
    slot_lane = lax.broadcasted_iota(jnp.int32, (16, LANES), 1)
    filled = jnp.zeros((16, LANES), jnp.float32)
    for slot in range(CAP):
        picked = jnp.sum(jnp.where(place == slot, code, 0.0), axis=1, keepdims=True)
        filled = jnp.where(slot_lane == slot, picked, filled)
    filled = filled.astype(jnp.int32)
    table[...] = filled
    for bucket in range(9):
        rows_out[bucket] = filled[bucket : bucket + 1]
    to_scalar = pltpu.make_async_copy(table, table_scalar, table_sem)
    to_scalar.start()

    loads[0].wait()
    loads[1].wait()
    pack_strip(0, side, LANES - HALO)
    pack_strip(1, LANES, 0)
    for at, step in enumerate(DIRS):
        @pl.when(exists(step))
        def _():
            rim_copy(at).start()
            label_copy(at).start()
    to_scalar.wait()
    lax.fori_loop(1, 4, functools.partial(send_slot, True), 0)
    for load in loads[5:]:
        load.start()
    lax.fori_loop(4, RELAYED, functools.partial(send_slot, True), 0)
    lax.fori_loop(RELAYED, EARLY, functools.partial(send_slot, False), 0)

    loads[8].wait()
    lane = lax.broadcasted_iota(jnp.int32, (8, side), 1)
    u = ((col * side + lane).astype(jnp.float32) + 0.5) * (2.0 / (side * cols)) - 1.0
    for basis in range(BASES):
        for power_v in range(DEGREE + 1):
            total = jnp.zeros_like(u)
            for power_u in reversed(range(DEGREE + 1 - power_v)):
                total = total * u + coef[basis, term_powers.index((power_u, power_v))]
            inner[basis, power_v] = total

    for load in loads[5:8]:
        load.wait()
    wide = padded.shape[1]

    @pl.when(row == 0)
    def _():
        padded[pl.ds(0, HALO)] = jnp.zeros((HALO, wide), jnp.bfloat16)

    @pl.when(row == rows - 1)
    def _():
        padded[pl.ds(side + HALO, HALO)] = jnp.zeros((HALO, wide), jnp.bfloat16)

    @pl.when(col == 0)
    def _():
        padded[:, pl.ds(0, LANES)] = jnp.zeros((padded.shape[0], LANES), jnp.bfloat16)

    @pl.when(col == cols - 1)
    def _():
        padded[:, pl.ds(side + LANES, LANES)] = jnp.zeros((padded.shape[0], LANES), jnp.bfloat16)

    for at, step in enumerate(DIRS):
        @pl.when(exists(opposite(step)))
        def _():
            rim_copy(at).wait_recv()

    def unpack_strip(strip, first_col, first_lane):
        packed = strip_in[strip].astype(jnp.float32)
        for group in range(side // LANES):
            moved = pltpu.roll(packed, (first_lane - group * HALO) % LANES, 1)
            padded[pl.ds(HALO + group * LANES, LANES), pl.ds(first_col, LANES)] = moved.astype(jnp.bfloat16)

    @pl.when(col > 0)
    def _():
        unpack_strip(0, 0, LANES - HALO)

    @pl.when(col < cols - 1)
    def _():
        unpack_strip(1, side + LANES, 0)

    tall = padded.shape[0]
    chunk = tall // 3
    blocks = side // LANES
    for basis in range(BASES):
        across[basis, pl.ds(tall, across.shape[1] - tall)] = jnp.zeros(
            (across.shape[1] - tall, side), jnp.bfloat16
        )

    def row_pass(block, carry):
        first = pl.multiple_of(block * LANES, LANES)
        for part in range(3):
            got = jnp.dot(
                padded[pl.ds(part * chunk, chunk), pl.ds(first, 3 * LANES)],
                row_band[...],
                preferred_element_type=jnp.float32,
            )
            for basis in range(BASES):
                across[basis, pl.ds(part * chunk, chunk), pl.ds(first, LANES)] = got[
                    :, basis * LANES : (basis + 1) * LANES
                ].astype(jnp.bfloat16)
        return carry

    lax.fori_loop(0, blocks, row_pass, 0)

    part_cols = 2 * LANES

    def column_pass(block, carry):
        first = pl.multiple_of(block * LANES, LANES)
        line = lax.broadcasted_iota(jnp.int32, (LANES, part_cols), 0)
        v = ((row * side + first + line).astype(jnp.float32) + 0.5) * (2.0 / (side * rows)) - 1.0
        for part in range(side // part_cols):
            columns = pl.ds(part * part_cols, part_cols)
            total = jnp.zeros((LANES, part_cols), jnp.float32)
            for basis in range(BASES):
                smoothed = jnp.dot(
                    down_band[basis],
                    across[basis, pl.ds(first, 2 * LANES), columns],
                    preferred_element_type=jnp.float32,
                )
                weight = jnp.broadcast_to(inner[basis, DEGREE, 0:1, columns], total.shape)
                for power_v in reversed(range(DEGREE)):
                    weight = weight * v + inner[basis, power_v, 0:1, columns]
                total = total - weight * smoothed
            matched[pl.ds(first, LANES), columns] = total
        return carry

    lax.fori_loop(0, blocks, column_pass, 0)

    for at in range(DIAGONALS):
        @pl.when(turns(DIRS[at]))
        def _():
            relay_copy(at, pl.ds(0, RELAYED)).wait_recv()

            def pass_on(slot, carry):
                onward_copy(at, pl.ds(slot, 1)).start()
                return carry

            lax.fori_loop(0, RELAYED, pass_on, 0)
    for at, way, here, share_of in passes:
        for thirds in range(1, planes):
            @pl.when(here & (share_of == thirds))
            def _():
                detour_copy(at, way, pl.ds(0, DETOUR * thirds)).wait_recv()

                def rejoin(slot, carry):
                    rejoin_copy(at, way, pl.ds(slot, 1)).start()
                    return carry

                lax.fori_loop(0, DETOUR * thirds, rejoin, 0)
    lax.fori_loop(EARLY, CAP, functools.partial(send_slot, False), 0)

    for at, step in enumerate(DIRS):
        tags[pl.ds(at, 1)] = jnp.zeros((1, LANES), jnp.int32)

        @pl.when(exists(opposite(step)))
        def _():
            label_copy(at).wait_recv()
            tags[pl.ds(at, 1)] = arrived_table[at]
    tags[pl.ds(len(DIRS), 1)] = table[pl.ds(OWN, 1)]
    sort_plan(own, side // LANES, tags, plan, share)
    plan_copies = [
        pltpu.make_async_copy(plan, plan_scalar, load_sem.at[0]),
        pltpu.make_async_copy(share, share_scalar, load_sem.at[1]),
    ]
    for plan_copy in plan_copies:
        plan_copy.start()

    for at in range(DIAGONALS):
        @pl.when(turns(DIRS[at]))
        def _():
            onward_copy(at, pl.ds(0, RELAYED)).wait_send()
    for at, way, here, share_of in passes:
        for thirds in range(1, planes):
            @pl.when(here & (share_of == thirds))
            def _():
                rejoin_copy(at, way, pl.ds(0, DETOUR * thirds)).wait_send()
    for at, step in enumerate(DIRS):
        @pl.when(exists(step))
        def _():
            rim_copy(at).wait_send()
            label_copy(at).wait_send()
            bucket_copy(at).wait_send()

        @pl.when(exists(opposite(step)))
        def _():
            bucket_copy(at).wait_recv()
    for plan_copy in plan_copies:
        plan_copy.wait()


def join_kernel(plan, share, arrived, matched, out, total, out_sem):
    side = out.shape[1]
    per_row = side // LANES

    def row_lines(block_row):
        return pl.ds(pl.multiple_of(block_row * LANES, LANES), LANES)

    def out_copy(block_row):
        lines = row_lines(block_row)
        return pltpu.make_async_copy(total.at[lines], out.at[lines], out_sem.at[block_row])

    def join_row(block_row, start):
        end = plan[3, block_row]
        lines = row_lines(block_row)

        def add(at, carry):
            slot = plan[0, at]
            column = pl.multiple_of((plan[1, at] - block_row * per_row) * LANES, LANES)
            columns = pl.ds(column, LANES)
            piece = arrived[lax.div(slot, CAP), slot & (CAP - 1)].astype(jnp.float32)
            total[lines, columns] = total[lines, columns] + share[2, at] * piece
            return carry

        lax.fori_loop(start, end, add, 0)
        out_copy(block_row).start()
        return end

    lax.fori_loop(0, per_row, join_row, 0)
    for block_row in range(per_row):
        out_copy(block_row).wait()


def on_device(pieces, owner_map, offsets, template, coefficients):
    own, block_side = pieces.shape[0], pieces.shape[1]
    side = template.shape[0]
    smem = pl.BlockSpec(memory_space=pltpu.SMEM)
    vmem = pl.BlockSpec(memory_space=pltpu.VMEM)
    hbm = pl.BlockSpec(memory_space=pltpu.HBM)
    count = len(DIRS)

    band_across, band_down = band_tables()
    tall = side + 2 * HALO
    dma = pltpu.SemaphoreType.DMA
    arrived, plan, share, matched = pl.pallas_call(
        send_kernel,
        out_shape=[
            jax.ShapeDtypeStruct((count + 1, CAP, block_side, block_side), jnp.bfloat16),
            pltpu.SMEM((8, 2 * LANES), jnp.int32),
            pltpu.SMEM((8, 2 * LANES), jnp.float32),
            jax.ShapeDtypeStruct((side, side), jnp.float32),
        ],
        in_specs=[hbm] * 7,
        out_specs=[vmem, smem, smem, vmem],
        scratch_shapes=[
            pltpu.VMEM((8, 2 * LANES), jnp.int32),
            pltpu.VMEM((8, 2 * LANES), jnp.float32),
            pltpu.VMEM((own, block_side, block_side), jnp.bfloat16),
            pltpu.SMEM(coefficients.shape, jnp.float32),
            pltpu.VMEM((1, own), jnp.int32),
            pltpu.VMEM((1, own), jnp.int32),
            pltpu.VMEM((16, LANES), jnp.int32),
            pltpu.VMEM((9, 1, LANES), jnp.int32),
            pltpu.SMEM((16, LANES), jnp.int32),
            pltpu.VMEM((count, 1, LANES), jnp.int32),
            pltpu.VMEM((16, LANES), jnp.int32),
            pltpu.VMEM((count, CAP, block_side, block_side), jnp.bfloat16),
            pltpu.VMEM((tall, side + 2 * LANES), jnp.bfloat16),
            pltpu.VMEM((2, LANES, LANES), jnp.bfloat16),
            pltpu.VMEM((2, LANES, LANES), jnp.bfloat16),
            pltpu.VMEM((BASES, side + LANES, side), jnp.bfloat16),
            pltpu.VMEM((BASES, DEGREE + 1, 8, side), jnp.float32),
            pltpu.VMEM(band_across.shape, jnp.bfloat16),
            pltpu.VMEM(band_down.shape, jnp.bfloat16),
            pltpu.VMEM((DIAGONALS, RELAYED, block_side, block_side), jnp.bfloat16),
            dma((9,)), dma, dma((count,)), dma((count,)), dma((count,)), dma((count,)),
            dma((count,)), dma((count,)), dma((DIAGONALS,)), dma((DIAGONALS,)),
            pltpu.VMEM((3 * DETOUR, block_side, block_side), jnp.bfloat16), dma, dma,
        ],
        compiler_params=pltpu.CompilerParams(
            collective_id=0, has_side_effects=True, vmem_limit_bytes=40 << 20
        ),
        name="send",
    )(
        *(
            pltpu.with_memory_space_constraint(array, pltpu.HBM)
            for array in (
                owner_map.reshape(1, own), offsets.reshape(1, own), coefficients, pieces,
                template, jnp.asarray(band_across), jnp.asarray(band_down),
            )
        )
    )
    joined, _ = pl.pallas_call(
        join_kernel,
        out_shape=[jax.ShapeDtypeStruct((side, side), jnp.float32)] * 2,
        in_specs=[smem, smem, vmem, vmem],
        out_specs=[hbm, vmem],
        input_output_aliases={3: 1},
        scratch_shapes=[dma((side // block_side,))],
        compiler_params=pltpu.CompilerParams(vmem_limit_bytes=32 << 20),
        name="join",
    )(plan, share, arrived, matched)
    return joined


def solution(mesh):
    in_specs = (P(("py", "px"), None, None), P(("py", "px")), P(("py", "px")), P("py", "px"), P())
    out_specs = P("py", "px")
    return jax.shard_map(
        on_device, mesh=mesh, in_specs=in_specs, out_specs=out_specs, check_vma=False
    )
```

```python
import functools

import jax
import jax.numpy as jnp
import numpy as np
from jax import lax
from jax.experimental import pallas as pl
from jax.experimental.pallas import tpu as pltpu
from jax.sharding import PartitionSpec as P

HALO = 16
CAP = 16
LANES = 128
BASES = 3
DEGREE = 4

sigma_fractions = (0.09375, 0.1875, 0.375)
term_powers = [(degree - power_v, power_v) for degree in range(5) for power_v in range(degree + 1)]

DIRS = ((1, 1), (-1, -1), (1, -1), (-1, 1), (0, 1), (0, -1), (1, 0), (-1, 0))
DIAGONALS = 4
RELAYED = 8
PLANE = 4
DETOUR = 3
EARLY = 14
OWN = 4
MESH = pl.DeviceIdType.MESH


def bucket_of(step):
    return 3 * (step[0] + 1) + step[1] + 1


def gauss_taps():
    positions = np.arange(-HALO, HALO + 1).astype(np.float32)
    stacked = []
    for fraction in sigma_fractions:
        sigma = fraction * HALO
        values = np.exp(-positions * positions / np.float32(2.0 * sigma * sigma))
        stacked.append(values / np.sum(values))
    return np.stack(stacked).astype(jnp.bfloat16)


def band_tables():
    taps = gauss_taps()
    across = np.zeros((3 * LANES, BASES * LANES), taps.dtype)
    down = np.zeros((BASES, LANES, 2 * LANES), taps.dtype)
    for basis in range(BASES):
        for out in range(LANES):
            for tap in range(2 * HALO + 1):
                across[LANES - HALO + out + tap, basis * LANES + out] = taps[basis, tap]
                down[basis, out, out + tap] = taps[basis, tap]
    return across, down


def sort_plan(own, per_row, tags, plan, share):
    count = len(DIRS)
    blocks = per_row * per_row
    shape = (blocks, LANES)
    code = tags[...]
    block_tag = lax.shift_right_logical(code, own.bit_length() - 1).astype(jnp.float32)
    spread = jnp.zeros((8, LANES), jnp.float32)
    for at in range(count):
        one = jnp.broadcast_to(block_tag[at : at + 1], (8, LANES))
        spread = spread + pltpu.roll(one, at * CAP, 1)
    groups = (spread[0:1], block_tag[count : count + 1])

    block_id = lax.broadcasted_iota(jnp.int32, shape, 0).astype(jnp.float32)
    before = jnp.where(
        lax.broadcasted_iota(jnp.int32, (LANES, LANES), 0)
        < lax.broadcasted_iota(jnp.int32, (LANES, LANES), 1), 1.0, 0.0,
    )
    lower = jnp.where(
        lax.broadcasted_iota(jnp.int32, (blocks, blocks), 1)
        < lax.broadcasted_iota(jnp.int32, (blocks, blocks), 0), 1.0, 0.0,
    )
    hits = [jnp.where(jnp.broadcast_to(tag, shape) == block_id + 1, 1.0, 0.0) for tag in groups]
    sums = [jnp.broadcast_to(jnp.sum(hit, axis=1, keepdims=True), shape) for hit in hits]
    covered = sums[0] + sums[1]
    first = jnp.dot(lower, covered, preferred_element_type=jnp.float32)
    ahead = (first, first + sums[0])

    line = lax.broadcasted_iota(jnp.int32, (8, LANES), 0)
    lane = lax.broadcasted_iota(jnp.int32, (8, LANES), 1).astype(jnp.float32)
    target = lax.broadcasted_iota(jnp.int32, (2 * LANES, LANES), 0).astype(jnp.float32)
    over_lanes = (((1,), (1,)), ((), ()))
    listed = jnp.zeros((8, 2 * LANES), jnp.float32)
    ends = jnp.zeros((8, 2 * LANES), jnp.float32)
    for group in range(2):
        hit, tag = hits[group], groups[group]
        rank = ahead[group] + jnp.dot(hit, before, preferred_element_type=jnp.float32)
        place = jnp.sum(hit * rank, axis=0, keepdims=True)
        shares = jnp.sum(hit * covered, axis=0, keepdims=True)
        place = jnp.where(tag > 0, place, -1.0)
        chosen = jnp.where(jnp.broadcast_to(place, target.shape) == target, 1.0, 0.0)
        values = jnp.where(line == 0, lane + group * LANES, 0.0)
        values = jnp.where(line == 1, jnp.broadcast_to(tag - 1, values.shape), values)
        values = jnp.where(line == 2, jnp.broadcast_to(shares, values.shape), values)
        listed = listed + lax.dot_general(
            values, chosen, over_lanes, preferred_element_type=jnp.float32
        )
        wide_tag = jnp.broadcast_to(tag, target.shape)
        inside = jnp.where((wide_tag > 0) & (wide_tag <= (target + 1) * per_row), 1.0, 0.0)
        ends = ends + lax.dot_general(
            jnp.ones((8, LANES), jnp.float32), inside, over_lanes,
            preferred_element_type=jnp.float32,
        )
    wide_line = lax.broadcasted_iota(jnp.int32, listed.shape, 0)
    plan[...] = jnp.where(wide_line == 3, ends, listed).astype(jnp.int32)
    share[...] = 1.0 / jnp.maximum(listed, 1.0)


def send_kernel(
    owner, offset, coef_hbm, pieces, template, band_across, band_down,
    arrived, plan_scalar, share_scalar, matched,
    plan, share,
    held, coef, owner_row, offset_row, table, rows_out, table_scalar, arrived_table,
    tags, outgoing, padded, strip_out, strip_in, across, inner, row_band, down_band,
    relay, load_sem, table_sem, send_sem, recv_sem, label_send, label_recv, rim_send, rim_recv,
    relay_recv, onward_send, detour, detour_recv, detour_send,
):
    rows, cols = lax.axis_size("py"), lax.axis_size("px")
    row, col = lax.axis_index("py"), lax.axis_index("px")
    side = template.shape[0]
    last = side - LANES
    own = held.shape[0]

    def exists(step):
        r, c = row + step[0], col + step[1]
        return (r >= 0) & (r < rows) & (c >= 0) & (c < cols)

    def neighbour(step):
        return (row + step[0], col + step[1])

    plane = lax.div(col, PLANE)
    planes = cols // PLANE
    leads = col - plane * PLANE == 0
    trails = col - plane * PLANE == PLANE - 1

    barrier = pltpu.get_barrier_semaphore()
    for step in DIRS:
        @pl.when(exists(step))
        def _():
            pl.semaphore_signal(barrier, inc=1, device_id=neighbour(step), device_id_type=MESH)

    for far, there in (
        (PLANE - 1, leads),
        (1 - PLANE, trails),
        (PLANE, (leads | trails) & (plane < planes - 1)),
        (-PLANE, (leads | trails) & (plane > 0)),
    ):
        @pl.when(there)
        def _():
            pl.semaphore_signal(
                barrier, inc=1, device_id=(row, col + far), device_id_type=MESH
            )

    body = padded.at[pl.ds(HALO, side)]
    loads = [
        pltpu.make_async_copy(
            template.at[:, pl.ds(0, LANES)], body.at[:, pl.ds(LANES, LANES)], load_sem.at[0]
        ),
        pltpu.make_async_copy(
            template.at[:, pl.ds(last, LANES)], body.at[:, pl.ds(side, LANES)], load_sem.at[1]
        ),
        pltpu.make_async_copy(owner, owner_row, load_sem.at[2]),
        pltpu.make_async_copy(offset, offset_row, load_sem.at[3]),
        pltpu.make_async_copy(pieces, held, load_sem.at[4]),
        pltpu.make_async_copy(
            template.at[:, pl.ds(LANES, side - 2 * LANES)],
            body.at[:, pl.ds(2 * LANES, side - 2 * LANES)],
            load_sem.at[5],
        ),
        pltpu.make_async_copy(band_across, row_band, load_sem.at[6]),
        pltpu.make_async_copy(band_down, down_band, load_sem.at[7]),
        pltpu.make_async_copy(coef_hbm, coef, load_sem.at[8]),
    ]
    for load in (loads[2], loads[4], loads[3], loads[0], loads[1]):
        load.start()

    def opposite(step):
        return (-step[0], -step[1])

    def rim_copy(at):
        step = DIRS[at]
        if step[0] == 0:
            source = strip_out.at[0 if step[1] > 0 else 1]
            target = strip_in.at[0 if step[1] > 0 else 1]
        else:
            source_rows = pl.ds(side - HALO if step[0] > 0 else 0, HALO)
            target_rows = pl.ds(0 if step[0] > 0 else side + HALO, HALO)
            if step[1] == 0:
                source = template.at[source_rows]
                target = padded.at[target_rows, pl.ds(LANES, side)]
            else:
                source = template.at[source_rows, pl.ds(last if step[1] > 0 else 0, LANES)]
                target = padded.at[target_rows, pl.ds(0 if step[1] > 0 else side + LANES, LANES)]
        return pltpu.make_async_remote_copy(
            src_ref=source, dst_ref=target, send_sem=rim_send.at[at], recv_sem=rim_recv.at[at],
            device_id=neighbour(step), device_id_type=MESH,
        )

    def label_copy(at):
        return pltpu.make_async_remote_copy(
            src_ref=rows_out.at[bucket_of(DIRS[at])], dst_ref=arrived_table.at[at], send_sem=label_send.at[at],
            recv_sem=label_recv.at[at], device_id=neighbour(DIRS[at]), device_id_type=MESH,
        )

    def bucket_copy(at, slots=pl.ds(0, CAP)):
        return pltpu.make_async_remote_copy(
            src_ref=outgoing.at[at, slots], dst_ref=arrived.at[at, slots], send_sem=send_sem.at[at],
            recv_sem=recv_sem.at[at], device_id=neighbour(DIRS[at]), device_id_type=MESH,
        )

    def pack_strip(strip, first_col, first_lane):
        lane_group = lax.broadcasted_iota(jnp.int32, (LANES, LANES), 1) // HALO
        packed = jnp.zeros((LANES, LANES), jnp.float32)
        for group in range(side // LANES):
            block = padded[pl.ds(HALO + group * LANES, LANES), pl.ds(first_col, LANES)]
            moved = pltpu.roll(
                block.astype(jnp.float32), (group * HALO - first_lane) % LANES, 1
            )
            packed = jnp.where(lane_group == group, moved, packed)
        strip_out[strip] = packed.astype(jnp.bfloat16)

    def column_first(step):
        return row == (2 if step[0] < 0 else rows - 3)

    def row_first(step):
        return row == (1 if step[0] > 0 else rows - 2)

    def relay_copy(at, slots):
        step = DIRS[at]
        return pltpu.make_async_remote_copy(
            src_ref=outgoing.at[at, slots], dst_ref=relay.at[at, slots],
            send_sem=send_sem.at[at], recv_sem=relay_recv.at[at],
            device_id=(
                row + jnp.where(row_first(step), 0, step[0]),
                col + jnp.where(column_first(step), 0, step[1]),
            ),
            device_id_type=MESH,
        )

    def turns_column(step):
        return row == (1 if step[0] < 0 else rows - 2)

    def turns_row(step):
        return row == (1 if step[0] > 0 else rows - 2)

    def turns(step):
        ahead, behind = col + step[1], col - step[1]
        return (turns_column(step) & (ahead >= 0) & (ahead < cols)) | (
            turns_row(step) & (behind >= 0) & (behind < cols)
        )

    def onward_copy(at, slots):
        step = DIRS[at]
        return pltpu.make_async_remote_copy(
            src_ref=relay.at[at, slots], dst_ref=arrived.at[at, slots],
            send_sem=onward_send.at[at], recv_sem=recv_sem.at[at],
            device_id=(
                row + jnp.where(turns_row(step), step[0], 0),
                col + jnp.where(turns_column(step), step[1], 0),
            ),
            device_id_type=MESH,
        )

    detours = (
        (DIRS.index((0, 1)), 1, trails & (plane < planes - 1), DETOUR * (plane + 1)),
        (DIRS.index((0, -1)), -1, leads & (plane > 0), DETOUR * (planes - plane)),
    )
    passes = (
        (DIRS.index((0, 1)), 1, trails, plane),
        (DIRS.index((0, -1)), -1, leads, planes - 1 - plane),
    )

    def detour_copy(at, way, slots):
        return pltpu.make_async_remote_copy(
            src_ref=outgoing.at[at, slots], dst_ref=detour.at[slots],
            send_sem=send_sem.at[at], recv_sem=detour_recv,
            device_id=(row, col + way * PLANE), device_id_type=MESH,
        )

    def rejoin_copy(at, way, slots):
        return pltpu.make_async_remote_copy(
            src_ref=detour.at[slots], dst_ref=arrived.at[at, slots],
            send_sem=detour_send, recv_sem=recv_sem.at[at],
            device_id=(row, col - way * (PLANE - 1)), device_id_type=MESH,
        )

    def send_pieces(slot, piece_of, relayed):
        for at, step in enumerate(DIRS):
            outgoing[at, slot] = held[piece_of(bucket_of(step))]
            direct = exists(step)
            if relayed and at < DIAGONALS:
                turned = column_first(step) | row_first(step)

                @pl.when(direct & turned)
                def _():
                    relay_copy(at, pl.ds(slot, 1)).start()
                direct = direct & jnp.logical_not(turned)
            for detour_at, way, here, slots in detours:
                if at == detour_at:
                    around = here & (slot < slots)

                    @pl.when(around)
                    def _():
                        detour_copy(at, way, pl.ds(slot, 1)).start()
                    direct = direct & jnp.logical_not(around)

            @pl.when(direct)
            def _():
                bucket_copy(at, pl.ds(slot, 1)).start()
        arrived[len(DIRS), slot] = held[piece_of(OWN)]

    def send_slot(relayed, slot, carry):
        send_pieces(slot, lambda bucket: table_scalar[bucket, slot] & (own - 1), relayed)
        return carry

    loads[2].wait()
    bucket_id = lax.broadcasted_iota(jnp.int32, (16, own), 0)
    target = jnp.full((16, own), -1, jnp.int32)
    for bucket in range(9):
        tile = (row + bucket // 3 - 1) * cols + col + bucket % 3 - 1
        target = jnp.where(bucket_id == bucket, tile, target)
    belongs = target == jnp.broadcast_to(owner_row[...], (16, own))
    number = lax.broadcasted_iota(jnp.int32, (16, own), 1).astype(jnp.float32)
    leader = [
        jnp.min(jnp.where(belongs & (bucket_id == bucket), number, own - 1.0)).astype(jnp.int32)
        & (own - 1)
        for bucket in range(9)
    ]
    tall_group = 3 - jnp.where(row == 0, 1, 0) - jnp.where(row == rows - 1, 1, 0)
    wide_group = 3 - jnp.where(col == 0, 1, 0) - jnp.where(col == cols - 1, 1, 0)
    mates = 3 - jnp.where(plane == 0, 1, 0) - jnp.where(plane == planes - 1, 1, 0)
    mates = jnp.where(leads | trails, mates, 0)
    pl.semaphore_wait(barrier, tall_group * wide_group - 1 + mates)
    loads[4].wait()
    send_pieces(0, lambda bucket: leader[bucket], True)

    loads[3].wait()
    earlier = (
        lax.broadcasted_iota(jnp.int32, (own, own), 0)
        < lax.broadcasted_iota(jnp.int32, (own, own), 1)
    )
    place = jnp.dot(
        jnp.where(belongs, 1.0, 0.0), jnp.where(earlier, 1.0, 0.0),
        preferred_element_type=jnp.float32,
    )
    code = lax.broadcasted_iota(jnp.int32, (16, own), 1) + own * (
        jnp.broadcast_to(offset_row[...], (16, own)) + 1
    )
    code = jnp.where(belongs, code.astype(jnp.float32), 0.0)
    slot_lane = lax.broadcasted_iota(jnp.int32, (16, LANES), 1)
    filled = jnp.zeros((16, LANES), jnp.float32)
    for slot in range(CAP):
        picked = jnp.sum(jnp.where(place == slot, code, 0.0), axis=1, keepdims=True)
        filled = jnp.where(slot_lane == slot, picked, filled)
    filled = filled.astype(jnp.int32)
    table[...] = filled
    for bucket in range(9):
        rows_out[bucket] = filled[bucket : bucket + 1]
    to_scalar = pltpu.make_async_copy(table, table_scalar, table_sem)
    to_scalar.start()

    loads[0].wait()
    loads[1].wait()
    pack_strip(0, side, LANES - HALO)
    pack_strip(1, LANES, 0)
    for at, step in enumerate(DIRS):
        @pl.when(exists(step))
        def _():
            rim_copy(at).start()
            label_copy(at).start()
    to_scalar.wait()
    lax.fori_loop(1, 4, functools.partial(send_slot, True), 0)
    for load in loads[5:]:
        load.start()
    lax.fori_loop(4, RELAYED, functools.partial(send_slot, True), 0)
    lax.fori_loop(RELAYED, EARLY, functools.partial(send_slot, False), 0)

    loads[8].wait()
    lane = lax.broadcasted_iota(jnp.int32, (8, side), 1)
    u = ((col * side + lane).astype(jnp.float32) + 0.5) * (2.0 / (side * cols)) - 1.0
    for basis in range(BASES):
        for power_v in range(DEGREE + 1):
            total = jnp.zeros_like(u)
            for power_u in reversed(range(DEGREE + 1 - power_v)):
                total = total * u + coef[basis, term_powers.index((power_u, power_v))]
            inner[basis, power_v] = total

    for load in loads[5:8]:
        load.wait()
    wide = padded.shape[1]

    @pl.when(row == 0)
    def _():
        padded[pl.ds(0, HALO)] = jnp.zeros((HALO, wide), jnp.bfloat16)

    @pl.when(row == rows - 1)
    def _():
        padded[pl.ds(side + HALO, HALO)] = jnp.zeros((HALO, wide), jnp.bfloat16)

    @pl.when(col == 0)
    def _():
        padded[:, pl.ds(0, LANES)] = jnp.zeros((padded.shape[0], LANES), jnp.bfloat16)

    @pl.when(col == cols - 1)
    def _():
        padded[:, pl.ds(side + LANES, LANES)] = jnp.zeros((padded.shape[0], LANES), jnp.bfloat16)

    for at, step in enumerate(DIRS):
        @pl.when(exists(opposite(step)))
        def _():
            rim_copy(at).wait_recv()

    def unpack_strip(strip, first_col, first_lane):
        packed = strip_in[strip].astype(jnp.float32)
        for group in range(side // LANES):
            moved = pltpu.roll(packed, (first_lane - group * HALO) % LANES, 1)
            padded[pl.ds(HALO + group * LANES, LANES), pl.ds(first_col, LANES)] = moved.astype(jnp.bfloat16)

    @pl.when(col > 0)
    def _():
        unpack_strip(0, 0, LANES - HALO)

    @pl.when(col < cols - 1)
    def _():
        unpack_strip(1, side + LANES, 0)

    tall = padded.shape[0]
    chunk = tall // 3
    blocks = side // LANES
    for basis in range(BASES):
        across[basis, pl.ds(tall, across.shape[1] - tall)] = jnp.zeros(
            (across.shape[1] - tall, side), jnp.bfloat16
        )

    def row_pass(block, carry):
        first = pl.multiple_of(block * LANES, LANES)
        for part in range(3):
            got = jnp.dot(
                padded[pl.ds(part * chunk, chunk), pl.ds(first, 3 * LANES)],
                row_band[...],
                preferred_element_type=jnp.float32,
            )
            for basis in range(BASES):
                across[basis, pl.ds(part * chunk, chunk), pl.ds(first, LANES)] = got[
                    :, basis * LANES : (basis + 1) * LANES
                ].astype(jnp.bfloat16)
        return carry

    lax.fori_loop(0, blocks, row_pass, 0)

    part_cols = 2 * LANES

    def column_pass(block, carry):
        first = pl.multiple_of(block * LANES, LANES)
        line = lax.broadcasted_iota(jnp.int32, (LANES, part_cols), 0)
        v = ((row * side + first + line).astype(jnp.float32) + 0.5) * (2.0 / (side * rows)) - 1.0
        for part in range(side // part_cols):
            columns = pl.ds(part * part_cols, part_cols)
            total = jnp.zeros((LANES, part_cols), jnp.float32)
            for basis in range(BASES):
                smoothed = jnp.dot(
                    down_band[basis],
                    across[basis, pl.ds(first, 2 * LANES), columns],
                    preferred_element_type=jnp.float32,
                )
                weight = jnp.broadcast_to(inner[basis, DEGREE, 0:1, columns], total.shape)
                for power_v in reversed(range(DEGREE)):
                    weight = weight * v + inner[basis, power_v, 0:1, columns]
                total = total - weight * smoothed
            matched[pl.ds(first, LANES), columns] = total
        return carry

    lax.fori_loop(0, blocks, column_pass, 0)

    for at in range(DIAGONALS):
        @pl.when(turns(DIRS[at]))
        def _():
            relay_copy(at, pl.ds(0, RELAYED)).wait_recv()

            def pass_on(slot, carry):
                onward_copy(at, pl.ds(slot, 1)).start()
                return carry

            lax.fori_loop(0, RELAYED, pass_on, 0)
    for at, way, here, share_of in passes:
        for thirds in range(1, planes):
            @pl.when(here & (share_of == thirds))
            def _():
                detour_copy(at, way, pl.ds(0, DETOUR * thirds)).wait_recv()

                def rejoin(slot, carry):
                    rejoin_copy(at, way, pl.ds(slot, 1)).start()
                    return carry

                lax.fori_loop(0, DETOUR * thirds, rejoin, 0)
    lax.fori_loop(EARLY, CAP, functools.partial(send_slot, False), 0)

    for at, step in enumerate(DIRS):
        tags[pl.ds(at, 1)] = jnp.zeros((1, LANES), jnp.int32)

        @pl.when(exists(opposite(step)))
        def _():
            label_copy(at).wait_recv()
            tags[pl.ds(at, 1)] = arrived_table[at]
    tags[pl.ds(len(DIRS), 1)] = table[pl.ds(OWN, 1)]
    sort_plan(own, side // LANES, tags, plan, share)
    plan_copies = [
        pltpu.make_async_copy(plan, plan_scalar, load_sem.at[0]),
        pltpu.make_async_copy(share, share_scalar, load_sem.at[1]),
    ]
    for plan_copy in plan_copies:
        plan_copy.start()

    for at in range(DIAGONALS):
        @pl.when(turns(DIRS[at]))
        def _():
            onward_copy(at, pl.ds(0, RELAYED)).wait_send()
    for at, way, here, share_of in passes:
        for thirds in range(1, planes):
            @pl.when(here & (share_of == thirds))
            def _():
                rejoin_copy(at, way, pl.ds(0, DETOUR * thirds)).wait_send()
    for plan_copy in plan_copies:
        plan_copy.wait()
    for at, step in enumerate(DIRS):
        @pl.when(exists(step))
        def _():
            rim_copy(at).wait_send()
            label_copy(at).wait_send()
            bucket_copy(at).wait_send()
    for at in reversed(range(len(DIRS))):
        @pl.when(exists(opposite(DIRS[at])))
        def _():
            bucket_copy(at).wait_recv()


def join_kernel(plan, share, arrived, matched, out, total, out_sem):
    side = out.shape[1]
    per_row = side // LANES

    def row_lines(block_row):
        return pl.ds(pl.multiple_of(block_row * LANES, LANES), LANES)

    def out_copy(block_row):
        lines = row_lines(block_row)
        return pltpu.make_async_copy(total.at[lines], out.at[lines], out_sem.at[block_row])

    def join_row(block_row, start):
        end = plan[3, block_row]
        lines = row_lines(block_row)

        def add(at, carry):
            slot = plan[0, at]
            column = pl.multiple_of((plan[1, at] - block_row * per_row) * LANES, LANES)
            columns = pl.ds(column, LANES)
            piece = arrived[lax.div(slot, CAP), slot & (CAP - 1)].astype(jnp.float32)
            total[lines, columns] = total[lines, columns] + share[2, at] * piece
            return carry

        lax.fori_loop(start, end, add, 0)
        out_copy(block_row).start()
        return end

    lax.fori_loop(0, per_row, join_row, 0)
    for block_row in range(per_row):
        out_copy(block_row).wait()


def on_device(pieces, owner_map, offsets, template, coefficients):
    own, block_side = pieces.shape[0], pieces.shape[1]
    side = template.shape[0]
    smem = pl.BlockSpec(memory_space=pltpu.SMEM)
    vmem = pl.BlockSpec(memory_space=pltpu.VMEM)
    hbm = pl.BlockSpec(memory_space=pltpu.HBM)
    count = len(DIRS)

    band_across, band_down = band_tables()
    tall = side + 2 * HALO
    dma = pltpu.SemaphoreType.DMA
    arrived, plan, share, matched = pl.pallas_call(
        send_kernel,
        out_shape=[
            jax.ShapeDtypeStruct((count + 1, CAP, block_side, block_side), jnp.bfloat16),
            pltpu.SMEM((8, 2 * LANES), jnp.int32),
            pltpu.SMEM((8, 2 * LANES), jnp.float32),
            jax.ShapeDtypeStruct((side, side), jnp.float32),
        ],
        in_specs=[hbm] * 7,
        out_specs=[vmem, smem, smem, vmem],
        scratch_shapes=[
            pltpu.VMEM((8, 2 * LANES), jnp.int32),
            pltpu.VMEM((8, 2 * LANES), jnp.float32),
            pltpu.VMEM((own, block_side, block_side), jnp.bfloat16),
            pltpu.SMEM(coefficients.shape, jnp.float32),
            pltpu.VMEM((1, own), jnp.int32),
            pltpu.VMEM((1, own), jnp.int32),
            pltpu.VMEM((16, LANES), jnp.int32),
            pltpu.VMEM((9, 1, LANES), jnp.int32),
            pltpu.SMEM((16, LANES), jnp.int32),
            pltpu.VMEM((count, 1, LANES), jnp.int32),
            pltpu.VMEM((16, LANES), jnp.int32),
            pltpu.VMEM((count, CAP, block_side, block_side), jnp.bfloat16),
            pltpu.VMEM((tall, side + 2 * LANES), jnp.bfloat16),
            pltpu.VMEM((2, LANES, LANES), jnp.bfloat16),
            pltpu.VMEM((2, LANES, LANES), jnp.bfloat16),
            pltpu.VMEM((BASES, side + LANES, side), jnp.bfloat16),
            pltpu.VMEM((BASES, DEGREE + 1, 8, side), jnp.float32),
            pltpu.VMEM(band_across.shape, jnp.bfloat16),
            pltpu.VMEM(band_down.shape, jnp.bfloat16),
            pltpu.VMEM((DIAGONALS, RELAYED, block_side, block_side), jnp.bfloat16),
            dma((9,)), dma, dma((count,)), dma((count,)), dma((count,)), dma((count,)),
            dma((count,)), dma((count,)), dma((DIAGONALS,)), dma((DIAGONALS,)),
            pltpu.VMEM((3 * DETOUR, block_side, block_side), jnp.bfloat16), dma, dma,
        ],
        compiler_params=pltpu.CompilerParams(
            collective_id=0, has_side_effects=True, vmem_limit_bytes=40 << 20
        ),
        name="send",
    )(
        *(
            pltpu.with_memory_space_constraint(array, pltpu.HBM)
            for array in (
                owner_map.reshape(1, own), offsets.reshape(1, own), coefficients, pieces,
                template, jnp.asarray(band_across), jnp.asarray(band_down),
            )
        )
    )
    joined, _ = pl.pallas_call(
        join_kernel,
        out_shape=[jax.ShapeDtypeStruct((side, side), jnp.float32)] * 2,
        in_specs=[smem, smem, vmem, vmem],
        out_specs=[hbm, vmem],
        input_output_aliases={3: 1},
        scratch_shapes=[dma((side // block_side,))],
        compiler_params=pltpu.CompilerParams(vmem_limit_bytes=32 << 20),
        name="join",
    )(plan, share, arrived, matched)
    return joined


def solution(mesh):
    in_specs = (P(("py", "px"), None, None), P(("py", "px")), P(("py", "px")), P("py", "px"), P())
    out_specs = P("py", "px")
    return jax.shard_map(
        on_device, mesh=mesh, in_specs=in_specs, out_specs=out_specs, check_vma=False
    )
```

```python
import functools

import jax
import jax.numpy as jnp
import numpy as np
from jax import lax
from jax.experimental import pallas as pl
from jax.experimental.pallas import tpu as pltpu
from jax.sharding import PartitionSpec as P

HALO = 16
CAP = 16
LANES = 128
BASES = 3
DEGREE = 4

sigma_fractions = (0.09375, 0.1875, 0.375)
term_powers = [(degree - power_v, power_v) for degree in range(5) for power_v in range(degree + 1)]

DIRS = ((1, 1), (-1, -1), (1, -1), (-1, 1), (0, 1), (0, -1), (1, 0), (-1, 0))
DIAGONALS = 4
COLUMN_RELAYED = 9
ROW_RELAYED = 8
PLANE = 4
DETOUR = 3
EARLY = 14
OWN = 4
MESH = pl.DeviceIdType.MESH


def bucket_of(step):
    return 3 * (step[0] + 1) + step[1] + 1


def gauss_taps():
    positions = np.arange(-HALO, HALO + 1).astype(np.float32)
    stacked = []
    for fraction in sigma_fractions:
        sigma = fraction * HALO
        values = np.exp(-positions * positions / np.float32(2.0 * sigma * sigma))
        stacked.append(values / np.sum(values))
    return np.stack(stacked).astype(jnp.bfloat16)


def band_tables():
    taps = gauss_taps()
    across = np.zeros((3 * LANES, BASES * LANES), taps.dtype)
    down = np.zeros((BASES, LANES, 2 * LANES), taps.dtype)
    for basis in range(BASES):
        for out in range(LANES):
            for tap in range(2 * HALO + 1):
                across[LANES - HALO + out + tap, basis * LANES + out] = taps[basis, tap]
                down[basis, out, out + tap] = taps[basis, tap]
    return across, down


def sort_plan(own, per_row, tags, plan, share):
    count = len(DIRS)
    blocks = per_row * per_row
    shape = (blocks, LANES)
    code = tags[...]
    block_tag = lax.shift_right_logical(code, own.bit_length() - 1).astype(jnp.float32)
    spread = jnp.zeros((8, LANES), jnp.float32)
    for at in range(count):
        one = jnp.broadcast_to(block_tag[at : at + 1], (8, LANES))
        spread = spread + pltpu.roll(one, at * CAP, 1)
    groups = (spread[0:1], block_tag[count : count + 1])

    block_id = lax.broadcasted_iota(jnp.int32, shape, 0).astype(jnp.float32)
    before = jnp.where(
        lax.broadcasted_iota(jnp.int32, (LANES, LANES), 0)
        < lax.broadcasted_iota(jnp.int32, (LANES, LANES), 1), 1.0, 0.0,
    )
    lower = jnp.where(
        lax.broadcasted_iota(jnp.int32, (blocks, blocks), 1)
        < lax.broadcasted_iota(jnp.int32, (blocks, blocks), 0), 1.0, 0.0,
    )
    hits = [jnp.where(jnp.broadcast_to(tag, shape) == block_id + 1, 1.0, 0.0) for tag in groups]
    sums = [jnp.broadcast_to(jnp.sum(hit, axis=1, keepdims=True), shape) for hit in hits]
    covered = sums[0] + sums[1]
    first = jnp.dot(lower, covered, preferred_element_type=jnp.float32)
    ahead = (first, first + sums[0])

    line = lax.broadcasted_iota(jnp.int32, (8, LANES), 0)
    lane = lax.broadcasted_iota(jnp.int32, (8, LANES), 1).astype(jnp.float32)
    target = lax.broadcasted_iota(jnp.int32, (2 * LANES, LANES), 0).astype(jnp.float32)
    over_lanes = (((1,), (1,)), ((), ()))
    listed = jnp.zeros((8, 2 * LANES), jnp.float32)
    ends = jnp.zeros((8, 2 * LANES), jnp.float32)
    for group in range(2):
        hit, tag = hits[group], groups[group]
        rank = ahead[group] + jnp.dot(hit, before, preferred_element_type=jnp.float32)
        place = jnp.sum(hit * rank, axis=0, keepdims=True)
        shares = jnp.sum(hit * covered, axis=0, keepdims=True)
        place = jnp.where(tag > 0, place, -1.0)
        chosen = jnp.where(jnp.broadcast_to(place, target.shape) == target, 1.0, 0.0)
        values = jnp.where(line == 0, lane + group * LANES, 0.0)
        values = jnp.where(line == 1, jnp.broadcast_to(tag - 1, values.shape), values)
        values = jnp.where(line == 2, jnp.broadcast_to(shares, values.shape), values)
        listed = listed + lax.dot_general(
            values, chosen, over_lanes, preferred_element_type=jnp.float32
        )
        wide_tag = jnp.broadcast_to(tag, target.shape)
        inside = jnp.where((wide_tag > 0) & (wide_tag <= (target + 1) * per_row), 1.0, 0.0)
        ends = ends + lax.dot_general(
            jnp.ones((8, LANES), jnp.float32), inside, over_lanes,
            preferred_element_type=jnp.float32,
        )
    wide_line = lax.broadcasted_iota(jnp.int32, listed.shape, 0)
    plan[...] = jnp.where(wide_line == 3, ends, listed).astype(jnp.int32)
    share[...] = 1.0 / jnp.maximum(listed, 1.0)


def send_kernel(
    owner, offset, coef_hbm, pieces, template, band_across, band_down,
    arrived, plan_scalar, share_scalar, matched,
    plan, share,
    held, coef, owner_row, offset_row, table, rows_out, table_scalar, arrived_table,
    tags, outgoing, padded, strip_out, strip_in, across, inner, row_band, down_band,
    relay, load_sem, table_sem, send_sem, recv_sem, label_send, label_recv, rim_send, rim_recv,
    relay_recv, onward_send, detour, detour_recv, detour_send,
):
    rows, cols = lax.axis_size("py"), lax.axis_size("px")
    row, col = lax.axis_index("py"), lax.axis_index("px")
    side = template.shape[0]
    last = side - LANES
    own = held.shape[0]

    def exists(step):
        r, c = row + step[0], col + step[1]
        return (r >= 0) & (r < rows) & (c >= 0) & (c < cols)

    def neighbour(step):
        return (row + step[0], col + step[1])

    plane = lax.div(col, PLANE)
    planes = cols // PLANE
    leads = col - plane * PLANE == 0
    trails = col - plane * PLANE == PLANE - 1

    barrier = pltpu.get_barrier_semaphore()
    for step in DIRS:
        @pl.when(exists(step))
        def _():
            pl.semaphore_signal(barrier, inc=1, device_id=neighbour(step), device_id_type=MESH)

    for far, there in (
        (PLANE - 1, leads),
        (1 - PLANE, trails),
        (PLANE, (leads | trails) & (plane < planes - 1)),
        (-PLANE, (leads | trails) & (plane > 0)),
    ):
        @pl.when(there)
        def _():
            pl.semaphore_signal(
                barrier, inc=1, device_id=(row, col + far), device_id_type=MESH
            )

    body = padded.at[pl.ds(HALO, side)]
    loads = [
        pltpu.make_async_copy(
            template.at[:, pl.ds(0, LANES)], body.at[:, pl.ds(LANES, LANES)], load_sem.at[0]
        ),
        pltpu.make_async_copy(
            template.at[:, pl.ds(last, LANES)], body.at[:, pl.ds(side, LANES)], load_sem.at[1]
        ),
        pltpu.make_async_copy(owner, owner_row, load_sem.at[2]),
        pltpu.make_async_copy(offset, offset_row, load_sem.at[3]),
        pltpu.make_async_copy(pieces, held, load_sem.at[4]),
        pltpu.make_async_copy(
            template.at[:, pl.ds(LANES, side - 2 * LANES)],
            body.at[:, pl.ds(2 * LANES, side - 2 * LANES)],
            load_sem.at[5],
        ),
        pltpu.make_async_copy(band_across, row_band, load_sem.at[6]),
        pltpu.make_async_copy(band_down, down_band, load_sem.at[7]),
        pltpu.make_async_copy(coef_hbm, coef, load_sem.at[8]),
    ]
    for load in (loads[2], loads[4], loads[3], loads[0], loads[1]):
        load.start()

    def opposite(step):
        return (-step[0], -step[1])

    def rim_copy(at):
        step = DIRS[at]
        if step[0] == 0:
            source = strip_out.at[0 if step[1] > 0 else 1]
            target = strip_in.at[0 if step[1] > 0 else 1]
        else:
            source_rows = pl.ds(side - HALO if step[0] > 0 else 0, HALO)
            target_rows = pl.ds(0 if step[0] > 0 else side + HALO, HALO)
            if step[1] == 0:
                source = template.at[source_rows]
                target = padded.at[target_rows, pl.ds(LANES, side)]
            else:
                source = template.at[source_rows, pl.ds(last if step[1] > 0 else 0, LANES)]
                target = padded.at[target_rows, pl.ds(0 if step[1] > 0 else side + LANES, LANES)]
        return pltpu.make_async_remote_copy(
            src_ref=source, dst_ref=target, send_sem=rim_send.at[at], recv_sem=rim_recv.at[at],
            device_id=neighbour(step), device_id_type=MESH,
        )

    def label_copy(at):
        return pltpu.make_async_remote_copy(
            src_ref=rows_out.at[bucket_of(DIRS[at])], dst_ref=arrived_table.at[at], send_sem=label_send.at[at],
            recv_sem=label_recv.at[at], device_id=neighbour(DIRS[at]), device_id_type=MESH,
        )

    def bucket_copy(at, slots=pl.ds(0, CAP)):
        return pltpu.make_async_remote_copy(
            src_ref=outgoing.at[at, slots], dst_ref=arrived.at[at, slots], send_sem=send_sem.at[at],
            recv_sem=recv_sem.at[at], device_id=neighbour(DIRS[at]), device_id_type=MESH,
        )

    def pack_strip(strip, first_col, first_lane):
        lane_group = lax.broadcasted_iota(jnp.int32, (LANES, LANES), 1) // HALO
        packed = jnp.zeros((LANES, LANES), jnp.float32)
        for group in range(side // LANES):
            block = padded[pl.ds(HALO + group * LANES, LANES), pl.ds(first_col, LANES)]
            moved = pltpu.roll(
                block.astype(jnp.float32), (group * HALO - first_lane) % LANES, 1
            )
            packed = jnp.where(lane_group == group, moved, packed)
        strip_out[strip] = packed.astype(jnp.bfloat16)

    def column_first(step):
        return row == (2 if step[0] < 0 else rows - 3)

    def row_first(step):
        return row == (1 if step[0] > 0 else rows - 2)

    def relay_copy(at, slots):
        step = DIRS[at]
        return pltpu.make_async_remote_copy(
            src_ref=outgoing.at[at, slots], dst_ref=relay.at[at, slots],
            send_sem=send_sem.at[at], recv_sem=relay_recv.at[at],
            device_id=(
                row + jnp.where(row_first(step), 0, step[0]),
                col + jnp.where(column_first(step), 0, step[1]),
            ),
            device_id_type=MESH,
        )

    def turns_column(step):
        return row == (1 if step[0] < 0 else rows - 2)

    def turns_row(step):
        return row == (1 if step[0] > 0 else rows - 2)

    def turns(step):
        ahead, behind = col + step[1], col - step[1]
        return (
            (turns_column(step) & (ahead >= 0) & (ahead < cols), COLUMN_RELAYED),
            (turns_row(step) & (behind >= 0) & (behind < cols), ROW_RELAYED),
        )

    def onward_copy(at, slots):
        step = DIRS[at]
        return pltpu.make_async_remote_copy(
            src_ref=relay.at[at, slots], dst_ref=arrived.at[at, slots],
            send_sem=onward_send.at[at], recv_sem=recv_sem.at[at],
            device_id=(
                row + jnp.where(turns_row(step), step[0], 0),
                col + jnp.where(turns_column(step), step[1], 0),
            ),
            device_id_type=MESH,
        )

    detours = (
        (DIRS.index((0, 1)), 1, trails & (plane < planes - 1), DETOUR * (plane + 1)),
        (DIRS.index((0, -1)), -1, leads & (plane > 0), DETOUR * (planes - plane)),
    )
    passes = (
        (DIRS.index((0, 1)), 1, trails, plane),
        (DIRS.index((0, -1)), -1, leads, planes - 1 - plane),
    )

    def detour_copy(at, way, slots):
        return pltpu.make_async_remote_copy(
            src_ref=outgoing.at[at, slots], dst_ref=detour.at[slots],
            send_sem=send_sem.at[at], recv_sem=detour_recv,
            device_id=(row, col + way * PLANE), device_id_type=MESH,
        )

    def rejoin_copy(at, way, slots):
        return pltpu.make_async_remote_copy(
            src_ref=detour.at[slots], dst_ref=arrived.at[at, slots],
            send_sem=detour_send, recv_sem=recv_sem.at[at],
            device_id=(row, col - way * (PLANE - 1)), device_id_type=MESH,
        )

    def send_pieces(slot, piece_of, relayed):
        for at, step in enumerate(DIRS):
            outgoing[at, slot] = held[piece_of(bucket_of(step))]
            direct = exists(step)
            if relayed and at < DIAGONALS:
                turned = (column_first(step) & (slot < COLUMN_RELAYED)) | (
                    row_first(step) & (slot < ROW_RELAYED)
                )

                @pl.when(direct & turned)
                def _():
                    relay_copy(at, pl.ds(slot, 1)).start()
                direct = direct & jnp.logical_not(turned)
            for detour_at, way, here, slots in detours:
                if at == detour_at:
                    around = here & (slot < slots)

                    @pl.when(around)
                    def _():
                        detour_copy(at, way, pl.ds(slot, 1)).start()
                    direct = direct & jnp.logical_not(around)

            @pl.when(direct)
            def _():
                bucket_copy(at, pl.ds(slot, 1)).start()
        arrived[len(DIRS), slot] = held[piece_of(OWN)]

    def send_slot(relayed, slot, carry):
        send_pieces(slot, lambda bucket: table_scalar[bucket, slot] & (own - 1), relayed)
        return carry

    loads[2].wait()
    bucket_id = lax.broadcasted_iota(jnp.int32, (16, own), 0)
    target = jnp.full((16, own), -1, jnp.int32)
    for bucket in range(9):
        tile = (row + bucket // 3 - 1) * cols + col + bucket % 3 - 1
        target = jnp.where(bucket_id == bucket, tile, target)
    belongs = target == jnp.broadcast_to(owner_row[...], (16, own))
    number = lax.broadcasted_iota(jnp.int32, (16, own), 1).astype(jnp.float32)
    leader = [
        jnp.min(jnp.where(belongs & (bucket_id == bucket), number, own - 1.0)).astype(jnp.int32)
        & (own - 1)
        for bucket in range(9)
    ]
    tall_group = 3 - jnp.where(row == 0, 1, 0) - jnp.where(row == rows - 1, 1, 0)
    wide_group = 3 - jnp.where(col == 0, 1, 0) - jnp.where(col == cols - 1, 1, 0)
    mates = 3 - jnp.where(plane == 0, 1, 0) - jnp.where(plane == planes - 1, 1, 0)
    mates = jnp.where(leads | trails, mates, 0)
    pl.semaphore_wait(barrier, tall_group * wide_group - 1 + mates)
    loads[4].wait()
    send_pieces(0, lambda bucket: leader[bucket], True)

    loads[3].wait()
    earlier = (
        lax.broadcasted_iota(jnp.int32, (own, own), 0)
        < lax.broadcasted_iota(jnp.int32, (own, own), 1)
    )
    place = jnp.dot(
        jnp.where(belongs, 1.0, 0.0), jnp.where(earlier, 1.0, 0.0),
        preferred_element_type=jnp.float32,
    )
    code = lax.broadcasted_iota(jnp.int32, (16, own), 1) + own * (
        jnp.broadcast_to(offset_row[...], (16, own)) + 1
    )
    code = jnp.where(belongs, code.astype(jnp.float32), 0.0)
    slot_lane = lax.broadcasted_iota(jnp.int32, (16, LANES), 1)
    filled = jnp.zeros((16, LANES), jnp.float32)
    for slot in range(CAP):
        picked = jnp.sum(jnp.where(place == slot, code, 0.0), axis=1, keepdims=True)
        filled = jnp.where(slot_lane == slot, picked, filled)
    filled = filled.astype(jnp.int32)
    table[...] = filled
    for bucket in range(9):
        rows_out[bucket] = filled[bucket : bucket + 1]
    to_scalar = pltpu.make_async_copy(table, table_scalar, table_sem)
    to_scalar.start()

    loads[0].wait()
    loads[1].wait()
    pack_strip(0, side, LANES - HALO)
    pack_strip(1, LANES, 0)
    for at, step in enumerate(DIRS):
        @pl.when(exists(step))
        def _():
            rim_copy(at).start()
            label_copy(at).start()
    to_scalar.wait()
    lax.fori_loop(1, 4, functools.partial(send_slot, True), 0)
    for load in loads[5:]:
        load.start()
    lax.fori_loop(4, COLUMN_RELAYED, functools.partial(send_slot, True), 0)
    lax.fori_loop(COLUMN_RELAYED, EARLY, functools.partial(send_slot, False), 0)

    loads[8].wait()
    lane = lax.broadcasted_iota(jnp.int32, (8, side), 1)
    u = ((col * side + lane).astype(jnp.float32) + 0.5) * (2.0 / (side * cols)) - 1.0
    for basis in range(BASES):
        for power_v in range(DEGREE + 1):
            total = jnp.zeros_like(u)
            for power_u in reversed(range(DEGREE + 1 - power_v)):
                total = total * u + coef[basis, term_powers.index((power_u, power_v))]
            inner[basis, power_v] = total

    for load in loads[5:8]:
        load.wait()
    wide = padded.shape[1]

    @pl.when(row == 0)
    def _():
        padded[pl.ds(0, HALO)] = jnp.zeros((HALO, wide), jnp.bfloat16)

    @pl.when(row == rows - 1)
    def _():
        padded[pl.ds(side + HALO, HALO)] = jnp.zeros((HALO, wide), jnp.bfloat16)

    @pl.when(col == 0)
    def _():
        padded[:, pl.ds(0, LANES)] = jnp.zeros((padded.shape[0], LANES), jnp.bfloat16)

    @pl.when(col == cols - 1)
    def _():
        padded[:, pl.ds(side + LANES, LANES)] = jnp.zeros((padded.shape[0], LANES), jnp.bfloat16)

    for at, step in enumerate(DIRS):
        @pl.when(exists(opposite(step)))
        def _():
            rim_copy(at).wait_recv()

    def unpack_strip(strip, first_col, first_lane):
        packed = strip_in[strip].astype(jnp.float32)
        for group in range(side // LANES):
            moved = pltpu.roll(packed, (first_lane - group * HALO) % LANES, 1)
            padded[pl.ds(HALO + group * LANES, LANES), pl.ds(first_col, LANES)] = moved.astype(jnp.bfloat16)

    @pl.when(col > 0)
    def _():
        unpack_strip(0, 0, LANES - HALO)

    @pl.when(col < cols - 1)
    def _():
        unpack_strip(1, side + LANES, 0)

    tall = padded.shape[0]
    chunk = tall // 3
    blocks = side // LANES
    for basis in range(BASES):
        across[basis, pl.ds(tall, across.shape[1] - tall)] = jnp.zeros(
            (across.shape[1] - tall, side), jnp.bfloat16
        )

    def row_pass(block, carry):
        first = pl.multiple_of(block * LANES, LANES)
        for part in range(3):
            got = jnp.dot(
                padded[pl.ds(part * chunk, chunk), pl.ds(first, 3 * LANES)],
                row_band[...],
                preferred_element_type=jnp.float32,
            )
            for basis in range(BASES):
                across[basis, pl.ds(part * chunk, chunk), pl.ds(first, LANES)] = got[
                    :, basis * LANES : (basis + 1) * LANES
                ].astype(jnp.bfloat16)
        return carry

    lax.fori_loop(0, blocks, row_pass, 0)

    part_cols = 2 * LANES

    def column_pass(block, carry):
        first = pl.multiple_of(block * LANES, LANES)
        line = lax.broadcasted_iota(jnp.int32, (LANES, part_cols), 0)
        v = ((row * side + first + line).astype(jnp.float32) + 0.5) * (2.0 / (side * rows)) - 1.0
        for part in range(side // part_cols):
            columns = pl.ds(part * part_cols, part_cols)
            total = jnp.zeros((LANES, part_cols), jnp.float32)
            for basis in range(BASES):
                smoothed = jnp.dot(
                    down_band[basis],
                    across[basis, pl.ds(first, 2 * LANES), columns],
                    preferred_element_type=jnp.float32,
                )
                weight = jnp.broadcast_to(inner[basis, DEGREE, 0:1, columns], total.shape)
                for power_v in reversed(range(DEGREE)):
                    weight = weight * v + inner[basis, power_v, 0:1, columns]
                total = total - weight * smoothed
            matched[pl.ds(first, LANES), columns] = total
        return carry

    lax.fori_loop(0, blocks, column_pass, 0)

    for at, way, here, share_of in passes:
        for thirds in range(1, planes):
            @pl.when(here & (share_of == thirds))
            def _():
                detour_copy(at, way, pl.ds(0, DETOUR * thirds)).wait_recv()

                def rejoin(slot, carry):
                    rejoin_copy(at, way, pl.ds(slot, 1)).start()
                    return carry

                lax.fori_loop(0, DETOUR * thirds, rejoin, 0)
    for at in range(DIAGONALS):
        for here, slots in turns(DIRS[at]):
            @pl.when(here)
            def _():
                relay_copy(at, pl.ds(0, slots)).wait_recv()

                def pass_on(slot, carry):
                    onward_copy(at, pl.ds(slot, 1)).start()
                    return carry

                lax.fori_loop(0, slots, pass_on, 0)
    lax.fori_loop(EARLY, CAP, functools.partial(send_slot, False), 0)

    for at, step in enumerate(DIRS):
        tags[pl.ds(at, 1)] = jnp.zeros((1, LANES), jnp.int32)

        @pl.when(exists(opposite(step)))
        def _():
            label_copy(at).wait_recv()
            tags[pl.ds(at, 1)] = arrived_table[at]
    tags[pl.ds(len(DIRS), 1)] = table[pl.ds(OWN, 1)]
    sort_plan(own, side // LANES, tags, plan, share)
    plan_copies = [
        pltpu.make_async_copy(plan, plan_scalar, load_sem.at[0]),
        pltpu.make_async_copy(share, share_scalar, load_sem.at[1]),
    ]
    for plan_copy in plan_copies:
        plan_copy.start()

    for at in range(DIAGONALS):
        for here, slots in turns(DIRS[at]):
            @pl.when(here)
            def _():
                onward_copy(at, pl.ds(0, slots)).wait_send()
    for at, way, here, share_of in passes:
        for thirds in range(1, planes):
            @pl.when(here & (share_of == thirds))
            def _():
                rejoin_copy(at, way, pl.ds(0, DETOUR * thirds)).wait_send()
    for plan_copy in plan_copies:
        plan_copy.wait()
    for at, step in enumerate(DIRS):
        @pl.when(exists(step))
        def _():
            rim_copy(at).wait_send()
            label_copy(at).wait_send()
            bucket_copy(at).wait_send()
    for at in reversed(range(len(DIRS))):
        @pl.when(exists(opposite(DIRS[at])))
        def _():
            bucket_copy(at).wait_recv()


def join_kernel(plan, share, arrived, matched, out, total, out_sem):
    side = out.shape[1]
    per_row = side // LANES

    def row_lines(block_row):
        return pl.ds(pl.multiple_of(block_row * LANES, LANES), LANES)

    def out_copy(block_row):
        lines = row_lines(block_row)
        return pltpu.make_async_copy(total.at[lines], out.at[lines], out_sem.at[block_row])

    def join_row(block_row, start):
        end = plan[3, block_row]
        lines = row_lines(block_row)

        def add(at, carry):
            slot = plan[0, at]
            column = pl.multiple_of((plan[1, at] - block_row * per_row) * LANES, LANES)
            columns = pl.ds(column, LANES)
            piece = arrived[lax.div(slot, CAP), slot & (CAP - 1)].astype(jnp.float32)
            total[lines, columns] = total[lines, columns] + share[2, at] * piece
            return carry

        lax.fori_loop(start, end, add, 0)
        out_copy(block_row).start()
        return end

    lax.fori_loop(0, per_row, join_row, 0)
    for block_row in range(per_row):
        out_copy(block_row).wait()


def on_device(pieces, owner_map, offsets, template, coefficients):
    own, block_side = pieces.shape[0], pieces.shape[1]
    side = template.shape[0]
    smem = pl.BlockSpec(memory_space=pltpu.SMEM)
    vmem = pl.BlockSpec(memory_space=pltpu.VMEM)
    hbm = pl.BlockSpec(memory_space=pltpu.HBM)
    count = len(DIRS)

    band_across, band_down = band_tables()
    tall = side + 2 * HALO
    dma = pltpu.SemaphoreType.DMA
    arrived, plan, share, matched = pl.pallas_call(
        send_kernel,
        out_shape=[
            jax.ShapeDtypeStruct((count + 1, CAP, block_side, block_side), jnp.bfloat16),
            pltpu.SMEM((8, 2 * LANES), jnp.int32),
            pltpu.SMEM((8, 2 * LANES), jnp.float32),
            jax.ShapeDtypeStruct((side, side), jnp.float32),
        ],
        in_specs=[hbm] * 7,
        out_specs=[vmem, smem, smem, vmem],
        scratch_shapes=[
            pltpu.VMEM((8, 2 * LANES), jnp.int32),
            pltpu.VMEM((8, 2 * LANES), jnp.float32),
            pltpu.VMEM((own, block_side, block_side), jnp.bfloat16),
            pltpu.SMEM(coefficients.shape, jnp.float32),
            pltpu.VMEM((1, own), jnp.int32),
            pltpu.VMEM((1, own), jnp.int32),
            pltpu.VMEM((16, LANES), jnp.int32),
            pltpu.VMEM((9, 1, LANES), jnp.int32),
            pltpu.SMEM((16, LANES), jnp.int32),
            pltpu.VMEM((count, 1, LANES), jnp.int32),
            pltpu.VMEM((16, LANES), jnp.int32),
            pltpu.VMEM((count, CAP, block_side, block_side), jnp.bfloat16),
            pltpu.VMEM((tall, side + 2 * LANES), jnp.bfloat16),
            pltpu.VMEM((2, LANES, LANES), jnp.bfloat16),
            pltpu.VMEM((2, LANES, LANES), jnp.bfloat16),
            pltpu.VMEM((BASES, side + LANES, side), jnp.bfloat16),
            pltpu.VMEM((BASES, DEGREE + 1, 8, side), jnp.float32),
            pltpu.VMEM(band_across.shape, jnp.bfloat16),
            pltpu.VMEM(band_down.shape, jnp.bfloat16),
            pltpu.VMEM((DIAGONALS, COLUMN_RELAYED, block_side, block_side), jnp.bfloat16),
            dma((9,)), dma, dma((count,)), dma((count,)), dma((count,)), dma((count,)),
            dma((count,)), dma((count,)), dma((DIAGONALS,)), dma((DIAGONALS,)),
            pltpu.VMEM((3 * DETOUR, block_side, block_side), jnp.bfloat16), dma, dma,
        ],
        compiler_params=pltpu.CompilerParams(
            collective_id=0, has_side_effects=True, vmem_limit_bytes=40 << 20
        ),
        name="send",
    )(
        *(
            pltpu.with_memory_space_constraint(array, pltpu.HBM)
            for array in (
                owner_map.reshape(1, own), offsets.reshape(1, own), coefficients, pieces,
                template, jnp.asarray(band_across), jnp.asarray(band_down),
            )
        )
    )
    joined, _ = pl.pallas_call(
        join_kernel,
        out_shape=[jax.ShapeDtypeStruct((side, side), jnp.float32)] * 2,
        in_specs=[smem, smem, vmem, vmem],
        out_specs=[hbm, vmem],
        input_output_aliases={3: 1},
        scratch_shapes=[dma((side // block_side,))],
        compiler_params=pltpu.CompilerParams(vmem_limit_bytes=32 << 20),
        name="join",
    )(plan, share, arrived, matched)
    return joined


def solution(mesh):
    in_specs = (P(("py", "px"), None, None), P(("py", "px")), P(("py", "px")), P("py", "px"), P())
    out_specs = P("py", "px")
    return jax.shard_map(
        on_device, mesh=mesh, in_specs=in_specs, out_specs=out_specs, check_vma=False
    )
```
